256 devices in a mesh: frame: 16 (over z, core), mp: 8 (over x, y_hi), dp: 2 (over y_lo).
Axes of the slice: x: 4, y: 4 (y_hi: 2, y_lo: 2; y = y_hi * 2 + y_lo), z: 8, core: 2. Of those that a mesh axis runs over, the one named last changes fastest.
Arguments:
- tokens: bfloat16 [4, 16, 160, 5120], P('dp', 'frame', None, 'mp'), may hold values from -30 to 30
- token_mask: int32 [4, 16, 160], P('dp', 'frame'), may hold values 0 or 1
- mask_embed: bfloat16 [5120], P('mp'), may hold values from -6 to 6
- w_qkv: bfloat16 [5120, 3, 3072], P('frame', None, 'mp'), may hold values from -0.078125 to 0.078125
- w_out: bfloat16 [3072, 5120], P('mp'), may hold values from -0.109375 to 0.109375
- action_idx: int32 [4, 16], P('dp', 'frame'), may hold values from 0 to 7
- codebook: float32 [8, 32], replicated, may hold values from -6 to 6
- act_proj: float32 [32, 5120], P(None, 'mp'), may hold values from -1 to 1
- cotangent: bfloat16 [4, 16, 160, 5120], P('dp', 'frame', None, 'mp'), may hold values from -6 to 6
Outputs:
- next_state: bfloat16 [4, 16, 160, 5120], P('dp', 'frame', None, 'mp')
- grad_proj: float32 [32, 5120], P(None, 'mp')
The draws below stay inside these ranges and needn't reach their ends.
All inputs are finite; a program needn't handle non-finite values. No bound on the sum of `token_mask` on one device may be relied on, other than what follows from the above.
Results may differ from the reference program's by a relative error of at most 0.0098.
Values may be sent and summed in bfloat16 or wider, within the bound.
No kernel may reach another device: no remote copies, remote signals or barrier semaphores. Data moves between devices by JAX's collectives and lax.ppermute only.
A program may use at most 128 MiB of HBM per device.

```python
import jax
import jax.numpy as jnp
from jax import lax

D = 5120
HEADS = 24
HS = 128
CODES = 8
D_ACT = 32
P_SIZE = 160
CLIPS = 4
FRAMES = 16


def draw_tokens(key, part):
    shape = (CLIPS, FRAMES, P_SIZE, D)
    return jax.random.truncated_normal(key, -6.0, 6.0, shape, jnp.float32).astype(jnp.bfloat16)


def touch_ends(result, rng, low, largest):
    longest = result.shape.index(max(result.shape))
    spots = []
    for shift in (0, 1):
        where = [jax.random.randint(jax.random.fold_in(rng, axis), (), 0, length) for axis, length in enumerate(result.shape)]
        where[longest] = (where[longest] + shift) % result.shape[longest]
        spots.append(tuple(where))
    return result.at[spots[0]].set(low).at[spots[1]].set(largest)


def block_scale(key, shape, cuts, smallest, high):
    factor_of, own = 1.0, jax.random.fold_in(key, 6)
    for axis_at, parts in cuts:
        heights = jnp.exp(jax.random.uniform(jax.random.fold_in(own, axis_at), (parts,), jnp.float32, smallest / len(cuts), high / len(cuts)))
        factor_of = factor_of * jnp.repeat(heights, shape[axis_at] // parts).reshape([-1 if axis == axis_at else 1 for axis in range(len(shape))])
    return factor_of


def centred(key, dims, scale, bound, cuts=(), dtype=jnp.bfloat16):
    factor_of = block_scale(key, dims, cuts, -0.22, 0.18) if cuts else 1.0
    array = jax.random.normal(key, dims, jnp.float32) * scale * factor_of
    return jnp.minimum(jnp.maximum(array, -bound), bound).astype(dtype)


def setup_inputs(seed: int = 0) -> dict:
    splits = jax.random.split(jax.random.key(seed), 10)
    tokens = draw_tokens(jax.random.fold_in(splits[9], 71), 0)
    token_mask = touch_ends((jax.random.randint(splits[1], (CLIPS, FRAMES, P_SIZE), 0, 2) < 1).astype(jnp.int32), jax.random.fold_in(splits[1], 1), 0, 1)
    mask_embed = centred(splits[2], (D,), 1.0, 6.0, ((0, 8),))
    w_qkv = centred(splits[3], (D, 3, HEADS * HS), D ** -0.5, 0.078125, ((0, 16), (2, 8)))
    w_out = centred(splits[4], (HEADS * HS, D), (HEADS * HS) ** -0.5, 0.109375, ((0, 8),))
    action_idx = touch_ends(jax.random.randint(splits[5], (CLIPS, FRAMES), 0, CODES), jax.random.fold_in(splits[5], 1), 0, CODES - 1).astype(jnp.int32)
    codebook = centred(splits[6], (CODES, D_ACT), 1.0, 6.0, (), jnp.float32)
    act_proj = centred(splits[7], (D_ACT, D), D_ACT ** -0.5, 1.0, ((1, 8),), jnp.float32)
    cotangent = centred(splits[8], (CLIPS, FRAMES, P_SIZE, D), 1.0, 6.0, ((0, 2), (1, 16), (3, 8)))
    return dict(tokens=tokens, token_mask=token_mask, mask_embed=mask_embed, w_qkv=w_qkv, w_out=w_out, action_idx=action_idx, codebook=codebook, act_proj=act_proj, cotangent=cotangent)


def reference(tokens, token_mask, mask_embed, w_qkv, w_out, action_idx, codebook, act_proj, cotangent):
    xin = jnp.where(token_mask[..., None] == 1, mask_embed, tokens)
    width_heads = HEADS * HS
    flat = xin.reshape(-1, D)
    qkv = jnp.dot(flat, w_qkv.reshape(D, 3 * width_heads), preferred_element_type=jnp.float32).astype(jnp.bfloat16)
    qkv = qkv.reshape(CLIPS, FRAMES, P_SIZE, 3, HEADS, HS)
    query = qkv[:, :, :, 0].astype(jnp.float32)
    keys = qkv[:, :, :, 1].astype(jnp.float32)
    values = qkv[:, :, :, 2].astype(jnp.float32)
    scores = jnp.einsum('cfphd,cuphd->cfphu', query, keys, precision=lax.Precision.HIGHEST) / jnp.sqrt(jnp.float32(HS))
    causal = (jnp.arange(FRAMES)[:, None] >= jnp.arange(FRAMES)[None, :])[None, :, None, None, :]
    peak = lax.optimization_barrier(jnp.max(jnp.where(causal, scores, -jnp.inf), axis=-1))
    weights = jnp.where(causal, jnp.exp(scores - peak[..., None]), 0.0)
    total = lax.optimization_barrier(jnp.sum(weights, axis=-1))
    accum = jnp.einsum('cfphu,cuphd->cfphd', weights, values, precision=lax.Precision.HIGHEST)
    attn = (accum / total[..., None]).astype(jnp.bfloat16).reshape(-1, width_heads)
    mixed = jnp.dot(attn, w_out, preferred_element_type=jnp.float32).reshape(CLIPS, FRAMES, P_SIZE, D)
    codevec = codebook[action_idx].reshape(-1, D_ACT)
    gate = jnp.dot(codevec, act_proj, precision=lax.Precision.HIGHEST).reshape(CLIPS, FRAMES, 1, D)
    next_state = (xin.astype(jnp.float32) + gate * mixed).astype(jnp.bfloat16)
    dgate = lax.optimization_barrier(jnp.sum(cotangent.astype(jnp.float32) * mixed, axis=2)).reshape(-1, D)
    grad_proj = jnp.dot(codevec.T, dgate, precision=lax.Precision.HIGHEST)
    return (next_state, grad_proj)
```

```python
import math

import jax
import jax.numpy as jnp
from jax import lax
from jax.experimental import pallas as pl
from jax.experimental.pallas import tpu as pltpu
from jax.sharding import PartitionSpec as P

HS = 128
MASKED = -1e30


def exchange(x, axis):
    return lax.all_to_all(x, axis, split_axis=0, concat_axis=0, tiled=True)


def from_everyone(x, axis):
    return exchange(jnp.broadcast_to(x, (lax.axis_size(axis), *x.shape)), axis)


def attend(q, k, v, bias):
    s = lax.dot_general(q, k, (((1,), (1,)), ((), ())), preferred_element_type=jnp.float32)
    s = s * (1.0 / math.sqrt(HS)) + bias
    peak = jnp.max(s, axis=1, keepdims=True)
    w = jnp.exp(s - peak)
    total = jnp.sum(w, axis=1, keepdims=True)
    high = w.astype(jnp.bfloat16)
    low = (w - high.astype(jnp.float32)).astype(jnp.bfloat16)
    accum = jnp.dot(high, v, preferred_element_type=jnp.float32)
    accum += jnp.dot(low, v, preferred_element_type=jnp.float32)
    return (accum / total).astype(jnp.bfloat16)


def qkv_attention_kernel(x_ref, w_ref, bias_ref, out_ref, acc):
    step = pl.program_id(0)
    x = x_ref[0]
    for i in range(3):
        part = jnp.dot(x, w_ref[i], preferred_element_type=jnp.float32)

        @pl.when(step == 0)
        def _():
            acc[i] = part

        @pl.when(step > 0)
        def _():
            acc[i] += part

    @pl.when(step == pl.num_programs(0) - 1)
    def _():
        frames, spots, width = out_ref.shape
        bias = bias_ref[...]
        for h in range(width // HS):
            cols = slice(h * HS, (h + 1) * HS)
            q, k, v = (acc[i, :, cols].astype(jnp.bfloat16) for i in range(3))
            o = attend(q, k, v, bias)
            for t in range(frames):
                out_ref[t, :, cols] = o[t * spots : (t + 1) * spots]


def qkv_attention(x, w, frames):
    mp, rows, width = x.shape
    heads = w.shape[2]
    spots = rows // frames
    r = jnp.arange(rows)
    seen = (r[:, None] % spots == r[None, :] % spots) & (r[:, None] >= r[None, :])
    bias = jnp.where(seen, 0.0, MASKED).astype(jnp.float32)
    return pl.pallas_call(
        qkv_attention_kernel,
        grid=(mp,),
        in_specs=[
            pl.BlockSpec((1, rows, width), lambda m: (m, 0, 0)),
            pl.BlockSpec((3, width, heads), lambda m: (0, m, 0)),
            pl.BlockSpec((rows, rows), lambda m: (0, 0)),
        ],
        out_specs=pl.BlockSpec((frames, spots, heads), lambda m: (0, 0, 0)),
        out_shape=jax.ShapeDtypeStruct((frames, spots, heads), jnp.bfloat16),
        scratch_shapes=[pltpu.VMEM((3, rows, heads), jnp.float32)],
        compiler_params=pltpu.CompilerParams(vmem_limit_bytes=40 * 1024 * 1024),
    )(x, w, bias)


def body(tokens, token_mask, mask_embed, w_qkv, w_out, action_idx, codebook, act_proj, cotangent):
    clips, _, spots, width = tokens.shape
    rows = clips * spots
    frames = lax.axis_size("frame")
    mp = lax.axis_size("mp")
    heads = w_qkv.shape[2]
    weights = lax.all_gather(w_qkv, "frame", axis=0, tiled=True).transpose(1, 0, 2)
    xin = jnp.where(token_mask[..., None] == 1, mask_embed, tokens)
    mine = exchange(xin.reshape(frames, rows // frames, width), "frame").reshape(rows, width)
    features = from_everyone(mine, "mp")
    w_out, features = lax.optimization_barrier((w_out, features))
    out_block = lax.all_to_all(
        w_out.reshape(heads, mp, width).transpose(1, 0, 2), "mp", split_axis=0, concat_axis=0, tiled=True
    )
    attn = qkv_attention(features, weights, frames)
    attn = exchange(attn, "frame").reshape(rows, heads)
    all_heads = from_everyone(attn, "mp")
    mixed = lax.dot_general(
        all_heads, out_block, (((0, 2), (0, 1)), ((), ())), preferred_element_type=jnp.float32
    ).reshape(clips, spots, width)
    onehot = (action_idx.reshape(clips)[:, None] == jnp.arange(codebook.shape[0])[None, :]).astype(
        jnp.float32
    )
    codevec = jnp.dot(onehot, codebook, precision=lax.Precision.HIGHEST)
    gate = jnp.dot(codevec, act_proj, precision=lax.Precision.HIGHEST)
    xin = xin.reshape(clips, spots, width)
    next_state = (xin.astype(jnp.float32) + gate[:, None, :] * mixed).astype(jnp.bfloat16)
    dgate = jnp.sum(cotangent.reshape(clips, spots, width).astype(jnp.float32) * mixed, axis=1)
    terms = from_everyone(jnp.concatenate([dgate, codevec], axis=1), ("frame", "dp"))
    terms = terms.reshape(-1, terms.shape[-1])
    grad_proj = lax.dot_general(
        terms[:, width:],
        terms[:, :width],
        (((0,), (0,)), ((), ())),
        precision=lax.Precision.HIGHEST,
        preferred_element_type=jnp.float32,
    )
    return (next_state.reshape(tokens.shape), grad_proj)


def solution(mesh):
    return jax.shard_map(
        body,
        mesh=mesh,
        in_specs=(
            P("dp", "frame", None, "mp"),
            P("dp", "frame", None),
            P("mp"),
            P("frame", None, "mp"),
            P("mp", None),
            P("dp", "frame"),
            P(),
            P(None, "mp"),
            P("dp", "frame", None, "mp"),
        ),
        out_specs=(P("dp", "frame", None, "mp"), P(None, "mp")),
        check_vma=False,
    )
```

```python
import math

import jax
import jax.numpy as jnp
from jax import lax
from jax.experimental import pallas as pl
from jax.experimental.pallas import tpu as pltpu
from jax.sharding import Mesh
from jax.sharding import PartitionSpec as P

HS = 128
MASKED = -1e30
FRAME = ("z", "core")
MP = ("x", "yhi")
VMEM = pltpu.CompilerParams(vmem_limit_bytes=50 * 1024 * 1024)


def exchange(x, axis):
    return lax.all_to_all(x, axis, split_axis=0, concat_axis=0, tiled=True)


def from_everyone(x, axis):
    return exchange(jnp.broadcast_to(x, (lax.axis_size(axis), *x.shape)), axis)


def shift(x, axis, by):
    n = lax.axis_size(axis)
    return lax.ppermute(x, axis, [(i, (i + by) % n) for i in range(n)])


def accumulate_kernel(counts, first, last, slots, core, x_ref, *refs):
    n = sum(counts)
    w_refs, rest = refs[:n], refs[n:]
    acc_in = None if first else rest[0]
    rest = rest if first else rest[1:]
    parts = [[None if first else acc_in[s, i] for i in range(3)] for s in range(2)]
    at = 0
    for j, count in enumerate(counts):
        x = x_ref[slots[j]]
        half = x.shape[1] // 2
        xs = (x[:, :half], x[:, half:])
        for i in range(3):
            pieces = [w_refs[at + c][i] for c in range(count)]
            w = pieces[0] if count == 1 else jnp.concatenate(pieces, axis=0)
            for s in range(2):
                d = jnp.dot(xs[s], w, preferred_element_type=jnp.float32)
                parts[s][i] = d if parts[s][i] is None else parts[s][i] + d
        at += count
    for i in range(3):
        if last:
            mine = core[0] == 0
            rest[0][i] = jnp.where(mine, parts[0][i], parts[1][i])
            rest[1][i] = jnp.where(mine, parts[1][i], parts[0][i]).astype(jnp.bfloat16)
        else:
            for s in range(2):
                rest[0][s, i] = parts[s][i]


def accumulate(x, shards, slots, core, acc=None, last=False):
    counts = [len(s) for s in shards]
    flat = [w for s in shards for w in s]
    rows, heads = x.shape[1], flat[0].shape[2]
    if last:
        out_shape = (
            jax.ShapeDtypeStruct((3, rows, heads), jnp.float32),
            jax.ShapeDtypeStruct((3, rows, heads), jnp.bfloat16),
        )
    else:
        out_shape = jax.ShapeDtypeStruct((2, 3, rows, heads), jnp.float32)

    def kernel(*refs):
        accumulate_kernel(counts, acc is None, last, *refs)

    smem = pl.BlockSpec(memory_space=pltpu.SMEM)
    vmem = pl.BlockSpec(memory_space=pltpu.VMEM)
    operands = [x, *flat] + ([] if acc is None else [acc])
    return pl.pallas_call(
        kernel,
        in_specs=[smem, smem] + [vmem] * len(operands),
        out_specs=(vmem, vmem) if last else vmem,
        out_shape=out_shape,
        compiler_params=VMEM,
    )(slots, core, *operands)


def attend(q, k, v, bias):
    s = lax.dot_general(q, k, (((1,), (1,)), ((), ())), preferred_element_type=jnp.float32)
    s = s * (1.0 / math.sqrt(HS)) + bias
    peak = jnp.max(s, axis=1, keepdims=True)
    w = jnp.exp(s - peak)
    total = jnp.sum(w, axis=1, keepdims=True)
    high = w.astype(jnp.bfloat16)
    low = (w - high.astype(jnp.float32)).astype(jnp.bfloat16)
    accum = jnp.dot(high, v, preferred_element_type=jnp.float32)
    accum += jnp.dot(low, v, preferred_element_type=jnp.float32)
    return (accum / total).astype(jnp.bfloat16)


def attention_kernel(own_ref, other_ref, bias_ref, out_ref):
    frames, spots, width = out_ref.shape
    bias = bias_ref[...]
    for h in range(width // HS):
        cols = slice(h * HS, (h + 1) * HS)
        q, k, v = (
            (own_ref[i, :, cols] + other_ref[i, :, cols].astype(jnp.float32)).astype(jnp.bfloat16)
            for i in range(3)
        )
        o = attend(q, k, v, bias)
        for t in range(frames):
            out_ref[t, :, cols] = o[t * spots : (t + 1) * spots]


def attention(own, other, frames):
    _, rows, heads = own.shape
    spots = rows // frames
    r = jnp.arange(rows)
    seen = (r[:, None] % spots == r[None, :] % spots) & (r[:, None] >= r[None, :])
    bias = jnp.where(seen, 0.0, MASKED).astype(jnp.float32)
    return pl.pallas_call(
        attention_kernel,
        out_shape=jax.ShapeDtypeStruct((frames, spots, heads), jnp.bfloat16),
        compiler_params=VMEM,
    )(own, other, bias)


def blocks_kernel(core, w_ref, out_ref):
    out_ref[0] = w_ref[...]


def column_blocks(w, core, width):
    heads, full = w.shape
    half, n = heads // 2, full // width
    return pl.pallas_call(
        blocks_kernel,
        grid_spec=pltpu.PrefetchScalarGridSpec(
            num_scalar_prefetch=1,
            grid=(n,),
            in_specs=[pl.BlockSpec((half, width), lambda m, core: (core[0], m))],
            out_specs=pl.BlockSpec((1, half, width), lambda m, core: (m, 0, 0)),
        ),
        out_shape=jax.ShapeDtypeStruct((n, half, width), w.dtype),
        compiler_params=VMEM,
    )(core, w)


def gather_features(mine):
    both = jnp.stack([mine, shift(mine, "yhi", 1)])
    half = mine.shape[0] // 2
    left, right = shift(both, "x", 1), shift(both, "x", -1)
    far = jnp.concatenate([shift(left[:, :half], "x", 1), shift(right[:, half:], "x", -1)], axis=1)
    return jnp.concatenate([both, right, far, left])


def body(tokens, token_mask, mask_embed, w_qkv, w_out, action_idx, codebook, act_proj, cotangent):
    clips, _, spots, width = tokens.shape
    rows = clips * spots
    zs, cores = lax.axis_size("z"), lax.axis_size("core")
    frames, mp = zs * cores, lax.axis_size(MP)
    depth, heads = w_qkv.shape[0], w_qkv.shape[2]
    z, core = lax.axis_index("z"), lax.axis_index("core")
    core1 = core.reshape(1).astype(jnp.int32)
    xin = jnp.where(token_mask[..., None] == 1, mask_embed, tokens).reshape(rows, width)
    mine = xin.reshape(zs, 2, rows // frames, cores, depth).transpose(0, 3, 2, 1, 4)
    mine = exchange(mine.reshape(frames, rows // frames, 2 * depth), FRAME).reshape(rows, 2 * depth)

    own = w_qkv.transpose(1, 0, 2)
    up1, down1 = shift(own, "z", 1), shift(own, "z", -1)
    features = gather_features(mine)
    up2, down2 = shift(up1, "z", 1), shift(down1, "z", -1)
    up3, down3 = shift(up2, "z", 1), shift(down2, "z", -1)
    up4 = shift(up3[:, : depth // 2], "z", 1)
    down4 = shift(down3[:, depth // 2 :], "z", -1)

    w_out, features = lax.optimization_barrier((w_out, features))
    half = exchange(column_blocks(w_out, core1, width), MP)
    other_half = shift(half, "core", 1)
    out_block = jnp.concatenate(
        [jnp.where(core == 0, half, other_half), jnp.where(core == 0, other_half, half)], axis=1
    )

    x, yhi = lax.axis_index("x"), lax.axis_index("yhi")

    def slots(*shifts):
        shard = (z + jnp.array(shifts, jnp.int32)) % zs
        return (2 * ((shard // 2 - x) % (mp // 2)) + (shard % 2) ^ yhi).astype(jnp.int32)

    acc = accumulate(
        features, [(own,), (up1,), (down1,), (up2,), (down2,)], slots(0, -1, 1, -2, 2), core1
    )
    acc = accumulate(features, [(up3,), (down3,)], slots(-3, 3), core1, acc)
    kept, sent = accumulate(features, [(up4, down4)], slots(-4), core1, acc, last=True)
    attn = attention(kept, shift(sent, "core", 1), frames)
    attn = exchange(attn, FRAME).reshape(rows, heads)
    all_heads = from_everyone(attn, MP)
    mixed = lax.dot_general(
        all_heads, out_block, (((0, 2), (0, 1)), ((), ())), preferred_element_type=jnp.float32
    ).reshape(clips, spots, width)
    onehot = (action_idx.reshape(clips)[:, None] == jnp.arange(codebook.shape[0])[None, :]).astype(
        jnp.float32
    )
    codevec = jnp.dot(onehot, codebook, precision=lax.Precision.HIGHEST)
    gate = jnp.dot(codevec, act_proj, precision=lax.Precision.HIGHEST)
    xin = xin.reshape(clips, spots, width)
    next_state = (xin.astype(jnp.float32) + gate[:, None, :] * mixed).astype(jnp.bfloat16)
    dgate = jnp.sum(cotangent.reshape(clips, spots, width).astype(jnp.float32) * mixed, axis=1)
    terms = from_everyone(jnp.concatenate([dgate, codevec], axis=1), FRAME + ("dp",))
    terms = terms.reshape(-1, terms.shape[-1])
    grad_proj = lax.dot_general(
        terms[:, width:],
        terms[:, :width],
        (((0,), (0,)), ((), ())),
        precision=lax.Precision.HIGHEST,
        preferred_element_type=jnp.float32,
    )
    return (next_state.reshape(tokens.shape), grad_proj)


def solution(mesh):
    split = Mesh(
        mesh.devices.reshape(mesh.shape["frame"] // 2, 2, mesh.shape["mp"] // 2, 2, mesh.shape["dp"]),
        ("z", "core", "x", "yhi", "dp"),
    )
    return jax.shard_map(
        body,
        mesh=split,
        in_specs=(
            P("dp", FRAME, None, MP),
            P("dp", FRAME, None),
            P(MP),
            P(FRAME, None, MP),
            P(MP, None),
            P("dp", FRAME),
            P(),
            P(None, MP),
            P("dp", FRAME, None, MP),
        ),
        out_specs=(P("dp", FRAME, None, MP), P(None, MP)),
        check_vma=False,
    )
```

```python
import math

import jax
import jax.numpy as jnp
from jax import lax
from jax.experimental import pallas as pl
from jax.experimental.pallas import tpu as pltpu
from jax.sharding import Mesh
from jax.sharding import PartitionSpec as P

HS = 128
MASKED = -1e30
FRAME = ("z", "core")
MP = ("x", "yhi")
SMALL = pltpu.CompilerParams(vmem_limit_bytes=16 * 1024 * 1024)


def exchange(x, axis):
    return lax.all_to_all(x, axis, split_axis=0, concat_axis=0, tiled=True)


def from_everyone(x, axis):
    return exchange(jnp.broadcast_to(x, (lax.axis_size(axis), *x.shape)), axis)


def shift(x, axis, by):
    n = lax.axis_size(axis)
    return lax.ppermute(x, axis, [(i, (i + by) % n) for i in range(n)])


def qkv_kernel(slots, core, x_any, *refs):
    n = len(refs) - 7
    shards, (kept, sent, x_ref, w_ref, acc, x_sem, w_sem) = refs[:n], refs[n:]
    copies, at = [], 0
    for j in range(x_ref.shape[0]):
        copies.append([pltpu.make_async_copy(x_any.at[slots[j]], x_ref.at[j], x_sem.at[j])])
        full = x_ref.shape[2] // 2
        row = 0
        while row < full:
            depth = shards[at].shape[1]
            target = w_ref.at[:, pl.ds(j * full + row, depth)]
            copies[j].append(pltpu.make_async_copy(shards[at], target, w_sem.at[at]))
            row += depth
            at += 1
    for group in copies:
        for copy in group:
            copy.start()
    rows, half = x_ref.shape[1], x_ref.shape[2] // 2
    for j in range(0, x_ref.shape[0], 2):
        for copy in copies[j] + copies[j + 1]:
            copy.wait()
        a, b = x_ref[j], x_ref[j + 1]
        low = jnp.concatenate([a[:, :half], b[:, :half]], axis=1)
        high = jnp.concatenate([a[:, half:], b[:, half:]], axis=1)
        x = jnp.concatenate([low, high], axis=0)
        depth = pl.ds(j * half, 2 * half)
        w = jnp.concatenate([w_ref[i, depth] for i in range(3)], axis=1)
        part = jnp.dot(x, w, preferred_element_type=jnp.float32)
        if j == 0:
            acc[...] = part
        else:
            acc[...] += part
    me = core[0]
    kept[...] = acc[pl.ds(me * rows, rows)]
    sent[...] = acc[pl.ds((1 - me) * rows, rows)].astype(jnp.bfloat16)


def project(x, shards, slots, core):
    n, rows, width = x.shape
    heads = 3 * shards[0].shape[2]
    smem = pl.BlockSpec(memory_space=pltpu.SMEM)
    vmem = pl.BlockSpec(memory_space=pltpu.VMEM)
    hbm = pl.BlockSpec(memory_space=pl.ANY)
    return pl.pallas_call(
        qkv_kernel,
        in_specs=[smem, smem] + [hbm] * (1 + len(shards)),
        out_specs=(vmem, vmem),
        out_shape=(
            jax.ShapeDtypeStruct((rows, heads), jnp.float32),
            jax.ShapeDtypeStruct((rows, heads), jnp.bfloat16),
        ),
        scratch_shapes=[
            pltpu.VMEM((n, rows, width), jnp.bfloat16),
            pltpu.VMEM((3, n * width // 2, heads // 3), jnp.bfloat16),
            pltpu.VMEM((2 * rows, heads), jnp.float32),
            pltpu.SemaphoreType.DMA((n,)),
            pltpu.SemaphoreType.DMA((len(shards),)),
        ],
        compiler_params=pltpu.CompilerParams(vmem_limit_bytes=28 * 1024 * 1024),
    )(slots, core, x, *shards)


def attend(q, k, v, bias):
    s = lax.dot_general(q, k, (((1,), (1,)), ((), ())), preferred_element_type=jnp.float32)
    s = s * (1.0 / math.sqrt(HS)) + bias
    peak = jnp.max(s, axis=1, keepdims=True)
    w = jnp.exp(s - peak)
    total = jnp.sum(w, axis=1, keepdims=True)
    high = w.astype(jnp.bfloat16)
    low = (w - high.astype(jnp.float32)).astype(jnp.bfloat16)
    accum = jnp.dot(high, v, preferred_element_type=jnp.float32)
    accum += jnp.dot(low, v, preferred_element_type=jnp.float32)
    return (accum / total).astype(jnp.bfloat16)


def attention_kernel(own_ref, other_ref, bias_ref, out_ref):
    frames, spots, width = out_ref.shape
    bias = bias_ref[...]
    for h in range(width // HS):
        q, k, v = (
            (own_ref[:, cols] + other_ref[:, cols].astype(jnp.float32)).astype(jnp.bfloat16)
            for cols in (slice(i * width + h * HS, i * width + (h + 1) * HS) for i in range(3))
        )
        o = attend(q, k, v, bias)
        for t in range(frames):
            out_ref[t, :, h * HS : (h + 1) * HS] = o[t * spots : (t + 1) * spots]


def attention(own, other, frames):
    rows, heads = own.shape[0], own.shape[1] // 3
    spots = rows // frames
    r = jnp.arange(rows)
    seen = (r[:, None] % spots == r[None, :] % spots) & (r[:, None] >= r[None, :])
    bias = jnp.where(seen, 0.0, MASKED).astype(jnp.float32)
    return pl.pallas_call(
        attention_kernel,
        out_shape=jax.ShapeDtypeStruct((frames, spots, heads), jnp.bfloat16),
        compiler_params=SMALL,
    )(own, other, bias)


def blocks_kernel(core, w_ref, out_ref):
    out_ref[0] = w_ref[...]


def column_blocks(w, core, width):
    heads, full = w.shape
    half, n = heads // 2, full // width
    return pl.pallas_call(
        blocks_kernel,
        grid_spec=pltpu.PrefetchScalarGridSpec(
            num_scalar_prefetch=1,
            grid=(n,),
            in_specs=[pl.BlockSpec((half, width), lambda m, core: (core[0], m))],
            out_specs=pl.BlockSpec((1, half, width), lambda m, core: (m, 0, 0)),
        ),
        out_shape=jax.ShapeDtypeStruct((n, half, width), w.dtype),
        compiler_params=SMALL,
    )(core, w)


def body(tokens, token_mask, mask_embed, w_qkv, w_out, action_idx, codebook, act_proj, cotangent):
    clips, _, spots, width = tokens.shape
    rows = clips * spots
    zs, cores = lax.axis_size("z"), lax.axis_size("core")
    frames, mp = zs * cores, lax.axis_size(MP)
    depth, heads = w_qkv.shape[0], w_qkv.shape[2]
    z, core = lax.axis_index("z"), lax.axis_index("core")
    core1 = core.reshape(1).astype(jnp.int32)
    xin = jnp.where(token_mask[..., None] == 1, mask_embed, tokens).reshape(rows, width)
    mine = xin.reshape(zs, 2, rows // frames, cores, depth).transpose(0, 3, 2, 1, 4)
    mine = exchange(mine.reshape(frames, rows // frames, 2 * depth), FRAME).reshape(rows, 2 * depth)

    own = w_qkv.transpose(1, 0, 2)
    up1, down1 = shift(own, "z", 1), shift(own, "z", -1)
    mine, up1, down1 = lax.optimization_barrier((mine, up1, down1))
    up2, down2 = shift(up1, "z", 1), shift(down1, "z", -1)
    both = jnp.stack([mine, shift(mine, "yhi", 1)])
    both, w_out = lax.optimization_barrier((both, w_out))
    left, right = shift(both, "x", 1), shift(both, "x", -1)
    blocks = column_blocks(w_out, core1, width)
    left, right, up2, down2, blocks = lax.optimization_barrier((left, right, up2, down2, blocks))
    up3, down3 = shift(up2, "z", 1), shift(down2, "z", -1)
    middle = rows // 2
    far = (shift(left[:, :middle], "x", 1), shift(right[:, middle:], "x", -1))
    up3, down3, far, blocks = lax.optimization_barrier((up3, down3, far, blocks))
    up4 = shift(up3[:, : depth // 2], "z", 1)
    down4 = shift(down3[:, depth // 2 :], "z", -1)
    features = jnp.concatenate([both, right, jnp.concatenate(far, axis=1), left])

    half = exchange(blocks, MP)
    other_half = shift(half, "core", 1)
    out_block = jnp.concatenate(
        [jnp.where(core == 0, half, other_half), jnp.where(core == 0, other_half, half)], axis=1
    )

    x, yhi = lax.axis_index("x"), lax.axis_index("yhi")
    shard = (z + jnp.array([0, zs - 1, 1, zs - 2, 2, zs - 3, 3, zs - 4], jnp.int32)) & (zs - 1)
    slots = (2 * (((shard >> 1) - x) & (mp // 2 - 1)) + ((shard & 1) ^ yhi)).astype(jnp.int32)
    shards = [own, up1, down1, up2, down2, up3, down3, up4, down4]
    kept, sent = project(features, shards, slots, core1)
    attn = attention(kept, shift(sent, "core", 1), frames)
    attn = exchange(attn, FRAME).reshape(rows, heads)
    all_heads = from_everyone(attn, MP)
    mixed = lax.dot_general(
        all_heads, out_block, (((0, 2), (0, 1)), ((), ())), preferred_element_type=jnp.float32
    ).reshape(clips, spots, width)
    onehot = (action_idx.reshape(clips)[:, None] == jnp.arange(codebook.shape[0])[None, :]).astype(
        jnp.float32
    )
    codevec = jnp.dot(onehot, codebook, precision=lax.Precision.HIGHEST)
    gate = jnp.dot(codevec, act_proj, precision=lax.Precision.HIGHEST)
    xin = xin.reshape(clips, spots, width)
    next_state = (xin.astype(jnp.float32) + gate[:, None, :] * mixed).astype(jnp.bfloat16)
    dgate = jnp.sum(cotangent.reshape(clips, spots, width).astype(jnp.float32) * mixed, axis=1)
    terms = from_everyone(jnp.concatenate([dgate, codevec], axis=1), FRAME + ("dp",))
    terms = terms.reshape(-1, terms.shape[-1])
    grad_proj = lax.dot_general(
        terms[:, width:],
        terms[:, :width],
        (((0,), (0,)), ((), ())),
        precision=lax.Precision.HIGHEST,
        preferred_element_type=jnp.float32,
    )
    return (next_state.reshape(tokens.shape), grad_proj)


def solution(mesh):
    split = Mesh(
        mesh.devices.reshape(mesh.shape["frame"] // 2, 2, mesh.shape["mp"] // 2, 2, mesh.shape["dp"]),
        ("z", "core", "x", "yhi", "dp"),
    )
    return jax.shard_map(
        body,
        mesh=split,
        in_specs=(
            P("dp", FRAME, None, MP),
            P("dp", FRAME, None),
            P(MP),
            P(FRAME, None, MP),
            P(MP, None),
            P("dp", FRAME),
            P(),
            P(None, MP),
            P("dp", FRAME, None, MP),
        ),
        out_specs=(P("dp", FRAME, None, MP), P(None, MP)),
        check_vma=False,
    )
```

```python
import math

import jax
import jax.numpy as jnp
from jax import lax
from jax.experimental import pallas as pl
from jax.experimental.pallas import tpu as pltpu
from jax.sharding import Mesh
from jax.sharding import PartitionSpec as P

HS = 128
MASKED = -1e30
LENT = 2
FRAME = ("z", "core")
MP = ("x", "yhi")
SMALL = pltpu.CompilerParams(vmem_limit_bytes=16 * 1024 * 1024)


def exchange(x, axis):
    return lax.all_to_all(x, axis, split_axis=0, concat_axis=0, tiled=True)


def from_everyone(x, axis):
    return exchange(jnp.broadcast_to(x, (lax.axis_size(axis), *x.shape)), axis)


def shift(x, axis, by):
    n = lax.axis_size(axis)
    return lax.ppermute(x, axis, [(i, (i + by) % n) for i in range(n)])


def qkv_kernel(places, slots, core, *refs):
    n_x, n_w = 5, len(refs) - 12
    (both, right, top, low, left), shards = refs[:n_x], refs[n_x : n_x + n_w]
    kept, sent, x_ref, w_ref, acc, x_sem, w_sem = refs[n_x + n_w :]
    rows, full = x_ref.shape[1], x_ref.shape[2] // 2
    copies, at = [], 0
    for j, pieces in enumerate(places):
        far, own = slots[j] >> 1, slots[j] & 1
        for k, source in ((0, both), (1, right), (3, left)):

            @pl.when(far == k)
            def _():
                pltpu.make_async_copy(source.at[own], x_ref.at[j], x_sem.at[j]).start()

        @pl.when(far == 2)
        def _():
            half = rows // 2
            pltpu.make_async_copy(top.at[own], x_ref.at[j, pl.ds(0, half)], x_sem.at[j]).start()
            pltpu.make_async_copy(low.at[own], x_ref.at[j, pl.ds(half, half)], x_sem.at[j]).start()

        copies.append([])
        row = j * full
        for index, part in pieces:
            source = shards[index] if part is None else shards[index].at[part]
            depth = source.shape[1]
            copy = pltpu.make_async_copy(source, w_ref.at[:, pl.ds(row, depth)], w_sem.at[at])
            copy.start()
            copies[j].append(copy)
            row += depth
            at += 1
    for j in range(0, len(places), 2):
        for i in (j, j + 1):
            pltpu.make_async_copy(both.at[0], x_ref.at[i], x_sem.at[i]).wait()
            for copy in copies[i]:
                copy.wait()
        a, b = x_ref[j], x_ref[j + 1]
        first = jnp.concatenate([a[:, :full], b[:, :full]], axis=1)
        second = jnp.concatenate([a[:, full:], b[:, full:]], axis=1)
        x = jnp.concatenate([first, second], axis=0)
        w = jnp.concatenate([w_ref[i, pl.ds(j * full, 2 * full)] for i in range(3)], axis=1)
        part = jnp.dot(x, w, preferred_element_type=jnp.float32)
        if j == 0:
            acc[...] = part
        else:
            acc[...] += part
    me = core[0]
    kept[...] = acc[pl.ds(me * rows, rows)]
    sent[...] = acc[pl.ds((1 - me) * rows, rows)].astype(jnp.bfloat16)


def project(features, shards, places, slots, core):
    _, rows, width = features[0].shape
    n, heads = len(places), shards[0].shape[-1]
    smem = pl.BlockSpec(memory_space=pltpu.SMEM)
    vmem = pl.BlockSpec(memory_space=pltpu.VMEM)
    hbm = pl.BlockSpec(memory_space=pl.ANY)

    def kernel(*refs):
        qkv_kernel(places, *refs)

    return pl.pallas_call(
        kernel,
        in_specs=[smem, smem] + [hbm] * (len(features) + len(shards)),
        out_specs=(vmem, vmem),
        out_shape=(
            jax.ShapeDtypeStruct((rows, 3 * heads), jnp.float32),
            jax.ShapeDtypeStruct((rows, 3 * heads), jnp.bfloat16),
        ),
        scratch_shapes=[
            pltpu.VMEM((n, rows, width), jnp.bfloat16),
            pltpu.VMEM((3, n * width // 2, heads), jnp.bfloat16),
            pltpu.VMEM((2 * rows, 3 * heads), jnp.float32),
            pltpu.SemaphoreType.DMA((n,)),
            pltpu.SemaphoreType.DMA((sum(len(p) for p in places),)),
        ],
        compiler_params=pltpu.CompilerParams(vmem_limit_bytes=28 * 1024 * 1024),
    )(slots, core, *features, *shards)


def attend(q, k, v, bias):
    s = lax.dot_general(q, k, (((1,), (1,)), ((), ())), preferred_element_type=jnp.float32)
    s = s * (1.0 / math.sqrt(HS)) + bias
    peak = jnp.max(s, axis=1, keepdims=True)
    w = jnp.exp(s - peak)
    total = jnp.sum(w, axis=1, keepdims=True)
    high = w.astype(jnp.bfloat16)
    low = (w - high.astype(jnp.float32)).astype(jnp.bfloat16)
    accum = jnp.dot(high, v, preferred_element_type=jnp.float32)
    accum += jnp.dot(low, v, preferred_element_type=jnp.float32)
    return (accum / total).astype(jnp.bfloat16)


def attention_kernel(own_ref, other_ref, bias_ref, out_ref):
    frames, spots, width = out_ref.shape
    bias = bias_ref[...]
    for h in range(width // HS):
        q, k, v = (
            (own_ref[:, cols] + other_ref[:, cols].astype(jnp.float32)).astype(jnp.bfloat16)
            for cols in (slice(i * width + h * HS, i * width + (h + 1) * HS) for i in range(3))
        )
        o = attend(q, k, v, bias)
        for t in range(frames):
            out_ref[t, :, h * HS : (h + 1) * HS] = o[t * spots : (t + 1) * spots]


def attention(own, other, frames):
    rows, heads = own.shape[0], own.shape[1] // 3
    spots = rows // frames
    r = jnp.arange(rows)
    seen = (r[:, None] % spots == r[None, :] % spots) & (r[:, None] >= r[None, :])
    bias = jnp.where(seen, 0.0, MASKED).astype(jnp.float32)
    return pl.pallas_call(
        attention_kernel,
        out_shape=jax.ShapeDtypeStruct((frames, spots, heads), jnp.bfloat16),
        compiler_params=SMALL,
    )(own, other, bias)


def blocks_kernel(core, w_ref, out_ref):
    out_ref[0] = w_ref[...]


def column_blocks(w, core, width):
    heads, full = w.shape
    half, n = heads // 2, full // width
    return pl.pallas_call(
        blocks_kernel,
        grid_spec=pltpu.PrefetchScalarGridSpec(
            num_scalar_prefetch=1,
            grid=(n,),
            in_specs=[pl.BlockSpec((half, width), lambda m, core: (core[0], m))],
            out_specs=pl.BlockSpec((1, half, width), lambda m, core: (m, 0, 0)),
        ),
        out_shape=jax.ShapeDtypeStruct((n, half, width), w.dtype),
        compiler_params=SMALL,
    )(core, w)


def body(tokens, token_mask, mask_embed, w_qkv, w_out, action_idx, codebook, act_proj, cotangent):
    clips, _, spots, width = tokens.shape
    rows = clips * spots
    zs, cores = lax.axis_size("z"), lax.axis_size("core")
    frames, mp = zs * cores, lax.axis_size(MP)
    depth, heads = w_qkv.shape[0], w_qkv.shape[2]
    z, core = lax.axis_index("z"), lax.axis_index("core")
    core1 = core.reshape(1).astype(jnp.int32)
    xin = jnp.where(token_mask[..., None] == 1, mask_embed, tokens).reshape(rows, width)
    lent = LENT * depth // 10
    kept_rows = depth - lent
    dp = lax.axis_index("dp")
    rolled = xin.reshape(rows, cores, depth)
    rolled = jnp.concatenate([rolled[..., lent:], rolled[..., :lent]], axis=2)
    mine = jnp.where(dp == 0, xin, rolled.reshape(rows, width))
    mine = mine.reshape(zs, 2, rows // frames, cores, depth).transpose(0, 3, 2, 1, 4)
    mine = exchange(mine.reshape(frames, rows // frames, 2 * depth), FRAME).reshape(rows, 2 * depth)

    def lend(*pieces):
        start = dp * (kept_rows - lent)
        cut = [lax.dynamic_slice_in_dim(p, start, lent, 1) for p in pieces]
        return shift(jnp.stack(cut), "dp", 1)

    whole = w_qkv.transpose(1, 0, 2)
    own = lax.dynamic_slice_in_dim(whole, dp * lent, kept_rows, 1)
    rest = lax.dynamic_slice_in_dim(whole, (1 - dp) * kept_rows, lent, 1)
    up1, down1 = shift(own, "z", 1), shift(own, "z", -1)
    mine, up1, down1 = lax.optimization_barrier((mine, up1, down1))
    up2, down2 = shift(up1, "z", 1), shift(down1, "z", -1)
    both = jnp.stack([mine, shift(mine, "yhi", 1)])
    both, w_out, up2, down2, up1, down1 = lax.optimization_barrier(
        (both, w_out, up2, down2, up1, down1)
    )
    left, right = shift(both, "x", 1), shift(both, "x", -1)
    up3, down3 = shift(up2, "z", 1), shift(down2, "z", -1)
    lent1, lent2 = lend(up1, down1), lend(up2, down2)
    blocks = column_blocks(w_out, core1, width)
    left, right, up3, down3, lent1, lent2, blocks = lax.optimization_barrier(
        (left, right, up3, down3, lent1, lent2, blocks)
    )
    middle = rows // 2
    top, low = shift(left[:, :middle], "x", 1), shift(right[:, middle:], "x", -1)
    up4 = shift(up3[:, : kept_rows // 2], "z", 1)
    down4 = shift(down3[:, kept_rows // 2 :], "z", -1)
    lent3 = lend(up3, down3)
    top, low, up4, down4, lent3, blocks = lax.optimization_barrier(
        (top, low, up4, down4, lent3, blocks)
    )
    cut = jnp.where(dp == 0, up4[:, :lent], down4[:, kept_rows // 2 - lent :])
    lent4 = shift(cut, "dp", 1)

    half = exchange(blocks, MP)
    other_half = shift(half, "core", 1)
    out_block = jnp.concatenate(
        [jnp.where(core == 0, half, other_half), jnp.where(core == 0, other_half, half)], axis=1
    )

    x, yhi = lax.axis_index("x"), lax.axis_index("yhi")
    shard = (z + jnp.array([0, zs - 1, 1, zs - 2, 2, zs - 3, 3, zs - 4], jnp.int32)) & (zs - 1)
    slots = (2 * (((shard >> 1) - x) & (mp // 2 - 1)) + ((shard & 1) ^ yhi)).astype(jnp.int32)
    shards = [own, rest, up1, down1, lent1, up2, down2, lent2, up3, down3, lent3, up4, down4, lent4]
    places = [[(0, None), (1, None)]]
    for k in (2, 5, 8):
        places += [[(k, None), (k + 2, 0)], [(k + 1, None), (k + 2, 1)]]
    places.append([(11, None), (12, None), (13, None)])
    kept, sent = project((both, right, top, low, left), shards, places, slots, core1)
    attn = attention(kept, shift(sent, "core", 1), frames)
    attn = exchange(attn, FRAME).reshape(rows, heads)
    all_heads = from_everyone(attn, MP)
    mixed = lax.dot_general(
        all_heads, out_block, (((0, 2), (0, 1)), ((), ())), preferred_element_type=jnp.float32
    ).reshape(clips, spots, width)
    onehot = (action_idx.reshape(clips)[:, None] == jnp.arange(codebook.shape[0])[None, :]).astype(
        jnp.float32
    )
    codevec = jnp.dot(onehot, codebook, precision=lax.Precision.HIGHEST)
    gate = jnp.dot(codevec, act_proj, precision=lax.Precision.HIGHEST)
    xin = xin.reshape(clips, spots, width)
    next_state = (xin.astype(jnp.float32) + gate[:, None, :] * mixed).astype(jnp.bfloat16)
    dgate = jnp.sum(cotangent.reshape(clips, spots, width).astype(jnp.float32) * mixed, axis=1)
    terms = from_everyone(jnp.concatenate([dgate, codevec], axis=1), FRAME + ("dp",))
    terms = terms.reshape(-1, terms.shape[-1])
    grad_proj = lax.dot_general(
        terms[:, width:],
        terms[:, :width],
        (((0,), (0,)), ((), ())),
        precision=lax.Precision.HIGHEST,
        preferred_element_type=jnp.float32,
    )
    return (next_state.reshape(tokens.shape), grad_proj)


def solution(mesh):
    split = Mesh(
        mesh.devices.reshape(mesh.shape["frame"] // 2, 2, mesh.shape["mp"] // 2, 2, mesh.shape["dp"]),
        ("z", "core", "x", "yhi", "dp"),
    )
    return jax.shard_map(
        body,
        mesh=split,
        in_specs=(
            P("dp", FRAME, None, MP),
            P("dp", FRAME, None),
            P(MP),
            P(FRAME, None, MP),
            P(MP, None),
            P("dp", FRAME),
            P(),
            P(None, MP),
            P("dp", FRAME, None, MP),
        ),
        out_specs=(P("dp", FRAME, None, MP), P(None, MP)),
        check_vma=False,
    )
```

```python
import math

import jax
import jax.numpy as jnp
from jax import lax
from jax.experimental import pallas as pl
from jax.experimental.pallas import tpu as pltpu
from jax.sharding import Mesh
from jax.sharding import PartitionSpec as P

HS = 128
MASKED = -1e30
LENT = 2
FRAME = ("z", "core")
MP = ("x", "yhi")
SMALL = pltpu.CompilerParams(vmem_limit_bytes=16 * 1024 * 1024)


def exchange(x, axis):
    return lax.all_to_all(x, axis, split_axis=0, concat_axis=0, tiled=True)


def from_everyone(x, axis):
    return exchange(jnp.broadcast_to(x, (lax.axis_size(axis), *x.shape)), axis)


def shift(x, axis, by):
    n = lax.axis_size(axis)
    return lax.ppermute(x, axis, [(i, (i + by) % n) for i in range(n)])


def qkv_kernel(places, slots, core, *refs):
    n_x, n_w = 5, len(refs) - 12
    (both, right, top, low, left), shards = refs[:n_x], refs[n_x : n_x + n_w]
    kept, sent, x_ref, w_ref, acc, x_sem, w_sem = refs[n_x + n_w :]
    rows, full = x_ref.shape[1], x_ref.shape[2] // 2
    copies, at = [], 0
    for j, pieces in enumerate(places):
        far, own = slots[j] >> 1, slots[j] & 1
        for k, source in ((0, both), (1, right), (3, left)):

            @pl.when(far == k)
            def _():
                pltpu.make_async_copy(source.at[own], x_ref.at[j], x_sem.at[j]).start()

        @pl.when(far == 2)
        def _():
            half = rows // 2
            pltpu.make_async_copy(top.at[own], x_ref.at[j, pl.ds(0, half)], x_sem.at[j]).start()
            pltpu.make_async_copy(low.at[own], x_ref.at[j, pl.ds(half, half)], x_sem.at[j]).start()

        copies.append([])
        row = j * full
        for index, part in pieces:
            source = shards[index] if part is None else shards[index].at[part]
            depth = source.shape[1]
            copy = pltpu.make_async_copy(source, w_ref.at[:, pl.ds(row, depth)], w_sem.at[at])
            copy.start()
            copies[j].append(copy)
            row += depth
            at += 1
    for j in range(0, len(places), 2):
        for i in (j, j + 1):
            pltpu.make_async_copy(both.at[0], x_ref.at[i], x_sem.at[i]).wait()
            for copy in copies[i]:
                copy.wait()
        a, b = x_ref[j], x_ref[j + 1]
        first = jnp.concatenate([a[:, :full], b[:, :full]], axis=1)
        second = jnp.concatenate([a[:, full:], b[:, full:]], axis=1)
        x = jnp.concatenate([first, second], axis=0)
        w = jnp.concatenate([w_ref[i, pl.ds(j * full, 2 * full)] for i in range(3)], axis=1)
        part = jnp.dot(x, w, preferred_element_type=jnp.float32)
        if j == 0:
            acc[...] = part
        else:
            acc[...] += part
    me = core[0]
    kept[...] = acc[pl.ds(me * rows, rows)]
    sent[...] = acc[pl.ds((1 - me) * rows, rows)].astype(jnp.bfloat16)


def project(features, shards, places, slots, core):
    _, rows, width = features[0].shape
    n, heads = len(places), shards[0].shape[-1]
    smem = pl.BlockSpec(memory_space=pltpu.SMEM)
    vmem = pl.BlockSpec(memory_space=pltpu.VMEM)
    hbm = pl.BlockSpec(memory_space=pltpu.HBM)

    def kernel(*refs):
        qkv_kernel(places, *refs)

    return pl.pallas_call(
        kernel,
        in_specs=[smem, smem] + [hbm] * (len(features) + len(shards)),
        out_specs=(vmem, vmem),
        out_shape=(
            jax.ShapeDtypeStruct((rows, 3 * heads), jnp.float32),
            jax.ShapeDtypeStruct((rows, 3 * heads), jnp.bfloat16),
        ),
        scratch_shapes=[
            pltpu.VMEM((n, rows, width), jnp.bfloat16),
            pltpu.VMEM((3, n * width // 2, heads), jnp.bfloat16),
            pltpu.VMEM((2 * rows, 3 * heads), jnp.float32),
            pltpu.SemaphoreType.DMA((n,)),
            pltpu.SemaphoreType.DMA((sum(len(p) for p in places),)),
        ],
        compiler_params=pltpu.CompilerParams(vmem_limit_bytes=28 * 1024 * 1024),
    )(slots, core, *features, *shards)


def attend(q, k, v, bias):
    s = lax.dot_general(q, k, (((1,), (1,)), ((), ())), preferred_element_type=jnp.float32)
    s = s * (1.0 / math.sqrt(HS)) + bias
    peak = jnp.max(s, axis=1, keepdims=True)
    w = jnp.exp(s - peak)
    total = jnp.sum(w, axis=1, keepdims=True)
    high = w.astype(jnp.bfloat16)
    low = (w - high.astype(jnp.float32)).astype(jnp.bfloat16)
    accum = jnp.dot(high, v, preferred_element_type=jnp.float32)
    accum += jnp.dot(low, v, preferred_element_type=jnp.float32)
    return (accum / total).astype(jnp.bfloat16)


def attention_kernel(own_ref, other_ref, bias_ref, out_ref):
    frames, spots, width = out_ref.shape
    bias = bias_ref[...]
    for h in range(width // HS):
        q, k, v = (
            (own_ref[:, cols] + other_ref[:, cols].astype(jnp.float32)).astype(jnp.bfloat16)
            for cols in (slice(i * width + h * HS, i * width + (h + 1) * HS) for i in range(3))
        )
        o = attend(q, k, v, bias)
        for t in range(frames):
            out_ref[t, :, h * HS : (h + 1) * HS] = o[t * spots : (t + 1) * spots]


def attention(own, other, frames):
    rows, heads = own.shape[0], own.shape[1] // 3
    spots = rows // frames
    r = jnp.arange(rows)
    seen = (r[:, None] % spots == r[None, :] % spots) & (r[:, None] >= r[None, :])
    bias = jnp.where(seen, 0.0, MASKED).astype(jnp.float32)
    return pl.pallas_call(
        attention_kernel,
        out_shape=jax.ShapeDtypeStruct((frames, spots, heads), jnp.bfloat16),
        compiler_params=SMALL,
    )(own, other, bias)


def blocks_kernel(core, w_ref, out_ref):
    out_ref[0] = w_ref[...]


def column_blocks(w, core, width):
    heads, full = w.shape
    half, n = heads // 2, full // width
    return pl.pallas_call(
        blocks_kernel,
        grid_spec=pltpu.PrefetchScalarGridSpec(
            num_scalar_prefetch=1,
            grid=(n,),
            in_specs=[pl.BlockSpec((half, width), lambda m, core: (core[0], m))],
            out_specs=pl.BlockSpec((1, half, width), lambda m, core: (m, 0, 0)),
        ),
        out_shape=jax.ShapeDtypeStruct((n, half, width), w.dtype),
        compiler_params=SMALL,
    )(core, w)


def body(tokens, token_mask, mask_embed, w_qkv, w_out, action_idx, codebook, act_proj, cotangent):
    clips, _, spots, width = tokens.shape
    rows = clips * spots
    zs, cores = lax.axis_size("z"), lax.axis_size("core")
    frames, mp = zs * cores, lax.axis_size(MP)
    depth, heads = w_qkv.shape[0], w_qkv.shape[2]
    z, core = lax.axis_index("z"), lax.axis_index("core")
    core1 = core.reshape(1).astype(jnp.int32)
    xin = jnp.where(token_mask[..., None] == 1, mask_embed, tokens).reshape(rows, width)
    lent = LENT * depth // 10
    kept_rows = depth - lent
    dp = lax.axis_index("dp")
    rolled = xin.reshape(rows, cores, depth)
    rolled = jnp.concatenate([rolled[..., lent:], rolled[..., :lent]], axis=2)
    mine = jnp.where(dp == 0, xin, rolled.reshape(rows, width))
    mine = mine.reshape(zs, 2, rows // frames, cores, depth).transpose(0, 3, 2, 1, 4)
    mine = exchange(mine.reshape(frames, rows // frames, 2 * depth), FRAME).reshape(rows, 2 * depth)

    def lend(*pieces):
        start = dp * (kept_rows - lent)
        cut = [lax.dynamic_slice_in_dim(p, start, lent, 1) for p in pieces]
        return shift(jnp.stack(cut), "dp", 1)

    whole = w_qkv.transpose(1, 0, 2)
    own = lax.dynamic_slice_in_dim(whole, dp * lent, kept_rows, 1)
    rest = lax.dynamic_slice_in_dim(whole, (1 - dp) * kept_rows, lent, 1)
    up1, down1 = shift(own, "z", 1), shift(own, "z", -1)
    both = jnp.stack([mine, shift(mine, "yhi", 1)])
    both, w_out, up1, down1 = lax.optimization_barrier((both, w_out, up1, down1))
    left, right = shift(both, "x", 1), shift(both, "x", -1)
    up2, down2 = shift(up1, "z", 1), shift(down1, "z", -1)
    lent1 = lend(up1, down1)
    blocks = column_blocks(w_out, core1, width)
    left, right, up2, down2, lent1, blocks = lax.optimization_barrier(
        (left, right, up2, down2, lent1, blocks)
    )
    middle = rows // 2
    top, low = shift(left[:, :middle], "x", 1), shift(right[:, middle:], "x", -1)
    up3, down3 = shift(up2, "z", 1), shift(down2, "z", -1)
    lent2 = lend(up2, down2)
    up3, down3, top, low, lent2 = lax.optimization_barrier((up3, down3, top, low, lent2))
    up4 = shift(up3[:, : kept_rows // 2], "z", 1)
    down4 = shift(down3[:, kept_rows // 2 :], "z", -1)
    lent3 = lend(up3, down3)
    cut = jnp.where(dp == 0, up4[:, :lent], down4[:, kept_rows // 2 - lent :])
    lent4 = shift(cut, "dp", 1)
    lent3, lent4, blocks = lax.optimization_barrier((lent3, lent4, blocks))

    half = exchange(blocks, MP)
    other_half = shift(half, "core", 1)
    out_block = jnp.concatenate(
        [jnp.where(core == 0, half, other_half), jnp.where(core == 0, other_half, half)], axis=1
    )

    x, yhi = lax.axis_index("x"), lax.axis_index("yhi")
    shard = (z + jnp.array([0, zs - 1, 1, zs - 2, 2, zs - 3, 3, zs - 4], jnp.int32)) & (zs - 1)
    slots = (2 * (((shard >> 1) - x) & (mp // 2 - 1)) + ((shard & 1) ^ yhi)).astype(jnp.int32)
    shards = [own, rest, up1, down1, lent1, up2, down2, lent2, up3, down3, lent3, up4, down4, lent4]
    places = [[(0, None), (1, None)]]
    for k in (2, 5, 8):
        places += [[(k, None), (k + 2, 0)], [(k + 1, None), (k + 2, 1)]]
    places.append([(11, None), (12, None), (13, None)])
    kept, sent = project((both, right, top, low, left), shards, places, slots, core1)
    attn = attention(kept, shift(sent, "core", 1), frames)
    attn = exchange(attn, FRAME).reshape(rows, heads)
    all_heads = from_everyone(attn, MP)
    mixed = lax.dot_general(
        all_heads, out_block, (((0, 2), (0, 1)), ((), ())), preferred_element_type=jnp.float32
    ).reshape(clips, spots, width)
    onehot = (action_idx.reshape(clips)[:, None] == jnp.arange(codebook.shape[0])[None, :]).astype(
        jnp.float32
    )
    codevec = jnp.dot(onehot, codebook, precision=lax.Precision.HIGHEST)
    gate = jnp.dot(codevec, act_proj, precision=lax.Precision.HIGHEST)
    xin = xin.reshape(clips, spots, width)
    next_state = (xin.astype(jnp.float32) + gate[:, None, :] * mixed).astype(jnp.bfloat16)
    dgate = jnp.sum(cotangent.reshape(clips, spots, width).astype(jnp.float32) * mixed, axis=1)
    terms = from_everyone(jnp.concatenate([dgate, codevec], axis=1), FRAME + ("dp",))
    terms = terms.reshape(-1, terms.shape[-1])
    grad_proj = lax.dot_general(
        terms[:, width:],
        terms[:, :width],
        (((0,), (0,)), ((), ())),
        precision=lax.Precision.HIGHEST,
        preferred_element_type=jnp.float32,
    )
    return (next_state.reshape(tokens.shape), grad_proj)


def solution(mesh):
    split = Mesh(
        mesh.devices.reshape(mesh.shape["frame"] // 2, 2, mesh.shape["mp"] // 2, 2, mesh.shape["dp"]),
        ("z", "core", "x", "yhi", "dp"),
    )
    return jax.shard_map(
        body,
        mesh=split,
        in_specs=(
            P("dp", FRAME, None, MP),
            P("dp", FRAME, None),
            P(MP),
            P(FRAME, None, MP),
            P(MP, None),
            P("dp", FRAME),
            P(),
            P(None, MP),
            P("dp", FRAME, None, MP),
        ),
        out_specs=(P("dp", FRAME, None, MP), P(None, MP)),
        check_vma=False,
    )
```

```python
import math

import jax
import jax.numpy as jnp
from jax import lax
from jax.experimental import pallas as pl
from jax.experimental.pallas import tpu as pltpu
from jax.sharding import Mesh
from jax.sharding import PartitionSpec as P

HS = 128
MASKED = -1e30
FRAME = ("z", "core")
MP = ("x", "yhi")
SMALL = pltpu.CompilerParams(vmem_limit_bytes=16 * 1024 * 1024)


def exchange(x, axis):
    return lax.all_to_all(x, axis, split_axis=0, concat_axis=0, tiled=True)


def from_everyone(x, axis):
    return exchange(jnp.broadcast_to(x, (lax.axis_size(axis), *x.shape)), axis)


def shift(x, axis, by):
    n = lax.axis_size(axis)
    return lax.ppermute(x, axis, [(i, (i + by) % n) for i in range(n)])


def qkv_kernel(groups, first, last, slots, core, both, right, top, low, left, *refs):
    pieces = [w for group in groups for w in group]
    count = sum(pieces)
    shards, refs = refs[:count], refs[count:]
    acc_in, refs = (None, refs) if first else (refs[0], refs[1:])
    outs, x_ref = refs[:-1], refs[-1]
    rows, full = x_ref.shape[1], x_ref.shape[2] // 2
    for j in range(len(pieces)):
        far, own = slots[j] >> 1, slots[j] & 1
        for k, source in ((0, both), (1, right), (3, left)):

            @pl.when(far == k)
            def _():
                x_ref[j] = source[own]

        @pl.when(far == 2)
        def _():
            x_ref[j, : rows // 2] = top[own]
            x_ref[j, rows // 2 :] = low[own]

    at, j, acc = 0, 0, outs[0]
    for number, group in enumerate(groups):
        xs = [x_ref[j + i] for i in range(len(group))]
        x = jnp.concatenate(
            [
                jnp.concatenate([x[:, :full] for x in xs], axis=1),
                jnp.concatenate([x[:, full:] for x in xs], axis=1),
            ],
            axis=0,
        )
        use = shards[at : at + sum(group)]
        w = jnp.concatenate(
            [jnp.concatenate([u[i] for u in use], axis=0) for i in range(3)], axis=1
        )
        part = jnp.dot(x, w, preferred_element_type=jnp.float32)
        if number:
            acc[...] += part
        elif first:
            acc[...] = part
        else:
            acc[...] = acc_in[...] + part
        at += len(use)
        j += len(group)
    if last:
        me = core[0]
        outs[1][...] = acc[pl.ds(me * rows, rows)]
        outs[2][...] = acc[pl.ds((1 - me) * rows, rows)].astype(jnp.bfloat16)


def project(features, groups, slots, core, acc=None, last=False):
    _, rows, width = features[0].shape
    counts = [[len(s) for s in group] for group in groups]
    shards = [w for group in groups for s in group for w in s]
    heads = shards[0].shape[-1]
    smem = pl.BlockSpec(memory_space=pltpu.SMEM)
    vmem = pl.BlockSpec(memory_space=pltpu.VMEM)
    out_shape = [jax.ShapeDtypeStruct((2 * rows, 3 * heads), jnp.float32)]
    if last:
        out_shape += [
            jax.ShapeDtypeStruct((rows, 3 * heads), jnp.float32),
            jax.ShapeDtypeStruct((rows, 3 * heads), jnp.bfloat16),
        ]
    operands = [*features, *shards] + ([] if acc is None else [acc])

    def kernel(*refs):
        qkv_kernel(counts, acc is None, last, *refs)

    return pl.pallas_call(
        kernel,
        in_specs=[smem, smem] + [vmem] * len(operands),
        out_specs=[vmem] * len(out_shape),
        out_shape=out_shape,
        input_output_aliases={} if acc is None else {len(operands) + 1: 0},
        scratch_shapes=[pltpu.VMEM((sum(len(c) for c in counts), rows, width), jnp.bfloat16)],
        compiler_params=pltpu.CompilerParams(vmem_limit_bytes=32 * 1024 * 1024),
    )(slots, core, *operands)


def attend(q, k, v, bias):
    s = lax.dot_general(q, k, (((1,), (1,)), ((), ())), preferred_element_type=jnp.float32)
    s = s * (1.0 / math.sqrt(HS)) + bias
    peak = jnp.max(s, axis=1, keepdims=True)
    w = jnp.exp(s - peak)
    total = jnp.sum(w, axis=1, keepdims=True)
    high = w.astype(jnp.bfloat16)
    low = (w - high.astype(jnp.float32)).astype(jnp.bfloat16)
    accum = jnp.dot(high, v, preferred_element_type=jnp.float32)
    accum += jnp.dot(low, v, preferred_element_type=jnp.float32)
    return (accum / total).astype(jnp.bfloat16)


def attention_kernel(own_ref, other_ref, bias_ref, out_ref):
    frames, spots, width = out_ref.shape
    bias = bias_ref[...]
    for h in range(width // HS):
        q, k, v = (
            (own_ref[:, cols] + other_ref[:, cols].astype(jnp.float32)).astype(jnp.bfloat16)
            for cols in (slice(i * width + h * HS, i * width + (h + 1) * HS) for i in range(3))
        )
        o = attend(q, k, v, bias)
        for t in range(frames):
            out_ref[t, :, h * HS : (h + 1) * HS] = o[t * spots : (t + 1) * spots]


def attention(own, other, frames):
    rows, heads = own.shape[0], own.shape[1] // 3
    spots = rows // frames
    r = jnp.arange(rows)
    seen = (r[:, None] % spots == r[None, :] % spots) & (r[:, None] >= r[None, :])
    bias = jnp.where(seen, 0.0, MASKED).astype(jnp.float32)
    return pl.pallas_call(
        attention_kernel,
        out_shape=jax.ShapeDtypeStruct((frames, spots, heads), jnp.bfloat16),
        compiler_params=SMALL,
    )(own, other, bias)


def blocks_kernel(core, w_ref, out_ref):
    out_ref[0] = w_ref[...]


def column_blocks(w, core, width):
    heads, full = w.shape
    half, n = heads // 2, full // width
    return pl.pallas_call(
        blocks_kernel,
        grid_spec=pltpu.PrefetchScalarGridSpec(
            num_scalar_prefetch=1,
            grid=(n,),
            in_specs=[pl.BlockSpec((half, width), lambda m, core: (core[0], m))],
            out_specs=pl.BlockSpec((1, half, width), lambda m, core: (m, 0, 0)),
        ),
        out_shape=jax.ShapeDtypeStruct((n, half, width), w.dtype),
        compiler_params=SMALL,
    )(core, w)


def body(tokens, token_mask, mask_embed, w_qkv, w_out, action_idx, codebook, act_proj, cotangent):
    clips, _, spots, width = tokens.shape
    rows = clips * spots
    zs, cores = lax.axis_size("z"), lax.axis_size("core")
    frames, mp = zs * cores, lax.axis_size(MP)
    depth, heads = w_qkv.shape[0], w_qkv.shape[2]
    z, core = lax.axis_index("z"), lax.axis_index("core")
    core1 = core.reshape(1).astype(jnp.int32)
    xin = jnp.where(token_mask[..., None] == 1, mask_embed, tokens).reshape(rows, width)
    mine = xin.reshape(zs, 2, rows // frames, cores, depth).transpose(0, 3, 2, 1, 4)
    mine = exchange(mine.reshape(frames, rows // frames, 2 * depth), FRAME).reshape(rows, 2 * depth)

    own = w_qkv.transpose(1, 0, 2)
    up1, down1 = shift(own, "z", 1), shift(own, "z", -1)
    both = jnp.stack([mine, shift(mine, "yhi", 1)])
    both, w_out, up1, down1 = lax.optimization_barrier((both, w_out, up1, down1))
    left, right = shift(both, "x", 1), shift(both, "x", -1)
    up2, down2 = shift(up1, "z", 1), shift(down1, "z", -1)
    blocks = column_blocks(w_out, core1, width)
    left, right, up2, down2, blocks = lax.optimization_barrier((left, right, up2, down2, blocks))
    middle = rows // 2
    top, low = shift(left[:, :middle], "x", 1), shift(right[:, middle:], "x", -1)
    up3, down3 = shift(up2, "z", 1), shift(down2, "z", -1)
    up3, down3, top, low, blocks = lax.optimization_barrier((up3, down3, top, low, blocks))
    up4 = shift(up3[:, : depth // 2], "z", 1)
    down4 = shift(down3[:, depth // 2 :], "z", -1)

    half = exchange(blocks, MP)
    other_half = shift(half, "core", 1)
    out_block = jnp.concatenate(
        [jnp.where(core == 0, half, other_half), jnp.where(core == 0, other_half, half)], axis=1
    )

    x, yhi = lax.axis_index("x"), lax.axis_index("yhi")
    shard = (z + jnp.array([0, zs - 1, 1, zs - 2, 2, zs - 3, 3, zs - 4], jnp.int32)) & (zs - 1)
    slots = (2 * (((shard >> 1) - x) & (mp // 2 - 1)) + ((shard & 1) ^ yhi)).astype(jnp.int32)
    features = (both, right, top, low, left)
    early = [[(own,), (up1,)], [(down1,), (up2,)], [(down2,), (up3,)], [(down3,)]]
    (acc,) = project(features, early, slots[:7], core1)
    _, kept, sent = project(features, [[(up4, down4)]], slots[7:], core1, acc, last=True)
    attn = attention(kept, shift(sent, "core", 1), frames)
    attn = exchange(attn, FRAME).reshape(rows, heads)
    all_heads = from_everyone(attn, MP)
    mixed = lax.dot_general(
        all_heads, out_block, (((0, 2), (0, 1)), ((), ())), preferred_element_type=jnp.float32
    ).reshape(clips, spots, width)
    onehot = (action_idx.reshape(clips)[:, None] == jnp.arange(codebook.shape[0])[None, :]).astype(
        jnp.float32
    )
    codevec = jnp.dot(onehot, codebook, precision=lax.Precision.HIGHEST)
    gate = jnp.dot(codevec, act_proj, precision=lax.Precision.HIGHEST)
    xin = xin.reshape(clips, spots, width)
    next_state = (xin.astype(jnp.float32) + gate[:, None, :] * mixed).astype(jnp.bfloat16)
    dgate = jnp.sum(cotangent.reshape(clips, spots, width).astype(jnp.float32) * mixed, axis=1)
    terms = from_everyone(jnp.concatenate([dgate, codevec], axis=1), FRAME + ("dp",))
    terms = terms.reshape(-1, terms.shape[-1])
    grad_proj = lax.dot_general(
        terms[:, width:],
        terms[:, :width],
        (((0,), (0,)), ((), ())),
        precision=lax.Precision.HIGHEST,
        preferred_element_type=jnp.float32,
    )
    return (next_state.reshape(tokens.shape), grad_proj)


def solution(mesh):
    split = Mesh(
        mesh.devices.reshape(mesh.shape["frame"] // 2, 2, mesh.shape["mp"] // 2, 2, mesh.shape["dp"]),
        ("z", "core", "x", "yhi", "dp"),
    )
    return jax.shard_map(
        body,
        mesh=split,
        in_specs=(
            P("dp", FRAME, None, MP),
            P("dp", FRAME, None),
            P(MP),
            P(FRAME, None, MP),
            P(MP, None),
            P("dp", FRAME),
            P(),
            P(None, MP),
            P("dp", FRAME, None, MP),
        ),
        out_specs=(P("dp", FRAME, None, MP), P(None, MP)),
        check_vma=False,
    )
```

```python
import math

import jax
import jax.numpy as jnp
from jax import lax
from jax.experimental import pallas as pl
from jax.experimental.pallas import tpu as pltpu
from jax.sharding import Mesh
from jax.sharding import PartitionSpec as P

HS = 128
MASKED = -1e30
FRAME = ("z", "core")
MP = ("x", "yhi")
SMALL = pltpu.CompilerParams(vmem_limit_bytes=10 * 1024 * 1024)


def exchange(x, axis):
    return lax.all_to_all(x, axis, split_axis=0, concat_axis=0, tiled=True)


def shift(x, axis, by):
    n = lax.axis_size(axis)
    return lax.ppermute(x, axis, [(i, (i + by) % n) for i in range(n)])


def qkv_kernel(groups, first, last, slots, core, both, right, top, low, left, *refs):
    pieces = [w for group in groups for w in group]
    count = sum(pieces)
    shards, refs = refs[:count], refs[count:]
    acc_in, refs = (None, refs) if first else (refs[0], refs[1:])
    outs, x_ref = refs[:-1], refs[-1]
    rows, full = x_ref.shape[1], x_ref.shape[2] // 2
    for j in range(len(pieces)):
        far, own = slots[j] >> 1, slots[j] & 1
        for k, source in ((0, both), (1, right), (3, left)):

            @pl.when(far == k)
            def _():
                x_ref[j] = source[own]

        @pl.when(far == 2)
        def _():
            x_ref[j, : rows // 2] = top[own]
            x_ref[j, rows // 2 :] = low[own]

    at, j, acc = 0, 0, outs[0]
    for number, group in enumerate(groups):
        xs = [x_ref[j + i] for i in range(len(group))]
        x = jnp.concatenate(
            [
                jnp.concatenate([x[:, :full] for x in xs], axis=1),
                jnp.concatenate([x[:, full:] for x in xs], axis=1),
            ],
            axis=0,
        )
        use = shards[at : at + sum(group)]
        w = jnp.concatenate(
            [jnp.concatenate([u[i] for u in use], axis=0) for i in range(3)], axis=1
        )
        part = jnp.dot(x, w, preferred_element_type=jnp.float32)
        if number:
            acc[...] += part
        elif first:
            acc[...] = part
        else:
            acc[...] = acc_in[...] + part
        at += len(use)
        j += len(group)
    if last:
        me = core[0]
        outs[1][...] = acc[pl.ds(me * rows, rows)]
        outs[2][...] = acc[pl.ds((1 - me) * rows, rows)].astype(jnp.bfloat16)


def project(features, groups, slots, core, acc=None, last=False):
    _, rows, width = features[0].shape
    counts = [[len(s) for s in group] for group in groups]
    shards = [w for group in groups for s in group for w in s]
    heads = shards[0].shape[-1]
    smem = pl.BlockSpec(memory_space=pltpu.SMEM)
    vmem = pl.BlockSpec(memory_space=pltpu.VMEM)
    out_shape = [jax.ShapeDtypeStruct((2 * rows, 3 * heads), jnp.float32)]
    if last:
        out_shape += [
            jax.ShapeDtypeStruct((rows, 3 * heads), jnp.float32),
            jax.ShapeDtypeStruct((rows, 3 * heads), jnp.bfloat16),
        ]
    operands = [*features, *shards] + ([] if acc is None else [acc])

    def kernel(*refs):
        qkv_kernel(counts, acc is None, last, *refs)

    return pl.pallas_call(
        kernel,
        in_specs=[smem, smem] + [vmem] * len(operands),
        out_specs=[vmem] * len(out_shape),
        out_shape=out_shape,
        input_output_aliases={} if acc is None else {len(operands) + 1: 0},
        scratch_shapes=[pltpu.VMEM((sum(len(c) for c in counts), rows, width), jnp.bfloat16)],
        compiler_params=pltpu.CompilerParams(vmem_limit_bytes=20 * 1024 * 1024),
    )(slots, core, *operands)


def attend(q, k, v, bias):
    s = lax.dot_general(q, k, (((1,), (1,)), ((), ())), preferred_element_type=jnp.float32)
    s = s * (1.0 / math.sqrt(HS)) + bias
    peak = jnp.max(s, axis=1, keepdims=True)
    w = jnp.exp(s - peak)
    total = jnp.sum(w, axis=1, keepdims=True)
    high = w.astype(jnp.bfloat16)
    low = (w - high.astype(jnp.float32)).astype(jnp.bfloat16)
    accum = jnp.dot(high, v, preferred_element_type=jnp.float32)
    accum += jnp.dot(low, v, preferred_element_type=jnp.float32)
    return (accum / total).astype(jnp.bfloat16)


def attention_kernel(own_ref, other_ref, bias_ref, out_ref):
    frames, spots, width = out_ref.shape
    bias = bias_ref[...]
    for h in range(width // HS):
        q, k, v = (
            (own_ref[:, cols] + other_ref[:, cols].astype(jnp.float32)).astype(jnp.bfloat16)
            for cols in (slice(i * width + h * HS, i * width + (h + 1) * HS) for i in range(3))
        )
        o = attend(q, k, v, bias)
        for t in range(frames):
            out_ref[t, :, h * HS : (h + 1) * HS] = o[t * spots : (t + 1) * spots]


def attention(own, other, frames):
    rows, heads = own.shape[0], own.shape[1] // 3
    spots = rows // frames
    r = jnp.arange(rows)
    seen = (r[:, None] % spots == r[None, :] % spots) & (r[:, None] >= r[None, :])
    bias = jnp.where(seen, 0.0, MASKED).astype(jnp.float32)
    return pl.pallas_call(
        attention_kernel,
        out_shape=jax.ShapeDtypeStruct((frames, spots, heads), jnp.bfloat16),
        compiler_params=SMALL,
    )(own, other, bias)


def out_product(a, where, dx, half, other):
    n = half.shape[0] // 2
    block = 2 * ((where[1] + dx) & (n - 1))
    w = []
    for b in range(2):
        m = block + (b ^ where[2])
        mine, theirs = half[m], other[m]
        first = where[0] == 0
        w += [jnp.where(first, mine, theirs), jnp.where(first, theirs, mine)]
    x = jnp.concatenate(a, axis=1)
    return jnp.dot(x, jnp.concatenate(w, axis=0), preferred_element_type=jnp.float32)


def near_kernel(where, both, right, left, half, other, acc):
    acc[...] = out_product((both[0], both[1]), where, 0, half, other)
    acc[...] += out_product((right[0], right[1]), where, 1, half, other)
    acc[...] += out_product((left[0], left[1]), where, 3, half, other)


def far_kernel(where, top, low, half, other, acc, xin, gate, cot, codevec, next_ref, terms):
    far = tuple(jnp.concatenate([top[b], low[b]], axis=0) for b in range(2))
    mixed = acc[...] + out_product(far, where, 2, half, other)
    rows, width = mixed.shape
    clips = gate.shape[0]
    spots = rows // clips
    sums = []
    for c in range(clips):
        at = slice(c * spots, (c + 1) * spots)
        m = mixed[at]
        moved = xin[at].astype(jnp.float32) + gate[c : c + 1] * m
        next_ref[at] = moved.astype(jnp.bfloat16)
        sums.append(jnp.sum(cot[at].astype(jnp.float32) * m, axis=0, keepdims=True))
    dgate = jnp.concatenate(sums, axis=0)
    for i in range(terms.shape[0]):
        terms[i, :, :width] = dgate
        terms[i, :, width:] = codevec[...]


def near(where, *operands):
    rows, width = operands[0].shape[1], operands[3].shape[2]
    smem, vmem = pl.BlockSpec(memory_space=pltpu.SMEM), pl.BlockSpec(memory_space=pltpu.VMEM)
    return pl.pallas_call(
        near_kernel,
        in_specs=[smem] + [vmem] * 5,
        out_specs=vmem,
        out_shape=jax.ShapeDtypeStruct((rows, width), jnp.float32),
        compiler_params=SMALL,
    )(where, *operands)


def finish(where, peers, *operands):
    rows, width = operands[4].shape
    clips = operands[6].shape[0]
    smem, vmem = pl.BlockSpec(memory_space=pltpu.SMEM), pl.BlockSpec(memory_space=pltpu.VMEM)
    return pl.pallas_call(
        far_kernel,
        in_specs=[smem] + [vmem] * 9,
        out_specs=[vmem, vmem],
        out_shape=[
            jax.ShapeDtypeStruct((rows, width), jnp.bfloat16),
            jax.ShapeDtypeStruct((peers, clips, width + operands[8].shape[1]), jnp.float32),
        ],
        compiler_params=SMALL,
    )(where, *operands)


def blocks_kernel(core, w_ref, out_ref, sem):
    n, half, width = out_ref.shape
    rows = pl.ds(pl.multiple_of(core[0] * half, half), half)
    copies = [
        pltpu.make_async_copy(w_ref.at[rows, pl.ds(m * width, width)], out_ref.at[m], sem.at[m])
        for m in range(n)
    ]
    for copy in copies:
        copy.start()
    for copy in copies:
        copy.wait()


def column_blocks(w, core, width):
    heads, full = w.shape
    half, n = heads // 2, full // width
    hbm = pl.BlockSpec(memory_space=pltpu.HBM)
    return pl.pallas_call(
        blocks_kernel,
        in_specs=[pl.BlockSpec(memory_space=pltpu.SMEM), hbm],
        out_specs=hbm,
        out_shape=jax.ShapeDtypeStruct((n, half, width), w.dtype),
        scratch_shapes=[pltpu.SemaphoreType.DMA((n,))],
        compiler_params=SMALL,
    )(core, w)


def body(tokens, token_mask, mask_embed, w_qkv, w_out, action_idx, codebook, act_proj, cotangent):
    clips, _, spots, width = tokens.shape
    rows = clips * spots
    zs, cores = lax.axis_size("z"), lax.axis_size("core")
    frames, mp = zs * cores, lax.axis_size(MP)
    depth, heads = w_qkv.shape[0], w_qkv.shape[2]
    z, core = lax.axis_index("z"), lax.axis_index("core")
    core1 = core.reshape(1).astype(jnp.int32)
    xin = jnp.where(token_mask[..., None] == 1, mask_embed, tokens).reshape(rows, width)
    mine = xin.reshape(zs, 2, rows // frames, cores, depth).transpose(0, 3, 2, 1, 4)
    mine = exchange(mine.reshape(frames, rows // frames, 2 * depth), FRAME).reshape(rows, 2 * depth)

    own = w_qkv.transpose(1, 0, 2)
    up1, down1 = shift(own, "z", 1), shift(own, "z", -1)
    both = jnp.stack([mine, shift(mine, "yhi", 1)])
    both, w_out, up1, down1 = lax.optimization_barrier((both, w_out, up1, down1))
    left, right = shift(both, "x", 1), shift(both, "x", -1)
    up2, down2 = shift(up1, "z", 1), shift(down1, "z", -1)
    blocks = column_blocks(w_out, core1, width)
    left, right, up2, down2, blocks = lax.optimization_barrier((left, right, up2, down2, blocks))
    middle = rows // 2
    top, low = shift(left[:, :middle], "x", 1), shift(right[:, middle:], "x", -1)
    up3, down3 = shift(up2, "z", 1), shift(down2, "z", -1)
    top, low, blocks = lax.optimization_barrier((top, low, blocks))
    up3, down3, top, low = lax.optimization_barrier((up3, down3, top, low))
    up4 = shift(up3[:, : depth // 2], "z", 1)
    down4 = shift(down3[:, depth // 2 :], "z", -1)

    half = exchange(blocks, MP)

    x, yhi = lax.axis_index("x"), lax.axis_index("yhi")
    shard = (z + jnp.array([0, zs - 1, 1, zs - 2, 2, zs - 3, 3, zs - 4], jnp.int32)) & (zs - 1)
    slots = (2 * (((shard >> 1) - x) & (mp // 2 - 1)) + ((shard & 1) ^ yhi)).astype(jnp.int32)
    features = (both, right, top, low, left)
    early = [[(own,), (up1,)], [(down1,), (up2,)], [(down2,), (up3,)], [(down3,)]]
    (acc,) = project(features, early, slots[:7], core1)
    _, kept, sent = project(features, [[(up4, down4)]], slots[7:], core1, acc, last=True)
    attn = attention(kept, shift(sent, "core", 1), frames)
    attn, half = lax.optimization_barrier((attn, half))
    other_half = shift(half, "core", 1)
    attn = exchange(attn, FRAME).reshape(rows, heads)
    attn_both = jnp.stack([attn, shift(attn, "yhi", 1)])
    attn_left, attn_right = shift(attn_both, "x", 1), shift(attn_both, "x", -1)
    attn_top = shift(attn_left[:, :middle], "x", 1)
    attn_low = shift(attn_right[:, middle:], "x", -1)
    where = jnp.stack([core, x, yhi]).astype(jnp.int32)
    acc = near(where, attn_both, attn_right, attn_left, half, other_half)
    onehot = (action_idx.reshape(clips)[:, None] == jnp.arange(codebook.shape[0])[None, :]).astype(
        jnp.float32
    )
    codevec = jnp.dot(onehot, codebook, precision=lax.Precision.HIGHEST)
    gate = jnp.dot(codevec, act_proj, precision=lax.Precision.HIGHEST)
    peers = frames * lax.axis_size("dp")
    next_state, terms = finish(
        where, peers, attn_top, attn_low, half, other_half, acc, xin, gate,
        cotangent.reshape(rows, width), codevec,
    )
    terms = exchange(terms, FRAME + ("dp",))
    terms = terms.reshape(-1, terms.shape[-1])
    grad_proj = lax.dot_general(
        terms[:, width:],
        terms[:, :width],
        (((0,), (0,)), ((), ())),
        precision=lax.Precision.HIGHEST,
        preferred_element_type=jnp.float32,
    )
    return (next_state.reshape(tokens.shape), grad_proj)


def solution(mesh):
    split = Mesh(
        mesh.devices.reshape(mesh.shape["frame"] // 2, 2, mesh.shape["mp"] // 2, 2, mesh.shape["dp"]),
        ("z", "core", "x", "yhi", "dp"),
    )
    return jax.shard_map(
        body,
        mesh=split,
        in_specs=(
            P("dp", FRAME, None, MP),
            P("dp", FRAME, None),
            P(MP),
            P(FRAME, None, MP),
            P(MP, None),
            P("dp", FRAME),
            P(),
            P(None, MP),
            P("dp", FRAME, None, MP),
        ),
        out_specs=(P("dp", FRAME, None, MP), P(None, MP)),
        check_vma=False,
    )
```

```python
import math

import jax
import jax.numpy as jnp
from jax import lax
from jax.experimental import pallas as pl
from jax.experimental.pallas import tpu as pltpu
from jax.sharding import Mesh
from jax.sharding import PartitionSpec as P

HS = 128
MASKED = -1e30
QKV_VMEM = 58
FRAME = ("z", "core")
MP = ("x", "yhi")
SMALL = pltpu.CompilerParams(vmem_limit_bytes=10 * 1024 * 1024)


def exchange(x, axis):
    return lax.all_to_all(x, axis, split_axis=0, concat_axis=0, tiled=True)


def shift(x, axis, by):
    n = lax.axis_size(axis)
    return lax.ppermute(x, axis, [(i, (i + by) % n) for i in range(n)])


def qkv_kernel(groups, first, last, slots, core, both, right, top, low, left, *refs):
    pieces = [w for group in groups for w in group]
    count = sum(pieces)
    shards, refs = refs[:count], refs[count:]
    acc_in, refs = (None, refs) if first else (refs[0], refs[1:])
    outs, (x_ref, w_ref, x_sem, w_sem) = refs[:-4], refs[-4:]
    acc = outs[-1]
    rows, full = x_ref.shape[1], x_ref.shape[2] // 2
    copies, at = [], 0
    for j, n in enumerate(pieces):
        far, own = slots[j] >> 1, slots[j] & 1
        for k, source in ((0, both), (1, right), (3, left)):

            @pl.when(far == k)
            def _():
                pltpu.make_async_copy(source.at[own], x_ref.at[j], x_sem.at[j]).start()

        @pl.when(far == 2)
        def _():
            half = rows // 2
            pltpu.make_async_copy(top.at[own], x_ref.at[j, pl.ds(0, half)], x_sem.at[j]).start()
            pltpu.make_async_copy(low.at[own], x_ref.at[j, pl.ds(half, half)], x_sem.at[j]).start()

        copies.append([])
        row = j * full
        for source in shards[at : at + n]:
            depth = source.shape[1]
            copy = pltpu.make_async_copy(source, w_ref.at[:, pl.ds(row, depth)], w_sem.at[at])
            copy.start()
            copies[j].append(copy)
            row += depth
            at += 1

    j = 0
    for number, group in enumerate(groups):
        for i in range(j, j + len(group)):
            pltpu.make_async_copy(both.at[0], x_ref.at[i], x_sem.at[i]).wait()
            for copy in copies[i]:
                copy.wait()
        xs = [x_ref[j + i] for i in range(len(group))]
        x = jnp.concatenate(
            [
                jnp.concatenate([x[:, :full] for x in xs], axis=1),
                jnp.concatenate([x[:, full:] for x in xs], axis=1),
            ],
            axis=0,
        )
        span = pl.ds(j * full, len(group) * full)
        w = jnp.concatenate([w_ref[i, span] for i in range(3)], axis=1)
        part = jnp.dot(x, w, preferred_element_type=jnp.float32)
        if number:
            acc[...] += part
        elif first:
            acc[...] = part
        else:
            acc[...] = acc_in[...] + part
        j += len(group)
    if last:
        me = core[0]
        outs[0][...] = acc[pl.ds(me * rows, rows)]
        outs[1][...] = acc[pl.ds((1 - me) * rows, rows)].astype(jnp.bfloat16)


def project(features, groups, slots, core, acc=None, last=False):
    _, rows, width = features[0].shape
    counts = [[len(s) for s in group] for group in groups]
    shards = [w for group in groups for s in group for w in s]
    heads = shards[0].shape[-1]
    smem = pl.BlockSpec(memory_space=pltpu.SMEM)
    vmem = pl.BlockSpec(memory_space=pltpu.VMEM)
    anywhere = pl.BlockSpec(memory_space=pl.ANY)
    total = (2 * rows, 3 * heads)
    if last:
        out_shape = [
            jax.ShapeDtypeStruct((rows, 3 * heads), jnp.float32),
            jax.ShapeDtypeStruct((rows, 3 * heads), jnp.bfloat16),
        ]
    else:
        out_shape = [jax.ShapeDtypeStruct(total, jnp.float32)]
    pieces = [*features, *shards]
    operands = pieces + ([] if acc is None else [acc])
    n = sum(len(c) for c in counts)

    def kernel(*refs):
        qkv_kernel(counts, acc is None, last, *refs)

    return pl.pallas_call(
        kernel,
        in_specs=[smem, smem] + [anywhere] * len(pieces) + ([] if acc is None else [vmem]),
        out_specs=[vmem] * len(out_shape),
        out_shape=out_shape,
        scratch_shapes=([pltpu.VMEM(total, jnp.float32)] if last else [])
        + [
            pltpu.VMEM((n, rows, width), jnp.bfloat16),
            pltpu.VMEM((3, n * width // 2, heads), jnp.bfloat16),
            pltpu.SemaphoreType.DMA((n,)),
            pltpu.SemaphoreType.DMA((len(shards),)),
        ],
        compiler_params=pltpu.CompilerParams(vmem_limit_bytes=QKV_VMEM << 20),
    )(slots, core, *operands)


def attend(q, k, v, bias):
    s = lax.dot_general(q, k, (((1,), (1,)), ((), ())), preferred_element_type=jnp.float32)
    s = s * (1.0 / math.sqrt(HS)) + bias
    peak = jnp.max(s, axis=1, keepdims=True)
    w = jnp.exp(s - peak)
    total = jnp.sum(w, axis=1, keepdims=True)
    high = w.astype(jnp.bfloat16)
    low = (w - high.astype(jnp.float32)).astype(jnp.bfloat16)
    accum = jnp.dot(high, v, preferred_element_type=jnp.float32)
    accum += jnp.dot(low, v, preferred_element_type=jnp.float32)
    return (accum / total).astype(jnp.bfloat16)


def attention_kernel(own_ref, other_ref, bias_ref, out_ref):
    frames, spots, width = out_ref.shape
    bias = bias_ref[...]
    for h in range(width // HS):
        q, k, v = (
            (own_ref[:, cols] + other_ref[:, cols].astype(jnp.float32)).astype(jnp.bfloat16)
            for cols in (slice(i * width + h * HS, i * width + (h + 1) * HS) for i in range(3))
        )
        o = attend(q, k, v, bias)
        for t in range(frames):
            out_ref[t, :, h * HS : (h + 1) * HS] = o[t * spots : (t + 1) * spots]


def attention(own, other, frames):
    rows, heads = own.shape[0], own.shape[1] // 3
    spots = rows // frames
    r = jnp.arange(rows)
    seen = (r[:, None] % spots == r[None, :] % spots) & (r[:, None] >= r[None, :])
    bias = jnp.where(seen, 0.0, MASKED).astype(jnp.float32)
    return pl.pallas_call(
        attention_kernel,
        out_shape=jax.ShapeDtypeStruct((frames, spots, heads), jnp.bfloat16),
        compiler_params=SMALL,
    )(own, other, bias)


def out_product(a, where, dx, half, other):
    n = half.shape[0] // 2
    block = 2 * ((where[1] + dx) & (n - 1))
    w = []
    for b in range(2):
        m = block + (b ^ where[2])
        mine, theirs = half[m], other[m]
        first = where[0] == 0
        w += [jnp.where(first, mine, theirs), jnp.where(first, theirs, mine)]
    x = jnp.concatenate(a, axis=1)
    return jnp.dot(x, jnp.concatenate(w, axis=0), preferred_element_type=jnp.float32)


def near_kernel(where, both, right, left, half, other, acc):
    acc[...] = out_product((both[0], both[1]), where, 0, half, other)
    acc[...] += out_product((right[0], right[1]), where, 1, half, other)
    acc[...] += out_product((left[0], left[1]), where, 3, half, other)


def far_kernel(where, top, low, half, other, acc, xin, gate, cot, codevec, next_ref, terms):
    far = tuple(jnp.concatenate([top[b], low[b]], axis=0) for b in range(2))
    mixed = acc[...] + out_product(far, where, 2, half, other)
    rows, width = mixed.shape
    clips = gate.shape[0]
    spots = rows // clips
    sums = []
    for c in range(clips):
        at = slice(c * spots, (c + 1) * spots)
        m = mixed[at]
        moved = xin[at].astype(jnp.float32) + gate[c : c + 1] * m
        next_ref[at] = moved.astype(jnp.bfloat16)
        sums.append(jnp.sum(cot[at].astype(jnp.float32) * m, axis=0, keepdims=True))
    dgate = jnp.concatenate(sums, axis=0)
    for i in range(terms.shape[0]):
        terms[i, :, :width] = dgate
        terms[i, :, width:] = codevec[...]


def near(where, *operands):
    rows, width = operands[0].shape[1], operands[3].shape[2]
    smem, vmem = pl.BlockSpec(memory_space=pltpu.SMEM), pl.BlockSpec(memory_space=pltpu.VMEM)
    return pl.pallas_call(
        near_kernel,
        in_specs=[smem] + [vmem] * 5,
        out_specs=vmem,
        out_shape=jax.ShapeDtypeStruct((rows, width), jnp.float32),
        compiler_params=SMALL,
    )(where, *operands)


def finish(where, peers, *operands):
    rows, width = operands[4].shape
    clips = operands[6].shape[0]
    smem, vmem = pl.BlockSpec(memory_space=pltpu.SMEM), pl.BlockSpec(memory_space=pltpu.VMEM)
    return pl.pallas_call(
        far_kernel,
        in_specs=[smem] + [vmem] * 9,
        out_specs=[vmem, vmem],
        out_shape=[
            jax.ShapeDtypeStruct((rows, width), jnp.bfloat16),
            jax.ShapeDtypeStruct((peers, clips, width + operands[8].shape[1]), jnp.float32),
        ],
        compiler_params=SMALL,
    )(where, *operands)


def blocks_kernel(core, w_ref, out_ref, sem):
    n, half, width = out_ref.shape
    rows = pl.ds(pl.multiple_of(core[0] * half, half), half)
    copies = [
        pltpu.make_async_copy(w_ref.at[rows, pl.ds(m * width, width)], out_ref.at[m], sem.at[m])
        for m in range(n)
    ]
    for copy in copies:
        copy.start()
    for copy in copies:
        copy.wait()


def column_blocks(w, core, width):
    heads, full = w.shape
    half, n = heads // 2, full // width
    hbm = pl.BlockSpec(memory_space=pltpu.HBM)
    return pl.pallas_call(
        blocks_kernel,
        in_specs=[pl.BlockSpec(memory_space=pltpu.SMEM), hbm],
        out_specs=hbm,
        out_shape=jax.ShapeDtypeStruct((n, half, width), w.dtype),
        scratch_shapes=[pltpu.SemaphoreType.DMA((n,))],
        compiler_params=SMALL,
    )(core, w)


def body(tokens, token_mask, mask_embed, w_qkv, w_out, action_idx, codebook, act_proj, cotangent):
    clips, _, spots, width = tokens.shape
    rows = clips * spots
    zs, cores = lax.axis_size("z"), lax.axis_size("core")
    frames, mp = zs * cores, lax.axis_size(MP)
    depth, heads = w_qkv.shape[0], w_qkv.shape[2]
    z, core = lax.axis_index("z"), lax.axis_index("core")
    core1 = core.reshape(1).astype(jnp.int32)
    xin = jnp.where(token_mask[..., None] == 1, mask_embed, tokens).reshape(rows, width)
    mine = xin.reshape(zs, 2, rows // frames, cores, depth).transpose(0, 3, 2, 1, 4)
    mine = exchange(mine.reshape(frames, rows // frames, 2 * depth), FRAME).reshape(rows, 2 * depth)

    own = w_qkv.transpose(1, 0, 2)
    up1, down1 = shift(own, "z", 1), shift(own, "z", -1)
    both = jnp.stack([mine, shift(mine, "yhi", 1)])
    both, w_out, up1, down1 = lax.optimization_barrier((both, w_out, up1, down1))
    left, right = shift(both, "x", 1), shift(both, "x", -1)
    up2, down2 = shift(up1, "z", 1), shift(down1, "z", -1)
    blocks = column_blocks(w_out, core1, width)
    left, right, up2, down2, blocks = lax.optimization_barrier((left, right, up2, down2, blocks))
    middle = rows // 2
    top, low = shift(left[:, :middle], "x", 1), shift(right[:, middle:], "x", -1)
    up3, down3 = shift(up2, "z", 1), shift(down2, "z", -1)
    top, low, blocks = lax.optimization_barrier((top, low, blocks))
    up3, down3, top, low = lax.optimization_barrier((up3, down3, top, low))
    up4 = shift(up3[:, : depth // 2], "z", 1)
    down4 = shift(down3[:, depth // 2 :], "z", -1)

    half = exchange(blocks, MP)

    x, yhi = lax.axis_index("x"), lax.axis_index("yhi")
    shard = (z + jnp.array([0, zs - 1, 1, zs - 2, 2, zs - 3, 3, zs - 4], jnp.int32)) & (zs - 1)
    slots = (2 * (((shard >> 1) - x) & (mp // 2 - 1)) + ((shard & 1) ^ yhi)).astype(jnp.int32)
    features = (both, right, top, low, left)
    early = [[(own,), (up1,)], [(down1,), (up2,)], [(down2,), (up3,)], [(down3,)]]
    (acc,) = project(features, early, slots[:7], core1)
    kept, sent = project(features, [[(up4, down4)]], slots[7:], core1, acc, last=True)
    attn = attention(kept, shift(sent, "core", 1), frames)
    attn, half = lax.optimization_barrier((attn, half))
    other_half = shift(half, "core", 1)
    attn = exchange(attn, FRAME).reshape(rows, heads)
    attn_both = jnp.stack([attn, shift(attn, "yhi", 1)])
    attn_left, attn_right = shift(attn_both, "x", 1), shift(attn_both, "x", -1)
    attn_top = shift(attn_left[:, :middle], "x", 1)
    attn_low = shift(attn_right[:, middle:], "x", -1)
    where = jnp.stack([core, x, yhi]).astype(jnp.int32)
    acc = near(where, attn_both, attn_right, attn_left, half, other_half)
    onehot = (action_idx.reshape(clips)[:, None] == jnp.arange(codebook.shape[0])[None, :]).astype(
        jnp.float32
    )
    codevec = jnp.dot(onehot, codebook, precision=lax.Precision.HIGHEST)
    gate = jnp.dot(codevec, act_proj, precision=lax.Precision.HIGHEST)
    peers = frames * lax.axis_size("dp")
    next_state, terms = finish(
        where, peers, attn_top, attn_low, half, other_half, acc, xin, gate,
        cotangent.reshape(rows, width), codevec,
    )
    terms = exchange(terms, FRAME + ("dp",))
    terms = terms.reshape(-1, terms.shape[-1])
    grad_proj = lax.dot_general(
        terms[:, width:],
        terms[:, :width],
        (((0,), (0,)), ((), ())),
        precision=lax.Precision.HIGHEST,
        preferred_element_type=jnp.float32,
    )
    return (next_state.reshape(tokens.shape), grad_proj)


def solution(mesh):
    split = Mesh(
        mesh.devices.reshape(mesh.shape["frame"] // 2, 2, mesh.shape["mp"] // 2, 2, mesh.shape["dp"]),
        ("z", "core", "x", "yhi", "dp"),
    )
    return jax.shard_map(
        body,
        mesh=split,
        in_specs=(
            P("dp", FRAME, None, MP),
            P("dp", FRAME, None),
            P(MP),
            P(FRAME, None, MP),
            P(MP, None),
            P("dp", FRAME),
            P(),
            P(None, MP),
            P("dp", FRAME, None, MP),
        ),
        out_specs=(P("dp", FRAME, None, MP), P(None, MP)),
        check_vma=False,
    )
```

```python
import math

import jax
import jax.numpy as jnp
from jax import lax
from jax.experimental import pallas as pl
from jax.experimental.pallas import tpu as pltpu
from jax.sharding import Mesh
from jax.sharding import PartitionSpec as P

HS = 128
MASKED = -1e30
QKV_VMEM = 58
SMEM = pl.BlockSpec(memory_space=pltpu.SMEM)
WHOLE = pl.BlockSpec(memory_space=pltpu.VMEM)
ANYWHERE = pl.BlockSpec(memory_space=pl.ANY)
FRAME = ("z", "core")
MP = ("x", "yhi")
SMALL = pltpu.CompilerParams(vmem_limit_bytes=10 * 1024 * 1024)


def exchange(x, axis):
    return lax.all_to_all(x, axis, split_axis=0, concat_axis=0, tiled=True)


def shift(x, axis, by):
    n = lax.axis_size(axis)
    return lax.ppermute(x, axis, [(i, (i + by) % n) for i in range(n)])


def fetch_features(slot, both, right, top, low, left, target, sem):
    far, own = slot >> 1, slot & 1
    for k, source in ((0, both), (1, right), (3, left)):

        @pl.when(far == k)
        def _():
            pltpu.make_async_copy(source.at[own], target, sem).start()

    @pl.when(far == 2)
    def _():
        half = target.shape[0] // 2
        pltpu.make_async_copy(top.at[own], target.at[pl.ds(0, half)], sem).start()
        pltpu.make_async_copy(low.at[own], target.at[pl.ds(half, half)], sem).start()


def qkv_kernel(groups, slots, both, right, top, low, left, *refs):
    pieces = [w for group in groups for w in group]
    count = sum(pieces)
    shards, refs = refs[:count], refs[count:]
    acc, x_ref, w_ref, x_sem, w_sem = refs
    rows, full = x_ref.shape[1], x_ref.shape[2] // 2
    copies, at = [], 0
    for j, n in enumerate(pieces):
        fetch_features(slots[j], both, right, top, low, left, x_ref.at[j], x_sem.at[j])
        copies.append([])
        row = j * full
        for source in shards[at : at + n]:
            depth = source.shape[1]
            copy = pltpu.make_async_copy(source, w_ref.at[:, pl.ds(row, depth)], w_sem.at[at])
            copy.start()
            copies[j].append(copy)
            row += depth
            at += 1

    j = 0
    for number, group in enumerate(groups):
        for i in range(j, j + len(group)):
            pltpu.make_async_copy(both.at[0], x_ref.at[i], x_sem.at[i]).wait()
            for copy in copies[i]:
                copy.wait()
        xs = [x_ref[j + i] for i in range(len(group))]
        x = jnp.concatenate(
            [
                jnp.concatenate([x[:, :full] for x in xs], axis=1),
                jnp.concatenate([x[:, full:] for x in xs], axis=1),
            ],
            axis=0,
        )
        span = pl.ds(j * full, len(group) * full)
        w = jnp.concatenate([w_ref[i, span] for i in range(3)], axis=1)
        part = jnp.dot(x, w, preferred_element_type=jnp.float32)
        if number:
            acc[...] += part
        else:
            acc[...] = part
        j += len(group)


def project(features, groups, slots):
    _, rows, width = features[0].shape
    counts = [[len(s) for s in group] for group in groups]
    shards = [w for group in groups for s in group for w in s]
    heads = shards[0].shape[-1]
    operands = [*features, *shards]
    n = sum(len(c) for c in counts)

    def kernel(*refs):
        qkv_kernel(counts, *refs)

    return pl.pallas_call(
        kernel,
        in_specs=[SMEM] + [ANYWHERE] * len(operands),
        out_specs=WHOLE,
        out_shape=jax.ShapeDtypeStruct((2 * rows, 3 * heads), jnp.float32),
        scratch_shapes=[
            pltpu.VMEM((n, rows, width), jnp.bfloat16),
            pltpu.VMEM((3, n * width // 2, heads), jnp.bfloat16),
            pltpu.SemaphoreType.DMA((n,)),
            pltpu.SemaphoreType.DMA((len(shards),)),
        ],
        compiler_params=pltpu.CompilerParams(vmem_limit_bytes=QKV_VMEM << 20),
    )(slots, *operands)


def last_kernel(slots, side, both, right, top, low, left, first, second, acc, out, *refs):
    x_ref, w_ref, acc_ref, x_sem, w_sem = refs
    rows, full = x_ref.shape[0], x_ref.shape[1] // 2
    depth = first.shape[1]
    at = pl.multiple_of(side[0] * rows, rows)
    copies = [
        pltpu.make_async_copy(acc.at[pl.ds(at, rows)], acc_ref, w_sem.at[0]),
        pltpu.make_async_copy(first, w_ref.at[:, pl.ds(0, depth)], w_sem.at[1]),
        pltpu.make_async_copy(second, w_ref.at[:, pl.ds(depth, depth)], w_sem.at[2]),
    ]
    fetch_features(slots[0], both, right, top, low, left, x_ref, x_sem.at[0])
    for copy in copies:
        copy.start()
    pltpu.make_async_copy(both.at[0], x_ref, x_sem.at[0]).wait()
    for copy in copies:
        copy.wait()
    x = jnp.where(side[0] == 0, x_ref[:, :full], x_ref[:, full:])
    w = jnp.concatenate([w_ref[i] for i in range(3)], axis=1)
    total = acc_ref[...] + jnp.dot(x, w, preferred_element_type=jnp.float32)
    out[...] = total.astype(out.dtype)


def project_last(features, shard, slots, acc, side, dtype):
    _, rows, width = features[0].shape
    total, heads = acc.shape[1], shard[0].shape[-1]
    return pl.pallas_call(
        last_kernel,
        in_specs=[SMEM, SMEM] + [ANYWHERE] * (len(features) + 3),
        out_specs=WHOLE,
        out_shape=jax.ShapeDtypeStruct((rows, total), dtype),
        scratch_shapes=[
            pltpu.VMEM((rows, width), jnp.bfloat16),
            pltpu.VMEM((3, width // 2, heads), jnp.bfloat16),
            pltpu.VMEM((rows, total), jnp.float32),
            pltpu.SemaphoreType.DMA((1,)),
            pltpu.SemaphoreType.DMA((3,)),
        ],
        compiler_params=pltpu.CompilerParams(vmem_limit_bytes=QKV_VMEM << 20),
    )(slots, side, *features, *shard, acc)


def attend(q, k, v, bias):
    s = lax.dot_general(q, k, (((1,), (1,)), ((), ())), preferred_element_type=jnp.float32)
    s = s * (1.0 / math.sqrt(HS)) + bias
    peak = jnp.max(s, axis=1, keepdims=True)
    w = jnp.exp(s - peak)
    total = jnp.sum(w, axis=1, keepdims=True)
    high = w.astype(jnp.bfloat16)
    low = (w - high.astype(jnp.float32)).astype(jnp.bfloat16)
    accum = jnp.dot(high, v, preferred_element_type=jnp.float32)
    accum += jnp.dot(low, v, preferred_element_type=jnp.float32)
    return (accum / total).astype(jnp.bfloat16)


def attention_kernel(own_ref, other_ref, bias_ref, out_ref):
    frames, spots, width = out_ref.shape
    bias = bias_ref[...]
    for h in range(width // HS):
        q, k, v = (
            (own_ref[:, cols] + other_ref[:, cols].astype(jnp.float32)).astype(jnp.bfloat16)
            for cols in (slice(i * width + h * HS, i * width + (h + 1) * HS) for i in range(3))
        )
        o = attend(q, k, v, bias)
        for t in range(frames):
            out_ref[t, :, h * HS : (h + 1) * HS] = o[t * spots : (t + 1) * spots]


def attention(own, other, frames):
    rows, heads = own.shape[0], own.shape[1] // 3
    spots = rows // frames
    r = jnp.arange(rows)
    seen = (r[:, None] % spots == r[None, :] % spots) & (r[:, None] >= r[None, :])
    bias = jnp.where(seen, 0.0, MASKED).astype(jnp.float32)
    return pl.pallas_call(
        attention_kernel,
        out_shape=jax.ShapeDtypeStruct((frames, spots, heads), jnp.bfloat16),
        compiler_params=SMALL,
    )(own, other, bias)


def out_product(a, where, dx, half, other):
    n = half.shape[0] // 2
    block = 2 * ((where[1] + dx) & (n - 1))
    w = []
    for b in range(2):
        m = block + (b ^ where[2])
        mine, theirs = half[m], other[m]
        first = where[0] == 0
        w += [jnp.where(first, mine, theirs), jnp.where(first, theirs, mine)]
    x = jnp.concatenate(a, axis=1)
    return jnp.dot(x, jnp.concatenate(w, axis=0), preferred_element_type=jnp.float32)


def near_kernel(where, both, right, left, half, other, acc):
    acc[...] = out_product((both[0], both[1]), where, 0, half, other)
    acc[...] += out_product((right[0], right[1]), where, 1, half, other)
    acc[...] += out_product((left[0], left[1]), where, 3, half, other)


def far_kernel(where, top, low, half, other, acc, xin, gate, cot, codevec, next_ref, terms):
    far = tuple(jnp.concatenate([top[b], low[b]], axis=0) for b in range(2))
    mixed = acc[...] + out_product(far, where, 2, half, other)
    rows, width = mixed.shape
    clips = gate.shape[0]
    spots = rows // clips
    sums = []
    for c in range(clips):
        at = slice(c * spots, (c + 1) * spots)
        m = mixed[at]
        moved = xin[at].astype(jnp.float32) + gate[c : c + 1] * m
        next_ref[at] = moved.astype(jnp.bfloat16)
        sums.append(jnp.sum(cot[at].astype(jnp.float32) * m, axis=0, keepdims=True))
    dgate = jnp.concatenate(sums, axis=0)
    for i in range(terms.shape[0]):
        terms[i, :, :width] = dgate
        terms[i, :, width:] = codevec[...]


def near(where, *operands):
    rows, width = operands[0].shape[1], operands[3].shape[2]
    smem, vmem = pl.BlockSpec(memory_space=pltpu.SMEM), pl.BlockSpec(memory_space=pltpu.VMEM)
    return pl.pallas_call(
        near_kernel,
        in_specs=[smem] + [vmem] * 5,
        out_specs=vmem,
        out_shape=jax.ShapeDtypeStruct((rows, width), jnp.float32),
        compiler_params=SMALL,
    )(where, *operands)


def finish(where, peers, *operands):
    rows, width = operands[4].shape
    clips = operands[6].shape[0]
    smem, vmem = pl.BlockSpec(memory_space=pltpu.SMEM), pl.BlockSpec(memory_space=pltpu.VMEM)
    return pl.pallas_call(
        far_kernel,
        in_specs=[smem] + [vmem] * 9,
        out_specs=[vmem, vmem],
        out_shape=[
            jax.ShapeDtypeStruct((rows, width), jnp.bfloat16),
            jax.ShapeDtypeStruct((peers, clips, width + operands[8].shape[1]), jnp.float32),
        ],
        compiler_params=SMALL,
    )(where, *operands)


def blocks_kernel(core, w_ref, out_ref, sem):
    n, half, width = out_ref.shape
    rows = pl.ds(pl.multiple_of(core[0] * half, half), half)
    copies = [
        pltpu.make_async_copy(w_ref.at[rows, pl.ds(m * width, width)], out_ref.at[m], sem.at[m])
        for m in range(n)
    ]
    for copy in copies:
        copy.start()
    for copy in copies:
        copy.wait()


def column_blocks(w, core, width):
    heads, full = w.shape
    half, n = heads // 2, full // width
    hbm = pl.BlockSpec(memory_space=pltpu.HBM)
    return pl.pallas_call(
        blocks_kernel,
        in_specs=[pl.BlockSpec(memory_space=pltpu.SMEM), hbm],
        out_specs=hbm,
        out_shape=jax.ShapeDtypeStruct((n, half, width), w.dtype),
        scratch_shapes=[pltpu.SemaphoreType.DMA((n,))],
        compiler_params=SMALL,
    )(core, w)


def body(tokens, token_mask, mask_embed, w_qkv, w_out, action_idx, codebook, act_proj, cotangent):
    clips, _, spots, width = tokens.shape
    rows = clips * spots
    zs, cores = lax.axis_size("z"), lax.axis_size("core")
    frames, mp = zs * cores, lax.axis_size(MP)
    depth, heads = w_qkv.shape[0], w_qkv.shape[2]
    z, core = lax.axis_index("z"), lax.axis_index("core")
    core1 = core.reshape(1).astype(jnp.int32)
    xin = jnp.where(token_mask[..., None] == 1, mask_embed, tokens).reshape(rows, width)
    mine = xin.reshape(zs, 2, rows // frames, cores, depth).transpose(0, 3, 2, 1, 4)
    mine = exchange(mine.reshape(frames, rows // frames, 2 * depth), FRAME).reshape(rows, 2 * depth)

    own = w_qkv.transpose(1, 0, 2)
    up1, down1 = shift(own, "z", 1), shift(own, "z", -1)
    both = jnp.stack([mine, shift(mine, "yhi", 1)])
    both, w_out, up1, down1 = lax.optimization_barrier((both, w_out, up1, down1))
    left, right = shift(both, "x", 1), shift(both, "x", -1)
    up2, down2 = shift(up1, "z", 1), shift(down1, "z", -1)
    blocks = column_blocks(w_out, core1, width)
    left, right, up2, down2, blocks = lax.optimization_barrier((left, right, up2, down2, blocks))
    middle = rows // 2
    top, low = shift(left[:, :middle], "x", 1), shift(right[:, middle:], "x", -1)
    up3, down3 = shift(up2, "z", 1), shift(down2, "z", -1)
    top, low, blocks = lax.optimization_barrier((top, low, blocks))
    up3, down3, top, low = lax.optimization_barrier((up3, down3, top, low))
    up4 = shift(up3[:, : depth // 2], "z", 1)
    down4 = shift(down3[:, depth // 2 :], "z", -1)

    half = exchange(blocks, MP)

    x, yhi = lax.axis_index("x"), lax.axis_index("yhi")
    shard = (z + jnp.array([0, zs - 1, 1, zs - 2, 2, zs - 3, 3, zs - 4], jnp.int32)) & (zs - 1)
    slots = (2 * (((shard >> 1) - x) & (mp // 2 - 1)) + ((shard & 1) ^ yhi)).astype(jnp.int32)
    features = (both, right, top, low, left)
    early = [[(own,), (up1,)], [(down1,), (up2,)], [(down2,), (up3,)], [(down3,)]]
    acc = project(features, early, slots[:7])
    sent = project_last(features, (up4, down4), slots[7:], acc, 1 - core1, jnp.bfloat16)
    kept = project_last(features, (up4, down4), slots[7:], acc, core1, jnp.float32)
    attn = attention(kept, shift(sent, "core", 1), frames)
    attn, half = lax.optimization_barrier((attn, half))
    other_half = shift(half, "core", 1)
    attn = exchange(attn, FRAME).reshape(rows, heads)
    attn_both = jnp.stack([attn, shift(attn, "yhi", 1)])
    attn_left, attn_right = shift(attn_both, "x", 1), shift(attn_both, "x", -1)
    attn_top = shift(attn_left[:, :middle], "x", 1)
    attn_low = shift(attn_right[:, middle:], "x", -1)
    where = jnp.stack([core, x, yhi]).astype(jnp.int32)
    acc = near(where, attn_both, attn_right, attn_left, half, other_half)
    onehot = (action_idx.reshape(clips)[:, None] == jnp.arange(codebook.shape[0])[None, :]).astype(
        jnp.float32
    )
    codevec = jnp.dot(onehot, codebook, precision=lax.Precision.HIGHEST)
    gate = jnp.dot(codevec, act_proj, precision=lax.Precision.HIGHEST)
    peers = frames * lax.axis_size("dp")
    next_state, terms = finish(
        where, peers, attn_top, attn_low, half, other_half, acc, xin, gate,
        cotangent.reshape(rows, width), codevec,
    )
    terms = exchange(terms, FRAME + ("dp",))
    terms = terms.reshape(-1, terms.shape[-1])
    grad_proj = lax.dot_general(
        terms[:, width:],
        terms[:, :width],
        (((0,), (0,)), ((), ())),
        precision=lax.Precision.HIGHEST,
        preferred_element_type=jnp.float32,
    )
    return (next_state.reshape(tokens.shape), grad_proj)


def solution(mesh):
    split = Mesh(
        mesh.devices.reshape(mesh.shape["frame"] // 2, 2, mesh.shape["mp"] // 2, 2, mesh.shape["dp"]),
        ("z", "core", "x", "yhi", "dp"),
    )
    return jax.shard_map(
        body,
        mesh=split,
        in_specs=(
            P("dp", FRAME, None, MP),
            P("dp", FRAME, None),
            P(MP),
            P(FRAME, None, MP),
            P(MP, None),
            P("dp", FRAME),
            P(),
            P(None, MP),
            P("dp", FRAME, None, MP),
        ),
        out_specs=(P("dp", FRAME, None, MP), P(None, MP)),
        check_vma=False,
    )
```

```python
import math

import jax
import jax.numpy as jnp
from jax import lax
from jax.experimental import pallas as pl
from jax.experimental.pallas import tpu as pltpu
from jax.sharding import Mesh
from jax.sharding import PartitionSpec as P

HS = 128
MASKED = -1e30
QKV_VMEM = 58
SMEM = pl.BlockSpec(memory_space=pltpu.SMEM)
WHOLE = pl.BlockSpec(memory_space=pltpu.VMEM)
ANYWHERE = pl.BlockSpec(memory_space=pl.ANY)
FRAME = ("z", "core")
MP = ("x", "yhi")
SMALL = pltpu.CompilerParams(vmem_limit_bytes=12 << 20)


def exchange(x, axis):
    return lax.all_to_all(x, axis, split_axis=0, concat_axis=0, tiled=True)


def shift(x, axis, by):
    n = lax.axis_size(axis)
    return lax.ppermute(x, axis, [(i, (i + by) % n) for i in range(n)])


def fetch_features(slot, both, right, top, low, left, target, sem):
    far, own = slot >> 1, slot & 1
    for k, source in ((0, both), (1, right), (3, left)):

        @pl.when(far == k)
        def _():
            pltpu.make_async_copy(source.at[own], target, sem).start()

    @pl.when(far == 2)
    def _():
        half = target.shape[0] // 2
        pltpu.make_async_copy(top.at[own], target.at[pl.ds(0, half)], sem).start()
        pltpu.make_async_copy(low.at[own], target.at[pl.ds(half, half)], sem).start()


def qkv_kernel(groups, slots, both, right, top, low, left, *refs):
    pieces = [w for group in groups for w in group]
    count = sum(pieces)
    shards, refs = refs[:count], refs[count:]
    acc, spare, x_ref, w_ref, x_sem, w_sem = refs
    rows, full = x_ref.shape[1], x_ref.shape[2] // 2
    copies, at = [], 0
    for j, n in enumerate(pieces):
        fetch_features(slots[j], both, right, top, low, left, x_ref.at[j], x_sem.at[j])
        copies.append([])
        row = j * full
        for source in shards[at : at + n]:
            depth = source.shape[1]
            copy = pltpu.make_async_copy(source, w_ref.at[:, pl.ds(row, depth)], w_sem.at[at])
            copy.start()
            copies[j].append(copy)
            row += depth
            at += 1

    n = len(pieces)
    fetch_features(slots[n], both, right, top, low, left, spare, x_sem.at[n])
    j = 0
    for number, group in enumerate(groups):
        for i in range(j, j + len(group)):
            pltpu.make_async_copy(both.at[0], x_ref.at[i], x_sem.at[i]).wait()
            for copy in copies[i]:
                copy.wait()
        xs = [x_ref[j + i] for i in range(len(group))]
        x = jnp.concatenate(
            [
                jnp.concatenate([x[:, :full] for x in xs], axis=1),
                jnp.concatenate([x[:, full:] for x in xs], axis=1),
            ],
            axis=0,
        )
        span = pl.ds(j * full, len(group) * full)
        w = jnp.concatenate([w_ref[i, span] for i in range(3)], axis=1)
        part = jnp.dot(x, w, preferred_element_type=jnp.float32)
        if number:
            acc[...] += part
        else:
            acc[...] = part
        j += len(group)
    pltpu.make_async_copy(both.at[0], spare, x_sem.at[n]).wait()


def project(features, groups, slots):
    _, rows, width = features[0].shape
    counts = [[len(s) for s in group] for group in groups]
    shards = [w for group in groups for s in group for w in s]
    heads = shards[0].shape[-1]
    operands = [*features, *shards]
    n = sum(len(c) for c in counts)

    def kernel(*refs):
        qkv_kernel(counts, *refs)

    return pl.pallas_call(
        kernel,
        in_specs=[SMEM] + [ANYWHERE] * len(operands),
        out_specs=[WHOLE, WHOLE],
        out_shape=[
            jax.ShapeDtypeStruct((2 * rows, 3 * heads), jnp.float32),
            jax.ShapeDtypeStruct((rows, width), jnp.bfloat16),
        ],
        scratch_shapes=[
            pltpu.VMEM((n, rows, width), jnp.bfloat16),
            pltpu.VMEM((3, n * width // 2, heads), jnp.bfloat16),
            pltpu.SemaphoreType.DMA((n + 1,)),
            pltpu.SemaphoreType.DMA((len(shards),)),
        ],
        compiler_params=pltpu.CompilerParams(vmem_limit_bytes=QKV_VMEM << 20),
    )(slots, *operands)


def last_kernel(core, x_ref, first, second, acc, kept, sent):
    rows, full = x_ref.shape[0], x_ref.shape[1] // 2
    me = core[0]
    w = jnp.concatenate(
        [jnp.concatenate([first[i], second[i]], axis=0) for i in range(3)], axis=1
    )
    for side, out in ((me, kept), (1 - me, sent)):
        x = jnp.where(side == 0, x_ref[:, :full], x_ref[:, full:])
        part = jnp.dot(x, w, preferred_element_type=jnp.float32)
        out[...] = (acc[pl.ds(pl.multiple_of(side * rows, rows), rows)] + part).astype(out.dtype)


def project_last(core, x, first, second, acc):
    rows, total = x.shape[0], acc.shape[1]
    return pl.pallas_call(
        last_kernel,
        in_specs=[SMEM] + [WHOLE] * 4,
        out_specs=[WHOLE, WHOLE],
        out_shape=[
            jax.ShapeDtypeStruct((rows, total), jnp.float32),
            jax.ShapeDtypeStruct((rows, total), jnp.bfloat16),
        ],
        compiler_params=SMALL,
    )(core, x, first, second, acc)


def attend(q, k, v, bias):
    s = lax.dot_general(q, k, (((1,), (1,)), ((), ())), preferred_element_type=jnp.float32)
    s = s * (1.0 / math.sqrt(HS)) + bias
    peak = jnp.max(s, axis=1, keepdims=True)
    w = jnp.exp(s - peak)
    total = jnp.sum(w, axis=1, keepdims=True)
    high = w.astype(jnp.bfloat16)
    low = (w - high.astype(jnp.float32)).astype(jnp.bfloat16)
    accum = jnp.dot(high, v, preferred_element_type=jnp.float32)
    accum += jnp.dot(low, v, preferred_element_type=jnp.float32)
    return (accum / total).astype(jnp.bfloat16)


def attention_kernel(own_ref, other_ref, bias_ref, out_ref):
    frames, spots, width = out_ref.shape
    bias = bias_ref[...]
    for h in range(width // HS):
        q, k, v = (
            (own_ref[:, cols] + other_ref[:, cols].astype(jnp.float32)).astype(jnp.bfloat16)
            for cols in (slice(i * width + h * HS, i * width + (h + 1) * HS) for i in range(3))
        )
        o = attend(q, k, v, bias)
        for t in range(frames):
            out_ref[t, :, h * HS : (h + 1) * HS] = o[t * spots : (t + 1) * spots]


def attention(own, other, frames):
    rows, heads = own.shape[0], own.shape[1] // 3
    spots = rows // frames
    r = jnp.arange(rows)
    seen = (r[:, None] % spots == r[None, :] % spots) & (r[:, None] >= r[None, :])
    bias = jnp.where(seen, 0.0, MASKED).astype(jnp.float32)
    return pl.pallas_call(
        attention_kernel,
        out_shape=jax.ShapeDtypeStruct((frames, spots, heads), jnp.bfloat16),
        compiler_params=SMALL,
    )(own, other, bias)


def out_product(a, where, dx, half, other):
    n = half.shape[0] // 2
    block = 2 * ((where[1] + dx) & (n - 1))
    w = []
    for b in range(2):
        m = block + (b ^ where[2])
        mine, theirs = half[m], other[m]
        first = where[0] == 0
        w += [jnp.where(first, mine, theirs), jnp.where(first, theirs, mine)]
    x = jnp.concatenate(a, axis=1)
    return jnp.dot(x, jnp.concatenate(w, axis=0), preferred_element_type=jnp.float32)


def near_kernel(where, both, right, left, half, other, acc):
    acc[...] = out_product((both[0], both[1]), where, 0, half, other)
    acc[...] += out_product((right[0], right[1]), where, 1, half, other)
    acc[...] += out_product((left[0], left[1]), where, 3, half, other)


def far_kernel(where, top, low, half, other, acc, xin, gate, cot, codevec, next_ref, terms):
    far = tuple(jnp.concatenate([top[b], low[b]], axis=0) for b in range(2))
    mixed = acc[...] + out_product(far, where, 2, half, other)
    rows, width = mixed.shape
    clips = gate.shape[0]
    spots = rows // clips
    sums = []
    for c in range(clips):
        at = slice(c * spots, (c + 1) * spots)
        m = mixed[at]
        moved = xin[at].astype(jnp.float32) + gate[c : c + 1] * m
        next_ref[at] = moved.astype(jnp.bfloat16)
        sums.append(jnp.sum(cot[at].astype(jnp.float32) * m, axis=0, keepdims=True))
    dgate = jnp.concatenate(sums, axis=0)
    for i in range(terms.shape[0]):
        terms[i, :, :width] = dgate
        terms[i, :, width:] = codevec[...]


def near(where, *operands):
    rows, width = operands[0].shape[1], operands[3].shape[2]
    smem, vmem = pl.BlockSpec(memory_space=pltpu.SMEM), pl.BlockSpec(memory_space=pltpu.VMEM)
    return pl.pallas_call(
        near_kernel,
        in_specs=[smem] + [vmem] * 5,
        out_specs=vmem,
        out_shape=jax.ShapeDtypeStruct((rows, width), jnp.float32),
        compiler_params=SMALL,
    )(where, *operands)


def finish(where, peers, *operands):
    rows, width = operands[4].shape
    clips = operands[6].shape[0]
    smem, vmem = pl.BlockSpec(memory_space=pltpu.SMEM), pl.BlockSpec(memory_space=pltpu.VMEM)
    return pl.pallas_call(
        far_kernel,
        in_specs=[smem] + [vmem] * 9,
        out_specs=[vmem, vmem],
        out_shape=[
            jax.ShapeDtypeStruct((rows, width), jnp.bfloat16),
            jax.ShapeDtypeStruct((peers, clips, width + operands[8].shape[1]), jnp.float32),
        ],
        compiler_params=SMALL,
    )(where, *operands)


def blocks_kernel(core, w_ref, out_ref, sem):
    n, half, width = out_ref.shape
    rows = pl.ds(pl.multiple_of(core[0] * half, half), half)
    copies = [
        pltpu.make_async_copy(w_ref.at[rows, pl.ds(m * width, width)], out_ref.at[m], sem.at[m])
        for m in range(n)
    ]
    for copy in copies:
        copy.start()
    for copy in copies:
        copy.wait()


def column_blocks(w, core, width):
    heads, full = w.shape
    half, n = heads // 2, full // width
    hbm = pl.BlockSpec(memory_space=pltpu.HBM)
    return pl.pallas_call(
        blocks_kernel,
        in_specs=[pl.BlockSpec(memory_space=pltpu.SMEM), hbm],
        out_specs=hbm,
        out_shape=jax.ShapeDtypeStruct((n, half, width), w.dtype),
        scratch_shapes=[pltpu.SemaphoreType.DMA((n,))],
        compiler_params=SMALL,
    )(core, w)


def body(tokens, token_mask, mask_embed, w_qkv, w_out, action_idx, codebook, act_proj, cotangent):
    clips, _, spots, width = tokens.shape
    rows = clips * spots
    zs, cores = lax.axis_size("z"), lax.axis_size("core")
    frames, mp = zs * cores, lax.axis_size(MP)
    depth, heads = w_qkv.shape[0], w_qkv.shape[2]
    z, core = lax.axis_index("z"), lax.axis_index("core")
    core1 = core.reshape(1).astype(jnp.int32)
    xin = jnp.where(token_mask[..., None] == 1, mask_embed, tokens).reshape(rows, width)
    mine = xin.reshape(zs, 2, rows // frames, cores, depth).transpose(0, 3, 2, 1, 4)
    mine = exchange(mine.reshape(frames, rows // frames, 2 * depth), FRAME).reshape(rows, 2 * depth)

    own = w_qkv.transpose(1, 0, 2)
    up1, down1 = shift(own, "z", 1), shift(own, "z", -1)
    both = jnp.stack([mine, shift(mine, "yhi", 1)])
    both, w_out, up1, down1 = lax.optimization_barrier((both, w_out, up1, down1))
    left, right = shift(both, "x", 1), shift(both, "x", -1)
    up2, down2 = shift(up1, "z", 1), shift(down1, "z", -1)
    blocks = column_blocks(w_out, core1, width)
    left, right, up2, down2, blocks = lax.optimization_barrier((left, right, up2, down2, blocks))
    middle = rows // 2
    top, low = shift(left[:, :middle], "x", 1), shift(right[:, middle:], "x", -1)
    up3, down3 = shift(up2, "z", 1), shift(down2, "z", -1)
    top, low, blocks = lax.optimization_barrier((top, low, blocks))
    up3, down3, top, low = lax.optimization_barrier((up3, down3, top, low))
    up4 = shift(up3[:, : depth // 2], "z", 1)
    down4 = shift(down3[:, depth // 2 :], "z", -1)

    half = exchange(blocks, MP)

    x, yhi = lax.axis_index("x"), lax.axis_index("yhi")
    shard = (z + jnp.array([0, zs - 1, 1, zs - 2, 2, zs - 3, 3, zs - 4], jnp.int32)) & (zs - 1)
    slots = (2 * (((shard >> 1) - x) & (mp // 2 - 1)) + ((shard & 1) ^ yhi)).astype(jnp.int32)
    features = (both, right, top, low, left)
    early = [[(own,), (up1,)], [(down1,), (up2,)], [(down2,), (up3,)], [(down3,)]]
    acc, spare = project(features, early, slots)
    kept, sent = project_last(core1, spare, up4, down4, acc)
    attn = attention(kept, shift(sent, "core", 1), frames)
    attn, half = lax.optimization_barrier((attn, half))
    other_half = shift(half, "core", 1)
    attn = exchange(attn, FRAME).reshape(rows, heads)
    attn_both = jnp.stack([attn, shift(attn, "yhi", 1)])
    attn_left, attn_right = shift(attn_both, "x", 1), shift(attn_both, "x", -1)
    attn_top = shift(attn_left[:, :middle], "x", 1)
    attn_low = shift(attn_right[:, middle:], "x", -1)
    where = jnp.stack([core, x, yhi]).astype(jnp.int32)
    acc = near(where, attn_both, attn_right, attn_left, half, other_half)
    onehot = (action_idx.reshape(clips)[:, None] == jnp.arange(codebook.shape[0])[None, :]).astype(
        jnp.float32
    )
    codevec = jnp.dot(onehot, codebook, precision=lax.Precision.HIGHEST)
    gate = jnp.dot(codevec, act_proj, precision=lax.Precision.HIGHEST)
    peers = frames * lax.axis_size("dp")
    next_state, terms = finish(
        where, peers, attn_top, attn_low, half, other_half, acc, xin, gate,
        cotangent.reshape(rows, width), codevec,
    )
    terms = exchange(terms, FRAME + ("dp",))
    terms = terms.reshape(-1, terms.shape[-1])
    grad_proj = lax.dot_general(
        terms[:, width:],
        terms[:, :width],
        (((0,), (0,)), ((), ())),
        precision=lax.Precision.HIGHEST,
        preferred_element_type=jnp.float32,
    )
    return (next_state.reshape(tokens.shape), grad_proj)


def solution(mesh):
    split = Mesh(
        mesh.devices.reshape(mesh.shape["frame"] // 2, 2, mesh.shape["mp"] // 2, 2, mesh.shape["dp"]),
        ("z", "core", "x", "yhi", "dp"),
    )
    return jax.shard_map(
        body,
        mesh=split,
        in_specs=(
            P("dp", FRAME, None, MP),
            P("dp", FRAME, None),
            P(MP),
            P(FRAME, None, MP),
            P(MP, None),
            P("dp", FRAME),
            P(),
            P(None, MP),
            P("dp", FRAME, None, MP),
        ),
        out_specs=(P("dp", FRAME, None, MP), P(None, MP)),
        check_vma=False,
    )
```

```python
import math

import jax
import jax.numpy as jnp
from jax import lax
from jax.experimental import pallas as pl
from jax.experimental.pallas import tpu as pltpu
from jax.sharding import Mesh
from jax.sharding import PartitionSpec as P

HS = 128
MASKED = -1e30
QKV_VMEM = 58
SMEM = pl.BlockSpec(memory_space=pltpu.SMEM)
WHOLE = pl.BlockSpec(memory_space=pltpu.VMEM)
ANYWHERE = pl.BlockSpec(memory_space=pl.ANY)
FRAME = ("z", "core")
MP = ("x", "yhi")
SMALL = pltpu.CompilerParams(vmem_limit_bytes=12 << 20)


def exchange(x, axis):
    return lax.all_to_all(x, axis, split_axis=0, concat_axis=0, tiled=True)


def shift(x, axis, by):
    n = lax.axis_size(axis)
    return lax.ppermute(x, axis, [(i, (i + by) % n) for i in range(n)])


def fetch_features(slot, pieces, target, sem):
    half = target.shape[0] // 2
    for own in range(2):
        here, right, left, top, low = pieces[5 * own : 5 * own + 5]
        for k, source in ((0, here), (1, right), (3, left)):

            @pl.when(slot == 2 * k + own)
            def _():
                pltpu.make_async_copy(source, target, sem).start()

        @pl.when(slot == 4 + own)
        def _():
            pltpu.make_async_copy(top, target.at[pl.ds(0, half)], sem).start()
            pltpu.make_async_copy(low, target.at[pl.ds(half, half)], sem).start()


def qkv_kernel(groups, slots, *refs):
    features, refs = refs[:10], refs[10:]
    pieces = [w for group in groups for w in group]
    count = sum(pieces)
    shards, refs = refs[:count], refs[count:]
    acc, spare, x_ref, w_ref, x_sem, w_sem = refs
    rows, full = x_ref.shape[1], x_ref.shape[2] // 2
    copies, at = [], 0
    for j, n in enumerate(pieces):
        fetch_features(slots[j], features, x_ref.at[j], x_sem.at[j])
        copies.append([])
        row = j * full
        for source in shards[at : at + n]:
            depth = source.shape[1]
            copy = pltpu.make_async_copy(source, w_ref.at[:, pl.ds(row, depth)], w_sem.at[at])
            copy.start()
            copies[j].append(copy)
            row += depth
            at += 1

    n = len(pieces)
    fetch_features(slots[n], features, spare, x_sem.at[n])
    j = 0
    for number, group in enumerate(groups):
        for i in range(j, j + len(group)):
            pltpu.make_async_copy(features[0], x_ref.at[i], x_sem.at[i]).wait()
            for copy in copies[i]:
                copy.wait()
        xs = [x_ref[j + i] for i in range(len(group))]
        x = jnp.concatenate(
            [
                jnp.concatenate([x[:, :full] for x in xs], axis=1),
                jnp.concatenate([x[:, full:] for x in xs], axis=1),
            ],
            axis=0,
        )
        span = pl.ds(j * full, len(group) * full)
        w = jnp.concatenate([w_ref[i, span] for i in range(3)], axis=1)
        part = jnp.dot(x, w, preferred_element_type=jnp.float32)
        if number:
            acc[...] += part
        else:
            acc[...] = part
        j += len(group)
    pltpu.make_async_copy(features[0], spare, x_sem.at[n]).wait()


def project(features, groups, slots):
    rows, width = features[0].shape
    counts = [[len(s) for s in group] for group in groups]
    shards = [w for group in groups for s in group for w in s]
    heads = shards[0].shape[-1]
    operands = [*features, *shards]
    n = sum(len(c) for c in counts)

    def kernel(*refs):
        qkv_kernel(counts, *refs)

    return pl.pallas_call(
        kernel,
        in_specs=[SMEM] + [ANYWHERE] * len(operands),
        out_specs=[WHOLE, WHOLE],
        out_shape=[
            jax.ShapeDtypeStruct((2 * rows, 3 * heads), jnp.float32),
            jax.ShapeDtypeStruct((rows, width), jnp.bfloat16),
        ],
        scratch_shapes=[
            pltpu.VMEM((n, rows, width), jnp.bfloat16),
            pltpu.VMEM((3, n * width // 2, heads), jnp.bfloat16),
            pltpu.SemaphoreType.DMA((n + 1,)),
            pltpu.SemaphoreType.DMA((len(shards),)),
        ],
        compiler_params=pltpu.CompilerParams(vmem_limit_bytes=QKV_VMEM << 20),
    )(slots, *operands)


def last_kernel(core, x_ref, first, second, acc, kept, sent):
    rows, full = x_ref.shape[0], x_ref.shape[1] // 2
    me = core[0]
    w = jnp.concatenate(
        [jnp.concatenate([first[i], second[i]], axis=0) for i in range(3)], axis=1
    )
    for side, out in ((me, kept), (1 - me, sent)):
        x = jnp.where(side == 0, x_ref[:, :full], x_ref[:, full:])
        part = jnp.dot(x, w, preferred_element_type=jnp.float32)
        out[...] = (acc[pl.ds(pl.multiple_of(side * rows, rows), rows)] + part).astype(out.dtype)


def project_last(core, x, first, second, acc):
    rows, total = x.shape[0], acc.shape[1]
    return pl.pallas_call(
        last_kernel,
        in_specs=[SMEM] + [WHOLE] * 4,
        out_specs=[WHOLE, WHOLE],
        out_shape=[
            jax.ShapeDtypeStruct((rows, total), jnp.float32),
            jax.ShapeDtypeStruct((rows, total), jnp.bfloat16),
        ],
        compiler_params=SMALL,
    )(core, x, first, second, acc)


def attend(q, k, v, bias):
    s = lax.dot_general(q, k, (((1,), (1,)), ((), ())), preferred_element_type=jnp.float32)
    s = s * (1.0 / math.sqrt(HS)) + bias
    peak = jnp.max(s, axis=1, keepdims=True)
    w = jnp.exp(s - peak)
    total = jnp.sum(w, axis=1, keepdims=True)
    high = w.astype(jnp.bfloat16)
    low = (w - high.astype(jnp.float32)).astype(jnp.bfloat16)
    accum = jnp.dot(high, v, preferred_element_type=jnp.float32)
    accum += jnp.dot(low, v, preferred_element_type=jnp.float32)
    return (accum / total).astype(jnp.bfloat16)


def attention_kernel(own_ref, other_ref, bias_ref, out_ref):
    frames, spots, width = out_ref.shape
    bias = bias_ref[...]
    for h in range(width // HS):
        q, k, v = (
            (own_ref[:, cols] + other_ref[:, cols].astype(jnp.float32)).astype(jnp.bfloat16)
            for cols in (slice(i * width + h * HS, i * width + (h + 1) * HS) for i in range(3))
        )
        o = attend(q, k, v, bias)
        for t in range(frames):
            out_ref[t, :, h * HS : (h + 1) * HS] = o[t * spots : (t + 1) * spots]


def attention(own, other, frames):
    rows, heads = own.shape[0], own.shape[1] // 3
    spots = rows // frames
    r = jnp.arange(rows)
    seen = (r[:, None] % spots == r[None, :] % spots) & (r[:, None] >= r[None, :])
    bias = jnp.where(seen, 0.0, MASKED).astype(jnp.float32)
    return pl.pallas_call(
        attention_kernel,
        out_shape=jax.ShapeDtypeStruct((frames, spots, heads), jnp.bfloat16),
        compiler_params=SMALL,
    )(own, other, bias)


def out_product(a, where, dx, half, other):
    n = half.shape[0] // 2
    block = 2 * ((where[1] + dx) & (n - 1))
    w = []
    for b in range(2):
        m = block + (b ^ where[2])
        mine, theirs = half[m], other[m]
        first = where[0] == 0
        w += [jnp.where(first, mine, theirs), jnp.where(first, theirs, mine)]
    x = jnp.concatenate(a, axis=1)
    return jnp.dot(x, jnp.concatenate(w, axis=0), preferred_element_type=jnp.float32)


def near_kernel(where, m0, m1, r0, r1, l0, l1, half, other, acc):
    acc[...] = out_product((m0[...], m1[...]), where, 0, half, other)
    acc[...] += out_product((r0[...], r1[...]), where, 1, half, other)
    acc[...] += out_product((l0[...], l1[...]), where, 3, half, other)


def far_kernel(
    where, t0, w0, t1, w1, half, other, acc, xin, gate, cot, codevec, next_ref, terms
):
    far = tuple(jnp.concatenate([t[...], w[...]], axis=0) for t, w in ((t0, w0), (t1, w1)))
    mixed = acc[...] + out_product(far, where, 2, half, other)
    rows, width = mixed.shape
    clips = gate.shape[0]
    spots = rows // clips
    sums = []
    for c in range(clips):
        at = slice(c * spots, (c + 1) * spots)
        m = mixed[at]
        moved = xin[at].astype(jnp.float32) + gate[c : c + 1] * m
        next_ref[at] = moved.astype(jnp.bfloat16)
        sums.append(jnp.sum(cot[at].astype(jnp.float32) * m, axis=0, keepdims=True))
    dgate = jnp.concatenate(sums, axis=0)
    for i in range(terms.shape[0]):
        terms[i, :, :width] = dgate
        terms[i, :, width:] = codevec[...]


def near(where, *operands):
    rows, width = operands[0].shape[0], operands[6].shape[2]
    smem, vmem = pl.BlockSpec(memory_space=pltpu.SMEM), pl.BlockSpec(memory_space=pltpu.VMEM)
    return pl.pallas_call(
        near_kernel,
        in_specs=[smem] + [vmem] * 8,
        out_specs=vmem,
        out_shape=jax.ShapeDtypeStruct((rows, width), jnp.float32),
        compiler_params=SMALL,
    )(where, *operands)


def finish(where, peers, *operands):
    rows, width = operands[6].shape
    clips = operands[8].shape[0]
    smem, vmem = pl.BlockSpec(memory_space=pltpu.SMEM), pl.BlockSpec(memory_space=pltpu.VMEM)
    return pl.pallas_call(
        far_kernel,
        in_specs=[smem] + [vmem] * 11,
        out_specs=[vmem, vmem],
        out_shape=[
            jax.ShapeDtypeStruct((rows, width), jnp.bfloat16),
            jax.ShapeDtypeStruct((peers, clips, width + operands[10].shape[1]), jnp.float32),
        ],
        compiler_params=SMALL,
    )(where, *operands)


def blocks_kernel(core, w_ref, out_ref, sem):
    n, half, width = out_ref.shape
    rows = pl.ds(pl.multiple_of(core[0] * half, half), half)
    copies = [
        pltpu.make_async_copy(w_ref.at[rows, pl.ds(m * width, width)], out_ref.at[m], sem.at[m])
        for m in range(n)
    ]
    for copy in copies:
        copy.start()
    for copy in copies:
        copy.wait()


def column_blocks(w, core, width):
    heads, full = w.shape
    half, n = heads // 2, full // width
    hbm = pl.BlockSpec(memory_space=pltpu.HBM)
    return pl.pallas_call(
        blocks_kernel,
        in_specs=[pl.BlockSpec(memory_space=pltpu.SMEM), hbm],
        out_specs=hbm,
        out_shape=jax.ShapeDtypeStruct((n, half, width), w.dtype),
        scratch_shapes=[pltpu.SemaphoreType.DMA((n,))],
        compiler_params=SMALL,
    )(core, w)


def body(tokens, token_mask, mask_embed, w_qkv, w_out, action_idx, codebook, act_proj, cotangent):
    clips, _, spots, width = tokens.shape
    rows = clips * spots
    zs, cores = lax.axis_size("z"), lax.axis_size("core")
    frames, mp = zs * cores, lax.axis_size(MP)
    depth, heads = w_qkv.shape[0], w_qkv.shape[2]
    z, core = lax.axis_index("z"), lax.axis_index("core")
    core1 = core.reshape(1).astype(jnp.int32)
    xin = jnp.where(token_mask[..., None] == 1, mask_embed, tokens).reshape(rows, width)
    mine = xin.reshape(zs, 2, rows // frames, cores, depth).transpose(0, 3, 2, 1, 4)
    mine = exchange(mine.reshape(frames, rows // frames, 2 * depth), FRAME).reshape(rows, 2 * depth)

    own = w_qkv.transpose(1, 0, 2)
    up1, down1 = shift(own, "z", 1), shift(own, "z", -1)
    middle = rows // 2

    def sideways(block):
        return shift(block, "x", -1), shift(block, "x", 1)

    def onward(right, left):
        return shift(left[:middle], "x", 1), shift(right[middle:], "x", -1)

    other = shift(mine, "yhi", 1)
    side = sideways(mine)
    other, side, up1, down1 = lax.optimization_barrier((other, side, up1, down1))
    up2, down2 = shift(up1, "z", 1), shift(down1, "z", -1)
    other_side, far = sideways(other), onward(*side)
    other_side, far, up2, down2, w_out = lax.optimization_barrier(
        (other_side, far, up2, down2, w_out)
    )
    up3, down3 = shift(up2, "z", 1), shift(down2, "z", -1)
    other_far = onward(*other_side)
    blocks = column_blocks(w_out, core1, width)
    other_far, blocks = lax.optimization_barrier((other_far, blocks))
    up3, down3, other_far = lax.optimization_barrier((up3, down3, other_far))
    up4 = shift(up3[:, : depth // 2], "z", 1)
    down4 = shift(down3[:, depth // 2 :], "z", -1)

    half = exchange(blocks, MP)

    x, yhi = lax.axis_index("x"), lax.axis_index("yhi")
    shard = (z + jnp.array([0, zs - 1, 1, zs - 2, 2, zs - 3, 3, zs - 4], jnp.int32)) & (zs - 1)
    slots = (2 * (((shard >> 1) - x) & (mp // 2 - 1)) + ((shard & 1) ^ yhi)).astype(jnp.int32)
    features = (mine, *side, *far, other, *other_side, *other_far)
    early = [[(own,), (up1,)], [(down1,), (up2,)], [(down2,), (up3,)], [(down3,)]]
    acc, spare = project(features, early, slots)
    kept, sent = project_last(core1, spare, up4, down4, acc)
    attn = attention(kept, shift(sent, "core", 1), frames)
    attn, half = lax.optimization_barrier((attn, half))
    other_half = shift(half, "core", 1)
    attn = exchange(attn, FRAME).reshape(rows, heads)
    peer = shift(attn, "yhi", 1)
    side = sideways(attn)
    peer, side = lax.optimization_barrier((peer, side))
    peer_side, far = sideways(peer), onward(*side)
    peer_far = onward(*peer_side)
    where = jnp.stack([core, x, yhi]).astype(jnp.int32)
    acc = near(
        where, attn, peer, side[0], peer_side[0], side[1], peer_side[1], half, other_half
    )
    onehot = (action_idx.reshape(clips)[:, None] == jnp.arange(codebook.shape[0])[None, :]).astype(
        jnp.float32
    )
    codevec = jnp.dot(onehot, codebook, precision=lax.Precision.HIGHEST)
    gate = jnp.dot(codevec, act_proj, precision=lax.Precision.HIGHEST)
    peers = frames * lax.axis_size("dp")
    next_state, terms = finish(
        where, peers, *far, *peer_far, half, other_half, acc, xin, gate,
        cotangent.reshape(rows, width), codevec,
    )
    terms = exchange(terms, FRAME + ("dp",))
    terms = terms.reshape(-1, terms.shape[-1])
    grad_proj = lax.dot_general(
        terms[:, width:],
        terms[:, :width],
        (((0,), (0,)), ((), ())),
        precision=lax.Precision.HIGHEST,
        preferred_element_type=jnp.float32,
    )
    return (next_state.reshape(tokens.shape), grad_proj)


def solution(mesh):
    split = Mesh(
        mesh.devices.reshape(mesh.shape["frame"] // 2, 2, mesh.shape["mp"] // 2, 2, mesh.shape["dp"]),
        ("z", "core", "x", "yhi", "dp"),
    )
    return jax.shard_map(
        body,
        mesh=split,
        in_specs=(
            P("dp", FRAME, None, MP),
            P("dp", FRAME, None),
            P(MP),
            P(FRAME, None, MP),
            P(MP, None),
            P("dp", FRAME),
            P(),
            P(None, MP),
            P("dp", FRAME, None, MP),
        ),
        out_specs=(P("dp", FRAME, None, MP), P(None, MP)),
        check_vma=False,
    )
```

```python
import math

import jax
import jax.numpy as jnp
from jax import lax
from jax.experimental import pallas as pl
from jax.experimental.pallas import tpu as pltpu
from jax.sharding import Mesh
from jax.sharding import PartitionSpec as P

HS = 128
MASKED = -1e30
QKV_VMEM = 58
SMEM = pl.BlockSpec(memory_space=pltpu.SMEM)
WHOLE = pl.BlockSpec(memory_space=pltpu.VMEM)
ANYWHERE = pl.BlockSpec(memory_space=pl.ANY)
FRAME = ("z", "core")
MP = ("x", "yhi")
SMALL = pltpu.CompilerParams(vmem_limit_bytes=12 << 20)


def exchange(x, axis):
    return lax.all_to_all(x, axis, split_axis=0, concat_axis=0, tiled=True)


def shift(x, axis, by):
    n = lax.axis_size(axis)
    return lax.ppermute(x, axis, [(i, (i + by) % n) for i in range(n)])


def fetch_features(slot, pieces, target, sem):
    half = target.shape[0] // 2
    for own in range(2):
        here, right, left, top, low = pieces[5 * own : 5 * own + 5]
        for k, source in ((0, here), (1, right), (3, left)):

            @pl.when(slot == 2 * k + own)
            def _():
                pltpu.make_async_copy(source, target, sem).start()

        @pl.when(slot == 4 + own)
        def _():
            pltpu.make_async_copy(top, target.at[pl.ds(0, half)], sem).start()
            pltpu.make_async_copy(low, target.at[pl.ds(half, half)], sem).start()


def qkv_kernel(groups, slots, *refs):
    features, refs = refs[:10], refs[10:]
    pieces = [w for group in groups for w in group]
    count = sum(pieces)
    shards, refs = refs[:count], refs[count:]
    acc, spare, x_ref, w_ref, x_sem, w_sem = refs
    rows, full = x_ref.shape[1], x_ref.shape[2] // 2
    copies, at = [], 0
    for j, n in enumerate(pieces):
        fetch_features(slots[j], features, x_ref.at[j], x_sem.at[j])
        copies.append([])
        row = j * full
        for source in shards[at : at + n]:
            depth = source.shape[1]
            copy = pltpu.make_async_copy(source, w_ref.at[:, pl.ds(row, depth)], w_sem.at[at])
            copy.start()
            copies[j].append(copy)
            row += depth
            at += 1

    n = len(pieces)
    fetch_features(slots[n], features, spare, x_sem.at[n])
    j = 0
    for number, group in enumerate(groups):
        for i in range(j, j + len(group)):
            pltpu.make_async_copy(features[0], x_ref.at[i], x_sem.at[i]).wait()
            for copy in copies[i]:
                copy.wait()
        xs = [x_ref[j + i] for i in range(len(group))]
        x = jnp.concatenate(
            [
                jnp.concatenate([x[:, :full] for x in xs], axis=1),
                jnp.concatenate([x[:, full:] for x in xs], axis=1),
            ],
            axis=0,
        )
        span = pl.ds(j * full, len(group) * full)
        w = jnp.concatenate([w_ref[i, span] for i in range(3)], axis=1)
        part = jnp.dot(x, w, preferred_element_type=jnp.float32)
        if number:
            acc[...] += part
        else:
            acc[...] = part
        j += len(group)
    pltpu.make_async_copy(features[0], spare, x_sem.at[n]).wait()


def project(features, groups, slots):
    rows, width = features[0].shape
    counts = [[len(s) for s in group] for group in groups]
    shards = [w for group in groups for s in group for w in s]
    heads = shards[0].shape[-1]
    operands = [*features, *shards]
    n = sum(len(c) for c in counts)

    def kernel(*refs):
        qkv_kernel(counts, *refs)

    return pl.pallas_call(
        kernel,
        in_specs=[SMEM] + [ANYWHERE] * len(operands),
        out_specs=[WHOLE, WHOLE],
        out_shape=[
            jax.ShapeDtypeStruct((2 * rows, 3 * heads), jnp.float32),
            jax.ShapeDtypeStruct((rows, width), jnp.bfloat16),
        ],
        scratch_shapes=[
            pltpu.VMEM((n, rows, width), jnp.bfloat16),
            pltpu.VMEM((3, n * width // 2, heads), jnp.bfloat16),
            pltpu.SemaphoreType.DMA((n + 1,)),
            pltpu.SemaphoreType.DMA((len(shards),)),
        ],
        compiler_params=pltpu.CompilerParams(vmem_limit_bytes=QKV_VMEM << 20),
    )(slots, *operands)


def last_kernel(core, x_ref, first, second, acc, kept, sent):
    rows, full = x_ref.shape[0], x_ref.shape[1] // 2
    me = core[0]
    w = jnp.concatenate(
        [jnp.concatenate([first[i], second[i]], axis=0) for i in range(3)], axis=1
    )
    for side, out in ((me, kept), (1 - me, sent)):
        x = jnp.where(side == 0, x_ref[:, :full], x_ref[:, full:])
        part = jnp.dot(x, w, preferred_element_type=jnp.float32)
        out[...] = (acc[pl.ds(pl.multiple_of(side * rows, rows), rows)] + part).astype(out.dtype)


def project_last(core, x, first, second, acc):
    rows, total = x.shape[0], acc.shape[1]
    return pl.pallas_call(
        last_kernel,
        in_specs=[SMEM] + [WHOLE] * 4,
        out_specs=[WHOLE, WHOLE],
        out_shape=[
            jax.ShapeDtypeStruct((rows, total), jnp.float32),
            jax.ShapeDtypeStruct((rows, total), jnp.bfloat16),
        ],
        compiler_params=SMALL,
    )(core, x, first, second, acc)


def attend(q, k, v, bias):
    s = lax.dot_general(q, k, (((1,), (1,)), ((), ())), preferred_element_type=jnp.float32)
    s = s * (1.0 / math.sqrt(HS)) + bias
    peak = jnp.max(s, axis=1, keepdims=True)
    w = jnp.exp(s - peak)
    total = jnp.sum(w, axis=1, keepdims=True)
    high = w.astype(jnp.bfloat16)
    low = (w - high.astype(jnp.float32)).astype(jnp.bfloat16)
    accum = jnp.dot(high, v, preferred_element_type=jnp.float32)
    accum += jnp.dot(low, v, preferred_element_type=jnp.float32)
    return (accum / total).astype(jnp.bfloat16)


def attention_kernel(own_ref, other_ref, bias_ref, out_ref):
    frames, spots, width = out_ref.shape
    bias = bias_ref[...]
    for h in range(width // HS):
        q, k, v = (
            (own_ref[:, cols] + other_ref[:, cols].astype(jnp.float32)).astype(jnp.bfloat16)
            for cols in (slice(i * width + h * HS, i * width + (h + 1) * HS) for i in range(3))
        )
        o = attend(q, k, v, bias)
        for t in range(frames):
            out_ref[t, :, h * HS : (h + 1) * HS] = o[t * spots : (t + 1) * spots]


def attention(own, other, frames):
    rows, heads = own.shape[0], own.shape[1] // 3
    spots = rows // frames
    r = jnp.arange(rows)
    seen = (r[:, None] % spots == r[None, :] % spots) & (r[:, None] >= r[None, :])
    bias = jnp.where(seen, 0.0, MASKED).astype(jnp.float32)
    return pl.pallas_call(
        attention_kernel,
        out_shape=jax.ShapeDtypeStruct((frames, spots, heads), jnp.bfloat16),
        compiler_params=SMALL,
    )(own, other, bias)


def out_product(a, where, dx, half, other):
    n = half.shape[0] // 2
    block = 2 * ((where[1] + dx) & (n - 1))
    w = []
    for b in range(2):
        m = block + (b ^ where[2])
        mine, theirs = half[m], other[m]
        first = where[0] == 0
        w += [jnp.where(first, mine, theirs), jnp.where(first, theirs, mine)]
    x = jnp.concatenate(a, axis=1)
    return jnp.dot(x, jnp.concatenate(w, axis=0), preferred_element_type=jnp.float32)


def near_kernel(where, m0, m1, r0, r1, l0, l1, half, other, acc):
    acc[...] = out_product((m0[...], m1[...]), where, 0, half, other)
    acc[...] += out_product((r0[...], r1[...]), where, 1, half, other)
    acc[...] += out_product((l0[...], l1[...]), where, 3, half, other)


def far_kernel(
    where, t0, w0, t1, w1, half, other, acc, xin, gate, cot, codevec, next_ref, terms
):
    far = tuple(jnp.concatenate([t[...], w[...]], axis=0) for t, w in ((t0, w0), (t1, w1)))
    mixed = acc[...] + out_product(far, where, 2, half, other)
    rows, width = mixed.shape
    clips = gate.shape[0]
    spots = rows // clips
    sums = []
    for c in range(clips):
        at = slice(c * spots, (c + 1) * spots)
        m = mixed[at]
        moved = xin[at].astype(jnp.float32) + gate[c : c + 1] * m
        next_ref[at] = moved.astype(jnp.bfloat16)
        sums.append(jnp.sum(cot[at].astype(jnp.float32) * m, axis=0, keepdims=True))
    dgate = jnp.concatenate(sums, axis=0)
    for i in range(terms.shape[0]):
        terms[i, :, :width] = dgate
        terms[i, :, width:] = codevec[...]


def near(where, *operands):
    rows, width = operands[0].shape[0], operands[6].shape[2]
    smem, vmem = pl.BlockSpec(memory_space=pltpu.SMEM), pl.BlockSpec(memory_space=pltpu.VMEM)
    return pl.pallas_call(
        near_kernel,
        in_specs=[smem] + [vmem] * 8,
        out_specs=vmem,
        out_shape=jax.ShapeDtypeStruct((rows, width), jnp.float32),
        compiler_params=SMALL,
    )(where, *operands)


def finish(where, peers, *operands):
    rows, width = operands[6].shape
    clips = operands[8].shape[0]
    smem, vmem = pl.BlockSpec(memory_space=pltpu.SMEM), pl.BlockSpec(memory_space=pltpu.VMEM)
    return pl.pallas_call(
        far_kernel,
        in_specs=[smem] + [vmem] * 11,
        out_specs=[vmem, vmem],
        out_shape=[
            jax.ShapeDtypeStruct((rows, width), jnp.bfloat16),
            jax.ShapeDtypeStruct((peers, clips, width + operands[10].shape[1]), jnp.float32),
        ],
        compiler_params=SMALL,
    )(where, *operands)


def blocks_kernel(core, w_ref, out_ref, sem):
    n, half, width = out_ref.shape
    rows = pl.ds(pl.multiple_of(core[0] * half, half), half)
    copies = [
        pltpu.make_async_copy(w_ref.at[rows, pl.ds(m * width, width)], out_ref.at[m], sem.at[m])
        for m in range(n)
    ]
    for copy in copies:
        copy.start()
    for copy in copies:
        copy.wait()


def column_blocks(w, core, width):
    heads, full = w.shape
    half, n = heads // 2, full // width
    hbm = pl.BlockSpec(memory_space=pltpu.HBM)
    return pl.pallas_call(
        blocks_kernel,
        in_specs=[pl.BlockSpec(memory_space=pltpu.SMEM), hbm],
        out_specs=hbm,
        out_shape=jax.ShapeDtypeStruct((n, half, width), w.dtype),
        scratch_shapes=[pltpu.SemaphoreType.DMA((n,))],
        compiler_params=SMALL,
    )(core, w)


def body(tokens, token_mask, mask_embed, w_qkv, w_out, action_idx, codebook, act_proj, cotangent):
    clips, _, spots, width = tokens.shape
    rows = clips * spots
    zs, cores = lax.axis_size("z"), lax.axis_size("core")
    frames, mp = zs * cores, lax.axis_size(MP)
    depth, heads = w_qkv.shape[0], w_qkv.shape[2]
    z, core = lax.axis_index("z"), lax.axis_index("core")
    core1 = core.reshape(1).astype(jnp.int32)
    xin = jnp.where(token_mask[..., None] == 1, mask_embed, tokens).reshape(rows, width)
    mine = xin.reshape(zs, 2, rows // frames, cores, depth).transpose(0, 3, 2, 1, 4)
    mine = exchange(mine.reshape(frames, rows // frames, 2 * depth), FRAME).reshape(rows, 2 * depth)

    own = w_qkv.transpose(1, 0, 2)
    up1, down1 = shift(own, "z", 1), shift(own, "z", -1)
    middle = rows // 2

    def sideways(block):
        return shift(block, "x", -1), shift(block, "x", 1)

    def onward(right, left):
        return shift(left[:middle], "x", 1), shift(right[middle:], "x", -1)

    other = shift(mine, "yhi", 1)
    side = sideways(mine)
    other, side = lax.optimization_barrier((other, side))
    up2, down2 = shift(up1, "z", 1), shift(down1, "z", -1)
    other_side, far = sideways(other), onward(*side)
    other_side, far, w_out = lax.optimization_barrier((other_side, far, w_out))
    up3, down3 = shift(up2, "z", 1), shift(down2, "z", -1)
    other_far = onward(*other_side)
    blocks = column_blocks(w_out, core1, width)
    other_far, blocks = lax.optimization_barrier((other_far, blocks))
    up3, down3, other_far = lax.optimization_barrier((up3, down3, other_far))
    up4 = shift(up3[:, : depth // 2], "z", 1)
    down4 = shift(down3[:, depth // 2 :], "z", -1)

    half = exchange(blocks, MP)

    x, yhi = lax.axis_index("x"), lax.axis_index("yhi")
    shard = (z + jnp.array([0, zs - 1, 1, zs - 2, 2, zs - 3, 3, zs - 4], jnp.int32)) & (zs - 1)
    slots = (2 * (((shard >> 1) - x) & (mp // 2 - 1)) + ((shard & 1) ^ yhi)).astype(jnp.int32)
    features = (mine, *side, *far, other, *other_side, *other_far)
    early = [[(own,), (up1,)], [(down1,), (up2,)], [(down2,), (up3,)], [(down3,)]]
    acc, spare = project(features, early, slots)
    kept, sent = project_last(core1, spare, up4, down4, acc)
    attn = attention(kept, shift(sent, "core", 1), frames)
    attn, half = lax.optimization_barrier((attn, half))
    other_half = shift(half, "core", 1)
    attn = exchange(attn, FRAME).reshape(rows, heads)
    peer = shift(attn, "yhi", 1)
    side = sideways(attn)
    peer, side = lax.optimization_barrier((peer, side))
    peer_side, far = sideways(peer), onward(*side)
    peer_far = onward(*peer_side)
    where = jnp.stack([core, x, yhi]).astype(jnp.int32)
    acc = near(
        where, attn, peer, side[0], peer_side[0], side[1], peer_side[1], half, other_half
    )
    onehot = (action_idx.reshape(clips)[:, None] == jnp.arange(codebook.shape[0])[None, :]).astype(
        jnp.float32
    )
    codevec = jnp.dot(onehot, codebook, precision=lax.Precision.HIGHEST)
    gate = jnp.dot(codevec, act_proj, precision=lax.Precision.HIGHEST)
    peers = frames * lax.axis_size("dp")
    next_state, terms = finish(
        where, peers, *far, *peer_far, half, other_half, acc, xin, gate,
        cotangent.reshape(rows, width), codevec,
    )
    terms = exchange(terms, FRAME + ("dp",))
    terms = terms.reshape(-1, terms.shape[-1])
    grad_proj = lax.dot_general(
        terms[:, width:],
        terms[:, :width],
        (((0,), (0,)), ((), ())),
        precision=lax.Precision.HIGHEST,
        preferred_element_type=jnp.float32,
    )
    return (next_state.reshape(tokens.shape), grad_proj)


def solution(mesh):
    split = Mesh(
        mesh.devices.reshape(mesh.shape["frame"] // 2, 2, mesh.shape["mp"] // 2, 2, mesh.shape["dp"]),
        ("z", "core", "x", "yhi", "dp"),
    )
    return jax.shard_map(
        body,
        mesh=split,
        in_specs=(
            P("dp", FRAME, None, MP),
            P("dp", FRAME, None),
            P(MP),
            P(FRAME, None, MP),
            P(MP, None),
            P("dp", FRAME),
            P(),
            P(None, MP),
            P("dp", FRAME, None, MP),
        ),
        out_specs=(P("dp", FRAME, None, MP), P(None, MP)),
        check_vma=False,
    )
```

```python
import math

import jax
import jax.numpy as jnp
from jax import lax
from jax.experimental import pallas as pl
from jax.experimental.pallas import tpu as pltpu
from jax.sharding import Mesh
from jax.sharding import PartitionSpec as P

HS = 128
MASKED = -1e30
QKV_VMEM = 58
SMEM = pl.BlockSpec(memory_space=pltpu.SMEM)
WHOLE = pl.BlockSpec(memory_space=pltpu.VMEM)
ANYWHERE = pl.BlockSpec(memory_space=pl.ANY)
FRAME = ("z", "core")
MP = ("x", "yhi")
SMALL = pltpu.CompilerParams(vmem_limit_bytes=12 << 20)


def exchange(x, axis):
    return lax.all_to_all(x, axis, split_axis=0, concat_axis=0, tiled=True)


def shift(x, axis, by):
    n = lax.axis_size(axis)
    return lax.ppermute(x, axis, [(i, (i + by) % n) for i in range(n)])


def fetch_features(slot, pieces, target, sem):
    half = target.shape[0] // 2
    for own in range(2):
        here, right, left, top, low = pieces[5 * own : 5 * own + 5]
        for k, source in ((0, here), (1, right), (3, left)):

            @pl.when(slot == 2 * k + own)
            def _():
                pltpu.make_async_copy(source, target, sem).start()

        @pl.when(slot == 4 + own)
        def _():
            pltpu.make_async_copy(top, target.at[pl.ds(0, half)], sem).start()
            pltpu.make_async_copy(low, target.at[pl.ds(half, half)], sem).start()


def qkv_kernel(groups, slots, *refs):
    features, refs = refs[:10], refs[10:]
    pieces = [w for group in groups for w in group]
    count = sum(pieces)
    shards, refs = refs[:count], refs[count:]
    acc, spare, x_ref, w_ref, x_sem, w_sem = refs
    rows, full = x_ref.shape[1], x_ref.shape[2] // 2
    copies, at = [], 0
    for j, n in enumerate(pieces):
        fetch_features(slots[j], features, x_ref.at[j], x_sem.at[j])
        copies.append([])
        row = j * full
        for source in shards[at : at + n]:
            depth = source.shape[1]
            copy = pltpu.make_async_copy(source, w_ref.at[:, pl.ds(row, depth)], w_sem.at[at])
            copy.start()
            copies[j].append(copy)
            row += depth
            at += 1

    n = len(pieces)
    fetch_features(slots[n], features, spare, x_sem.at[n])
    j = 0
    for number, group in enumerate(groups):
        for i in range(j, j + len(group)):
            pltpu.make_async_copy(features[0], x_ref.at[i], x_sem.at[i]).wait()
            for copy in copies[i]:
                copy.wait()
        xs = [x_ref[j + i] for i in range(len(group))]
        x = jnp.concatenate(
            [
                jnp.concatenate([x[:, :full] for x in xs], axis=1),
                jnp.concatenate([x[:, full:] for x in xs], axis=1),
            ],
            axis=0,
        )
        span = pl.ds(j * full, len(group) * full)
        w = jnp.concatenate([w_ref[i, span] for i in range(3)], axis=1)
        part = jnp.dot(x, w, preferred_element_type=jnp.float32)
        if number:
            acc[...] += part
        else:
            acc[...] = part
        j += len(group)
    pltpu.make_async_copy(features[0], spare, x_sem.at[n]).wait()


def project(features, groups, slots):
    rows, width = features[0].shape
    counts = [[len(s) for s in group] for group in groups]
    shards = [w for group in groups for s in group for w in s]
    heads = shards[0].shape[-1]
    operands = [*features, *shards]
    n = sum(len(c) for c in counts)

    def kernel(*refs):
        qkv_kernel(counts, *refs)

    return pl.pallas_call(
        kernel,
        in_specs=[SMEM] + [ANYWHERE] * len(operands),
        out_specs=[WHOLE, WHOLE],
        out_shape=[
            jax.ShapeDtypeStruct((2 * rows, 3 * heads), jnp.float32),
            jax.ShapeDtypeStruct((rows, width), jnp.bfloat16),
        ],
        scratch_shapes=[
            pltpu.VMEM((n, rows, width), jnp.bfloat16),
            pltpu.VMEM((3, n * width // 2, heads), jnp.bfloat16),
            pltpu.SemaphoreType.DMA((n + 1,)),
            pltpu.SemaphoreType.DMA((len(shards),)),
        ],
        compiler_params=pltpu.CompilerParams(vmem_limit_bytes=QKV_VMEM << 20),
    )(slots, *operands)


def last_kernel(core, x_ref, first, second, acc, kept, sent):
    rows, full = x_ref.shape[0], x_ref.shape[1] // 2
    me = core[0]
    w = jnp.concatenate(
        [jnp.concatenate([first[i], second[i]], axis=0) for i in range(3)], axis=1
    )
    for side, out in ((me, kept), (1 - me, sent)):
        x = jnp.where(side == 0, x_ref[:, :full], x_ref[:, full:])
        part = jnp.dot(x, w, preferred_element_type=jnp.float32)
        out[...] = (acc[pl.ds(pl.multiple_of(side * rows, rows), rows)] + part).astype(out.dtype)


def project_last(core, x, first, second, acc):
    rows, total = x.shape[0], acc.shape[1]
    return pl.pallas_call(
        last_kernel,
        in_specs=[SMEM] + [WHOLE] * 4,
        out_specs=[WHOLE, WHOLE],
        out_shape=[
            jax.ShapeDtypeStruct((rows, total), jnp.float32),
            jax.ShapeDtypeStruct((rows, total), jnp.bfloat16),
        ],
        compiler_params=SMALL,
    )(core, x, first, second, acc)


def attend(q, k, v, bias):
    s = lax.dot_general(q, k, (((1,), (1,)), ((), ())), preferred_element_type=jnp.float32)
    s = s * (1.0 / math.sqrt(HS)) + bias
    peak = jnp.max(s, axis=1, keepdims=True)
    w = jnp.exp(s - peak)
    total = jnp.sum(w, axis=1, keepdims=True)
    high = w.astype(jnp.bfloat16)
    low = (w - high.astype(jnp.float32)).astype(jnp.bfloat16)
    accum = jnp.dot(high, v, preferred_element_type=jnp.float32)
    accum += jnp.dot(low, v, preferred_element_type=jnp.float32)
    return (accum / total).astype(jnp.bfloat16)


def attention_kernel(own_ref, other_ref, bias_ref, out_ref):
    frames, spots, width = out_ref.shape
    bias = bias_ref[...]
    for h in range(width // HS):
        q, k, v = (
            (own_ref[:, cols] + other_ref[:, cols].astype(jnp.float32)).astype(jnp.bfloat16)
            for cols in (slice(i * width + h * HS, i * width + (h + 1) * HS) for i in range(3))
        )
        o = attend(q, k, v, bias)
        for t in range(frames):
            out_ref[t, :, h * HS : (h + 1) * HS] = o[t * spots : (t + 1) * spots]


def attention(own, other, frames):
    rows, heads = own.shape[0], own.shape[1] // 3
    spots = rows // frames
    r = jnp.arange(rows)
    seen = (r[:, None] % spots == r[None, :] % spots) & (r[:, None] >= r[None, :])
    bias = jnp.where(seen, 0.0, MASKED).astype(jnp.float32)
    return pl.pallas_call(
        attention_kernel,
        out_shape=jax.ShapeDtypeStruct((frames, spots, heads), jnp.bfloat16),
        compiler_params=SMALL,
    )(own, other, bias)


def out_product(a, where, dx, half, other):
    n = half.shape[0] // 2
    block = 2 * ((where[1] + dx) & (n - 1))
    w = []
    for b in range(2):
        m = block + (b ^ where[2])
        mine, theirs = half[m], other[m]
        first = where[0] == 0
        w += [jnp.where(first, mine, theirs), jnp.where(first, theirs, mine)]
    x = jnp.concatenate(a, axis=1)
    return jnp.dot(x, jnp.concatenate(w, axis=0), preferred_element_type=jnp.float32)


def own_kernel(where, m0, m1, half, other, acc):
    acc[...] = out_product((m0[...], m1[...]), where, 0, half, other)


def side_kernel(where, r0, r1, l0, l1, half, other, own, acc):
    acc[...] = own[...] + out_product((r0[...], r1[...]), where, 1, half, other)
    acc[...] += out_product((l0[...], l1[...]), where, 3, half, other)


def far_kernel(
    where, t0, w0, t1, w1, half, other, acc, xin, gate, cot, codevec, next_ref, terms
):
    far = tuple(jnp.concatenate([t[...], w[...]], axis=0) for t, w in ((t0, w0), (t1, w1)))
    mixed = acc[...] + out_product(far, where, 2, half, other)
    rows, width = mixed.shape
    clips = gate.shape[0]
    spots = rows // clips
    sums = []
    for c in range(clips):
        at = slice(c * spots, (c + 1) * spots)
        m = mixed[at]
        moved = xin[at].astype(jnp.float32) + gate[c : c + 1] * m
        next_ref[at] = moved.astype(jnp.bfloat16)
        sums.append(jnp.sum(cot[at].astype(jnp.float32) * m, axis=0, keepdims=True))
    dgate = jnp.concatenate(sums, axis=0)
    for i in range(terms.shape[0]):
        terms[i, :, :width] = dgate
        terms[i, :, width:] = codevec[...]


def near(kernel, rows, width, where, *operands):
    return pl.pallas_call(
        kernel,
        in_specs=[SMEM] + [WHOLE] * len(operands),
        out_specs=WHOLE,
        out_shape=jax.ShapeDtypeStruct((rows, width), jnp.float32),
        compiler_params=SMALL,
    )(where, *operands)


def finish(where, peers, *operands):
    rows, width = operands[6].shape
    clips = operands[8].shape[0]
    smem, vmem = pl.BlockSpec(memory_space=pltpu.SMEM), pl.BlockSpec(memory_space=pltpu.VMEM)
    return pl.pallas_call(
        far_kernel,
        in_specs=[smem] + [vmem] * 11,
        out_specs=[vmem, vmem],
        out_shape=[
            jax.ShapeDtypeStruct((rows, width), jnp.bfloat16),
            jax.ShapeDtypeStruct((peers, clips, width + operands[10].shape[1]), jnp.float32),
        ],
        compiler_params=SMALL,
    )(where, *operands)


def blocks_kernel(core, w_ref, out_ref, sem):
    n, half, width = out_ref.shape
    rows = pl.ds(pl.multiple_of(core[0] * half, half), half)
    copies = [
        pltpu.make_async_copy(w_ref.at[rows, pl.ds(m * width, width)], out_ref.at[m], sem.at[m])
        for m in range(n)
    ]
    for copy in copies:
        copy.start()
    for copy in copies:
        copy.wait()


def column_blocks(w, core, width):
    heads, full = w.shape
    half, n = heads // 2, full // width
    hbm = pl.BlockSpec(memory_space=pltpu.HBM)
    return pl.pallas_call(
        blocks_kernel,
        in_specs=[pl.BlockSpec(memory_space=pltpu.SMEM), hbm],
        out_specs=hbm,
        out_shape=jax.ShapeDtypeStruct((n, half, width), w.dtype),
        scratch_shapes=[pltpu.SemaphoreType.DMA((n,))],
        compiler_params=SMALL,
    )(core, w)


def body(tokens, token_mask, mask_embed, w_qkv, w_out, action_idx, codebook, act_proj, cotangent):
    clips, _, spots, width = tokens.shape
    rows = clips * spots
    zs, cores = lax.axis_size("z"), lax.axis_size("core")
    frames, mp = zs * cores, lax.axis_size(MP)
    depth, heads = w_qkv.shape[0], w_qkv.shape[2]
    z, core = lax.axis_index("z"), lax.axis_index("core")
    core1 = core.reshape(1).astype(jnp.int32)
    xin = jnp.where(token_mask[..., None] == 1, mask_embed, tokens).reshape(rows, width)
    mine = xin.reshape(zs, 2, rows // frames, cores, depth).transpose(0, 3, 2, 1, 4)
    mine = exchange(mine.reshape(frames, rows // frames, 2 * depth), FRAME).reshape(rows, 2 * depth)

    own = w_qkv.transpose(1, 0, 2)
    up1, down1 = shift(own, "z", 1), shift(own, "z", -1)
    middle = rows // 2

    def sideways(block):
        return shift(block, "x", -1), shift(block, "x", 1)

    def onward(right, left):
        return shift(left[:middle], "x", 1), shift(right[middle:], "x", -1)

    other = shift(mine, "yhi", 1)
    side = sideways(mine)
    other, side = lax.optimization_barrier((other, side))
    x, yhi = lax.axis_index("x"), lax.axis_index("yhi")
    shard = (z + jnp.array([0, zs - 1, 1, zs - 2, 2, zs - 3, 3, zs - 4], jnp.int32)) & (zs - 1)
    slots = (2 * (((shard >> 1) - x) & (mp // 2 - 1)) + ((shard & 1) ^ yhi)).astype(jnp.int32)
    up2, down2 = shift(up1, "z", 1), shift(down1, "z", -1)
    other_side, far = sideways(other), onward(*side)
    other_side, far, w_out, slots = lax.optimization_barrier((other_side, far, w_out, slots))
    up3, down3 = shift(up2, "z", 1), shift(down2, "z", -1)
    other_far = onward(*other_side)
    blocks = column_blocks(w_out, core1, width)
    other_far, blocks = lax.optimization_barrier((other_far, blocks))
    up3, down3, other_far = lax.optimization_barrier((up3, down3, other_far))
    up4 = shift(up3[:, : depth // 2], "z", 1)
    down4 = shift(down3[:, depth // 2 :], "z", -1)

    half = exchange(blocks, MP)

    features = (mine, *side, *far, other, *other_side, *other_far)
    early = [[(own,), (up1,)], [(down1,), (up2,)], [(down2,), (up3,)], [(down3,)]]
    acc, spare = project(features, early, slots)
    kept, sent = project_last(core1, spare, up4, down4, acc)
    attn = attention(kept, shift(sent, "core", 1), frames)
    attn, half = lax.optimization_barrier((attn, half))
    other_half = shift(half, "core", 1)
    attn = exchange(attn, FRAME).reshape(rows, heads)
    peer = shift(attn, "yhi", 1)
    side = sideways(attn)
    peer_side = sideways(peer)
    _, side = lax.optimization_barrier((peer, side))
    far = onward(*side)
    where = jnp.stack([core, x, yhi]).astype(jnp.int32)
    acc = near(own_kernel, rows, width, where, attn, peer, half, other_half)
    peer_side, acc = lax.optimization_barrier((peer_side, acc))
    peer_far = onward(*peer_side)
    acc = near(
        side_kernel, rows, width, where,
        side[0], peer_side[0], side[1], peer_side[1], half, other_half, acc,
    )
    onehot = (action_idx.reshape(clips)[:, None] == jnp.arange(codebook.shape[0])[None, :]).astype(
        jnp.float32
    )
    codevec = jnp.dot(onehot, codebook, precision=lax.Precision.HIGHEST)
    gate = jnp.dot(codevec, act_proj, precision=lax.Precision.HIGHEST)
    peers = frames * lax.axis_size("dp")
    next_state, terms = finish(
        where, peers, *far, *peer_far, half, other_half, acc, xin, gate,
        cotangent.reshape(rows, width), codevec,
    )
    terms = exchange(terms, FRAME + ("dp",))
    terms = terms.reshape(-1, terms.shape[-1])
    grad_proj = lax.dot_general(
        terms[:, width:],
        terms[:, :width],
        (((0,), (0,)), ((), ())),
        precision=lax.Precision.HIGHEST,
        preferred_element_type=jnp.float32,
    )
    return (next_state.reshape(tokens.shape), grad_proj)


def solution(mesh):
    split = Mesh(
        mesh.devices.reshape(mesh.shape["frame"] // 2, 2, mesh.shape["mp"] // 2, 2, mesh.shape["dp"]),
        ("z", "core", "x", "yhi", "dp"),
    )
    return jax.shard_map(
        body,
        mesh=split,
        in_specs=(
            P("dp", FRAME, None, MP),
            P("dp", FRAME, None),
            P(MP),
            P(FRAME, None, MP),
            P(MP, None),
            P("dp", FRAME),
            P(),
            P(None, MP),
            P("dp", FRAME, None, MP),
        ),
        out_specs=(P("dp", FRAME, None, MP), P(None, MP)),
        check_vma=False,
    )
```

```python
import math

import jax
import jax.numpy as jnp
from jax import lax
from jax.experimental import pallas as pl
from jax.experimental.pallas import tpu as pltpu
from jax.sharding import Mesh
from jax.sharding import PartitionSpec as P

HS = 128
MASKED = -1e30
QKV_VMEM = 58
SMEM = pl.BlockSpec(memory_space=pltpu.SMEM)
WHOLE = pl.BlockSpec(memory_space=pltpu.VMEM)
ANYWHERE = pl.BlockSpec(memory_space=pl.ANY)
FRAME = ("z", "core")
MP = ("x", "yhi")
SMALL = pltpu.CompilerParams(vmem_limit_bytes=12 << 20)


def exchange(x, axis):
    return lax.all_to_all(x, axis, split_axis=0, concat_axis=0, tiled=True)


def shift(x, axis, by):
    n = lax.axis_size(axis)
    return lax.ppermute(x, axis, [(i, (i + by) % n) for i in range(n)])


def fetch_features(slot, pieces, target, sem):
    half = target.shape[0] // 2
    for own in range(2):
        here, right, left, top, low = pieces[5 * own : 5 * own + 5]
        for k, source in ((0, here), (1, right), (3, left)):

            @pl.when(slot == 2 * k + own)
            def _():
                pltpu.make_async_copy(source, target, sem).start()

        @pl.when(slot == 4 + own)
        def _():
            pltpu.make_async_copy(top, target.at[pl.ds(0, half)], sem).start()
            pltpu.make_async_copy(low, target.at[pl.ds(half, half)], sem).start()


def qkv_kernel(groups, slots, *refs):
    features, refs = refs[:10], refs[10:]
    pieces = [w for group in groups for w in group]
    count = sum(pieces)
    shards, refs = refs[:count], refs[count:]
    acc, spare, x_ref, w_ref, x_sem, w_sem = refs
    rows, full = x_ref.shape[1], x_ref.shape[2] // 2
    copies, at = [], 0
    for j, n in enumerate(pieces):
        fetch_features(slots[j], features, x_ref.at[j], x_sem.at[j])
        copies.append([])
        row = j * full
        for source in shards[at : at + n]:
            depth = source.shape[1]
            copy = pltpu.make_async_copy(source, w_ref.at[:, pl.ds(row, depth)], w_sem.at[at])
            copy.start()
            copies[j].append(copy)
            row += depth
            at += 1

    n = len(pieces)
    fetch_features(slots[n], features, spare, x_sem.at[n])
    j = 0
    for number, group in enumerate(groups):
        for i in range(j, j + len(group)):
            pltpu.make_async_copy(features[0], x_ref.at[i], x_sem.at[i]).wait()
            for copy in copies[i]:
                copy.wait()
        xs = [x_ref[j + i] for i in range(len(group))]
        x = jnp.concatenate(
            [
                jnp.concatenate([x[:, :full] for x in xs], axis=1),
                jnp.concatenate([x[:, full:] for x in xs], axis=1),
            ],
            axis=0,
        )
        span = pl.ds(j * full, len(group) * full)
        w = jnp.concatenate([w_ref[i, span] for i in range(3)], axis=1)
        part = jnp.dot(x, w, preferred_element_type=jnp.float32)
        if number:
            acc[...] += part
        else:
            acc[...] = part
        j += len(group)
    pltpu.make_async_copy(features[0], spare, x_sem.at[n]).wait()


def project(features, groups, slots):
    rows, width = features[0].shape
    counts = [[len(s) for s in group] for group in groups]
    shards = [w for group in groups for s in group for w in s]
    heads = shards[0].shape[-1]
    operands = [*features, *shards]
    n = sum(len(c) for c in counts)

    def kernel(*refs):
        qkv_kernel(counts, *refs)

    return pl.pallas_call(
        kernel,
        in_specs=[SMEM] + [ANYWHERE] * len(operands),
        out_specs=[WHOLE, WHOLE],
        out_shape=[
            jax.ShapeDtypeStruct((2 * rows, 3 * heads), jnp.float32),
            jax.ShapeDtypeStruct((rows, width), jnp.bfloat16),
        ],
        scratch_shapes=[
            pltpu.VMEM((n, rows, width), jnp.bfloat16),
            pltpu.VMEM((3, n * width // 2, heads), jnp.bfloat16),
            pltpu.SemaphoreType.DMA((n + 1,)),
            pltpu.SemaphoreType.DMA((len(shards),)),
        ],
        compiler_params=pltpu.CompilerParams(vmem_limit_bytes=QKV_VMEM << 20),
    )(slots, *operands)


def last_kernel(core, x_ref, first, second, acc, kept, sent):
    rows, full = x_ref.shape[0], x_ref.shape[1] // 2
    me = core[0]
    w = jnp.concatenate(
        [jnp.concatenate([first[i], second[i]], axis=0) for i in range(3)], axis=1
    )
    for side, out in ((me, kept), (1 - me, sent)):
        x = jnp.where(side == 0, x_ref[:, :full], x_ref[:, full:])
        part = jnp.dot(x, w, preferred_element_type=jnp.float32)
        out[...] = (acc[pl.ds(pl.multiple_of(side * rows, rows), rows)] + part).astype(out.dtype)


def project_last(core, x, first, second, acc):
    rows, total = x.shape[0], acc.shape[1]
    return pl.pallas_call(
        last_kernel,
        in_specs=[SMEM] + [WHOLE] * 4,
        out_specs=[WHOLE, WHOLE],
        out_shape=[
            jax.ShapeDtypeStruct((rows, total), jnp.float32),
            jax.ShapeDtypeStruct((rows, total), jnp.bfloat16),
        ],
        compiler_params=SMALL,
    )(core, x, first, second, acc)


def attend(q, k, v, bias):
    s = lax.dot_general(q, k, (((1,), (1,)), ((), ())), preferred_element_type=jnp.float32)
    s = s * (1.0 / math.sqrt(HS)) + bias
    peak = jnp.max(s, axis=1, keepdims=True)
    w = jnp.exp(s - peak)
    total = jnp.sum(w, axis=1, keepdims=True)
    high = w.astype(jnp.bfloat16)
    low = (w - high.astype(jnp.float32)).astype(jnp.bfloat16)
    accum = jnp.dot(high, v, preferred_element_type=jnp.float32)
    accum += jnp.dot(low, v, preferred_element_type=jnp.float32)
    return (accum / total).astype(jnp.bfloat16)


def attention_kernel(own_ref, other_ref, bias_ref, out_ref):
    frames, spots, width = out_ref.shape
    bias = bias_ref[...]
    for h in range(width // HS):
        q, k, v = (
            (own_ref[:, cols] + other_ref[:, cols].astype(jnp.float32)).astype(jnp.bfloat16)
            for cols in (slice(i * width + h * HS, i * width + (h + 1) * HS) for i in range(3))
        )
        o = attend(q, k, v, bias)
        for t in range(frames):
            out_ref[t, :, h * HS : (h + 1) * HS] = o[t * spots : (t + 1) * spots]


def attention(own, other, frames):
    rows, heads = own.shape[0], own.shape[1] // 3
    spots = rows // frames
    r = jnp.arange(rows)
    seen = (r[:, None] % spots == r[None, :] % spots) & (r[:, None] >= r[None, :])
    bias = jnp.where(seen, 0.0, MASKED).astype(jnp.float32)
    return pl.pallas_call(
        attention_kernel,
        out_shape=jax.ShapeDtypeStruct((frames, spots, heads), jnp.bfloat16),
        compiler_params=SMALL,
    )(own, other, bias)


def out_product(a, where, dx, half, other):
    n = half.shape[0] // 2
    block = 2 * ((where[1] + dx) & (n - 1))
    w = []
    for b in range(2):
        m = block + (b ^ where[2])
        mine, theirs = half[m], other[m]
        first = where[0] == 0
        w += [jnp.where(first, mine, theirs), jnp.where(first, theirs, mine)]
    x = jnp.concatenate(a, axis=1)
    return jnp.dot(x, jnp.concatenate(w, axis=0), preferred_element_type=jnp.float32)


def own_kernel(where, m0, m1, half, other, acc):
    acc[...] = out_product((m0[...], m1[...]), where, 0, half, other)


def side_kernel(where, r0, r1, l0, l1, half, other, own, acc):
    acc[...] = own[...] + out_product((r0[...], r1[...]), where, 1, half, other)
    acc[...] += out_product((l0[...], l1[...]), where, 3, half, other)


def far_kernel(
    where, t0, w0, t1, w1, half, other, acc, xin, gate, cot, codevec, next_ref, terms
):
    far = tuple(jnp.concatenate([t[...], w[...]], axis=0) for t, w in ((t0, w0), (t1, w1)))
    mixed = acc[...] + out_product(far, where, 2, half, other)
    rows, width = mixed.shape
    clips = gate.shape[0]
    spots = rows // clips
    sums = []
    for c in range(clips):
        at = slice(c * spots, (c + 1) * spots)
        m = mixed[at]
        moved = xin[at].astype(jnp.float32) + gate[c : c + 1] * m
        next_ref[at] = moved.astype(jnp.bfloat16)
        sums.append(jnp.sum(cot[at].astype(jnp.float32) * m, axis=0, keepdims=True))
    dgate = jnp.concatenate(sums, axis=0)
    for i in range(terms.shape[0]):
        terms[i, :, :width] = dgate
        terms[i, :, width:] = codevec[...]


def near(kernel, rows, width, where, *operands):
    return pl.pallas_call(
        kernel,
        in_specs=[SMEM] + [WHOLE] * len(operands),
        out_specs=WHOLE,
        out_shape=jax.ShapeDtypeStruct((rows, width), jnp.float32),
        compiler_params=SMALL,
    )(where, *operands)


def finish(where, peers, *operands):
    rows, width = operands[6].shape
    clips = operands[8].shape[0]
    smem, vmem = pl.BlockSpec(memory_space=pltpu.SMEM), pl.BlockSpec(memory_space=pltpu.VMEM)
    return pl.pallas_call(
        far_kernel,
        in_specs=[smem] + [vmem] * 11,
        out_specs=[vmem, vmem],
        out_shape=[
            jax.ShapeDtypeStruct((rows, width), jnp.bfloat16),
            jax.ShapeDtypeStruct((peers, clips, width + operands[10].shape[1]), jnp.float32),
        ],
        compiler_params=SMALL,
    )(where, *operands)


def blocks_kernel(core, w_ref, out_ref, sem):
    n, half, width = out_ref.shape
    rows = pl.ds(pl.multiple_of(core[0] * half, half), half)
    copies = [
        pltpu.make_async_copy(w_ref.at[rows, pl.ds(m * width, width)], out_ref.at[m], sem.at[m])
        for m in range(n)
    ]
    for copy in copies:
        copy.start()
    for copy in copies:
        copy.wait()


def column_blocks(w, core, width):
    heads, full = w.shape
    half, n = heads // 2, full // width
    hbm = pl.BlockSpec(memory_space=pltpu.HBM)
    return pl.pallas_call(
        blocks_kernel,
        in_specs=[pl.BlockSpec(memory_space=pltpu.SMEM), hbm],
        out_specs=hbm,
        out_shape=jax.ShapeDtypeStruct((n, half, width), w.dtype),
        scratch_shapes=[pltpu.SemaphoreType.DMA((n,))],
        compiler_params=SMALL,
    )(core, w)


def body(tokens, token_mask, mask_embed, w_qkv, w_out, action_idx, codebook, act_proj, cotangent):
    clips, _, spots, width = tokens.shape
    rows = clips * spots
    zs, cores = lax.axis_size("z"), lax.axis_size("core")
    frames, mp = zs * cores, lax.axis_size(MP)
    depth, heads = w_qkv.shape[0], w_qkv.shape[2]
    z, core = lax.axis_index("z"), lax.axis_index("core")
    core1 = core.reshape(1).astype(jnp.int32)
    xin = jnp.where(token_mask[..., None] == 1, mask_embed, tokens).reshape(rows, width)
    mine = xin.reshape(zs, 2, rows // frames, cores, depth).transpose(0, 3, 2, 1, 4)
    mine = exchange(mine.reshape(frames, rows // frames, 2 * depth), FRAME).reshape(rows, 2 * depth)

    own = w_qkv.transpose(1, 0, 2)
    up1, down1 = shift(own, "z", 1), shift(own, "z", -1)
    middle = rows // 2

    def sideways(block):
        return shift(block, "x", -1), shift(block, "x", 1)

    def onward(right, left):
        return shift(left[:middle], "x", 1), shift(right[middle:], "x", -1)

    other = shift(mine, "yhi", 1)
    side = sideways(mine)
    other, side = lax.optimization_barrier((other, side))
    x, yhi = lax.axis_index("x"), lax.axis_index("yhi")
    shard = (z + jnp.array([0, zs - 1, 1, zs - 2, 2, zs - 3, 3, zs - 4], jnp.int32)) & (zs - 1)
    slots = (2 * (((shard >> 1) - x) & (mp // 2 - 1)) + ((shard & 1) ^ yhi)).astype(jnp.int32)
    up2, down2 = shift(up1, "z", 1), shift(down1, "z", -1)
    other_side, far = sideways(other), onward(*side)
    other_side, far, w_out, slots = lax.optimization_barrier((other_side, far, w_out, slots))
    up3, down3 = shift(up2, "z", 1), shift(down2, "z", -1)
    other_far = onward(*other_side)
    blocks = column_blocks(w_out, core1, width)
    other_far, blocks = lax.optimization_barrier((other_far, blocks))
    up4 = shift(up3[:, : depth // 2], "z", 1)
    down4 = shift(down3[:, depth // 2 :], "z", -1)

    half = exchange(blocks, MP)

    features = (mine, *side, *far, other, *other_side, *other_far)
    early = [[(own,), (up1,)], [(down1,), (up2,)], [(down2,), (up3,)], [(down3,)]]
    acc, spare = project(features, early, slots)
    kept, sent = project_last(core1, spare, up4, down4, acc)
    attn = attention(kept, shift(sent, "core", 1), frames)
    attn, half = lax.optimization_barrier((attn, half))
    other_half = shift(half, "core", 1)
    attn = exchange(attn, FRAME).reshape(rows, heads)
    peer = shift(attn, "yhi", 1)
    side = sideways(attn)
    peer_side = sideways(peer)
    _, side = lax.optimization_barrier((peer, side))
    far = onward(*side)
    where = jnp.stack([core, x, yhi]).astype(jnp.int32)
    acc = near(own_kernel, rows, width, where, attn, peer, half, other_half)
    peer_side, acc = lax.optimization_barrier((peer_side, acc))
    peer_far = onward(*peer_side)
    acc = near(
        side_kernel, rows, width, where,
        side[0], peer_side[0], side[1], peer_side[1], half, other_half, acc,
    )
    onehot = (action_idx.reshape(clips)[:, None] == jnp.arange(codebook.shape[0])[None, :]).astype(
        jnp.float32
    )
    codevec = jnp.dot(onehot, codebook, precision=lax.Precision.HIGHEST)
    gate = jnp.dot(codevec, act_proj, precision=lax.Precision.HIGHEST)
    peers = frames * lax.axis_size("dp")
    next_state, terms = finish(
        where, peers, *far, *peer_far, half, other_half, acc, xin, gate,
        cotangent.reshape(rows, width), codevec,
    )
    terms = exchange(terms, FRAME + ("dp",))
    terms = terms.reshape(-1, terms.shape[-1])
    grad_proj = lax.dot_general(
        terms[:, width:],
        terms[:, :width],
        (((0,), (0,)), ((), ())),
        precision=lax.Precision.HIGHEST,
        preferred_element_type=jnp.float32,
    )
    return (next_state.reshape(tokens.shape), grad_proj)


def solution(mesh):
    split = Mesh(
        mesh.devices.reshape(mesh.shape["frame"] // 2, 2, mesh.shape["mp"] // 2, 2, mesh.shape["dp"]),
        ("z", "core", "x", "yhi", "dp"),
    )
    return jax.shard_map(
        body,
        mesh=split,
        in_specs=(
            P("dp", FRAME, None, MP),
            P("dp", FRAME, None),
            P(MP),
            P(FRAME, None, MP),
            P(MP, None),
            P("dp", FRAME),
            P(),
            P(None, MP),
            P("dp", FRAME, None, MP),
        ),
        out_specs=(P("dp", FRAME, None, MP), P(None, MP)),
        check_vma=False,
    )
```

```python
import math

import jax
import jax.numpy as jnp
from jax import lax
from jax.experimental import pallas as pl
from jax.experimental.pallas import tpu as pltpu
from jax.sharding import Mesh
from jax.sharding import PartitionSpec as P

HS = 128
MASKED = -1e30
QKV_VMEM = 58
SMEM = pl.BlockSpec(memory_space=pltpu.SMEM)
WHOLE = pl.BlockSpec(memory_space=pltpu.VMEM)
ANYWHERE = pl.BlockSpec(memory_space=pl.ANY)
FRAME = ("z", "core")
MP = ("x", "yhi")
SMALL = pltpu.CompilerParams(vmem_limit_bytes=12 << 20)


def exchange(x, axis):
    return lax.all_to_all(x, axis, split_axis=0, concat_axis=0, tiled=True)


def shift(x, axis, by):
    n = lax.axis_size(axis)
    return lax.ppermute(x, axis, [(i, (i + by) % n) for i in range(n)])


def fetch_features(slot, pieces, target, sem):
    half = target.shape[0] // 2
    for own in range(2):
        here, right, left, top, low = pieces[5 * own : 5 * own + 5]
        for k, source in ((0, here), (1, right), (3, left)):

            @pl.when(slot == 2 * k + own)
            def _():
                pltpu.make_async_copy(source, target, sem).start()

        @pl.when(slot == 4 + own)
        def _():
            pltpu.make_async_copy(top, target.at[pl.ds(0, half)], sem).start()
            pltpu.make_async_copy(low, target.at[pl.ds(half, half)], sem).start()


def qkv_kernel(groups, slots, *refs):
    features, refs = refs[:10], refs[10:]
    pieces = [w for group in groups for w in group]
    count = sum(pieces)
    shards, refs = refs[:count], refs[count:]
    acc, spare, x_ref, w_ref, x_sem, w_sem = refs
    rows, full = x_ref.shape[1], x_ref.shape[2] // 2
    copies, at = [], 0
    for j, n in enumerate(pieces):
        fetch_features(slots[j], features, x_ref.at[j], x_sem.at[j])
        copies.append([])
        row = j * full
        for source in shards[at : at + n]:
            depth = source.shape[1]
            copy = pltpu.make_async_copy(source, w_ref.at[:, pl.ds(row, depth)], w_sem.at[at])
            copy.start()
            copies[j].append(copy)
            row += depth
            at += 1

    n = len(pieces)
    fetch_features(slots[n], features, spare, x_sem.at[n])
    j = 0
    for number, group in enumerate(groups):
        for i in range(j, j + len(group)):
            pltpu.make_async_copy(features[0], x_ref.at[i], x_sem.at[i]).wait()
            for copy in copies[i]:
                copy.wait()
        xs = [x_ref[j + i] for i in range(len(group))]
        x = jnp.concatenate(
            [
                jnp.concatenate([x[:, :full] for x in xs], axis=1),
                jnp.concatenate([x[:, full:] for x in xs], axis=1),
            ],
            axis=0,
        )
        span = pl.ds(j * full, len(group) * full)
        w = jnp.concatenate([w_ref[i, span] for i in range(3)], axis=1)
        part = jnp.dot(x, w, preferred_element_type=jnp.float32)
        if number:
            acc[...] += part
        else:
            acc[...] = part
        j += len(group)
    pltpu.make_async_copy(features[0], spare, x_sem.at[n]).wait()


def project(features, groups, slots):
    rows, width = features[0].shape
    counts = [[len(s) for s in group] for group in groups]
    shards = [w for group in groups for s in group for w in s]
    heads = shards[0].shape[-1]
    operands = [*features, *shards]
    n = sum(len(c) for c in counts)

    def kernel(*refs):
        qkv_kernel(counts, *refs)

    return pl.pallas_call(
        kernel,
        in_specs=[SMEM] + [ANYWHERE] * len(operands),
        out_specs=[WHOLE, WHOLE],
        out_shape=[
            jax.ShapeDtypeStruct((2 * rows, 3 * heads), jnp.float32),
            jax.ShapeDtypeStruct((rows, width), jnp.bfloat16),
        ],
        scratch_shapes=[
            pltpu.VMEM((n, rows, width), jnp.bfloat16),
            pltpu.VMEM((3, n * width // 2, heads), jnp.bfloat16),
            pltpu.SemaphoreType.DMA((n + 1,)),
            pltpu.SemaphoreType.DMA((len(shards),)),
        ],
        compiler_params=pltpu.CompilerParams(vmem_limit_bytes=QKV_VMEM << 20),
    )(slots, *operands)


def last_kernel(core, x_ref, first, second, acc, kept, sent):
    rows, full = x_ref.shape[0], x_ref.shape[1] // 2
    me = core[0]
    w = jnp.concatenate(
        [jnp.concatenate([first[i], second[i]], axis=0) for i in range(3)], axis=1
    )
    for side, out in ((me, kept), (1 - me, sent)):
        x = jnp.where(side == 0, x_ref[:, :full], x_ref[:, full:])
        part = jnp.dot(x, w, preferred_element_type=jnp.float32)
        out[...] = (acc[pl.ds(pl.multiple_of(side * rows, rows), rows)] + part).astype(out.dtype)


def project_last(core, x, first, second, acc):
    rows, total = x.shape[0], acc.shape[1]
    return pl.pallas_call(
        last_kernel,
        in_specs=[SMEM] + [WHOLE] * 4,
        out_specs=[WHOLE, WHOLE],
        out_shape=[
            jax.ShapeDtypeStruct((rows, total), jnp.float32),
            jax.ShapeDtypeStruct((rows, total), jnp.bfloat16),
        ],
        compiler_params=SMALL,
    )(core, x, first, second, acc)


def attend(q, k, v, bias):
    s = lax.dot_general(q, k, (((1,), (1,)), ((), ())), preferred_element_type=jnp.float32)
    s = s * (1.0 / math.sqrt(HS)) + bias
    peak = jnp.max(s, axis=1, keepdims=True)
    w = jnp.exp(s - peak)
    total = jnp.sum(w, axis=1, keepdims=True)
    high = w.astype(jnp.bfloat16)
    low = (w - high.astype(jnp.float32)).astype(jnp.bfloat16)
    accum = jnp.dot(high, v, preferred_element_type=jnp.float32)
    accum += jnp.dot(low, v, preferred_element_type=jnp.float32)
    return (accum / total).astype(jnp.bfloat16)


def attention_kernel(own_ref, other_ref, bias_ref, out_ref):
    frames, spots, width = out_ref.shape
    bias = bias_ref[...]
    for h in range(width // HS):
        q, k, v = (
            (own_ref[:, cols] + other_ref[:, cols].astype(jnp.float32)).astype(jnp.bfloat16)
            for cols in (slice(i * width + h * HS, i * width + (h + 1) * HS) for i in range(3))
        )
        o = attend(q, k, v, bias)
        for t in range(frames):
            out_ref[t, :, h * HS : (h + 1) * HS] = o[t * spots : (t + 1) * spots]


def attention(own, other, frames):
    rows, heads = own.shape[0], own.shape[1] // 3
    spots = rows // frames
    r = jnp.arange(rows)
    seen = (r[:, None] % spots == r[None, :] % spots) & (r[:, None] >= r[None, :])
    bias = jnp.where(seen, 0.0, MASKED).astype(jnp.float32)
    return pl.pallas_call(
        attention_kernel,
        out_shape=jax.ShapeDtypeStruct((frames, spots, heads), jnp.bfloat16),
        compiler_params=SMALL,
    )(own, other, bias)


def out_product(a, where, dx, half, other):
    n = half.shape[0] // 2
    block = 2 * ((where[1] + dx) & (n - 1))
    w = []
    for b in range(2):
        m = block + (b ^ where[2])
        mine, theirs = half[m], other[m]
        first = where[0] == 0
        w += [jnp.where(first, mine, theirs), jnp.where(first, theirs, mine)]
    x = jnp.concatenate(a, axis=1)
    return jnp.dot(x, jnp.concatenate(w, axis=0), preferred_element_type=jnp.float32)


def own_kernel(where, m0, m1, half, other, acc):
    acc[...] = out_product((m0[...], m1[...]), where, 0, half, other)


def side_kernel(where, r0, r1, l0, l1, half, other, own, acc):
    acc[...] = own[...] + out_product((r0[...], r1[...]), where, 1, half, other)
    acc[...] += out_product((l0[...], l1[...]), where, 3, half, other)


def far_kernel(
    where, t0, w0, t1, w1, half, other, acc, xin, gate, cot, codevec, next_ref, terms
):
    far = tuple(jnp.concatenate([t[...], w[...]], axis=0) for t, w in ((t0, w0), (t1, w1)))
    mixed = acc[...] + out_product(far, where, 2, half, other)
    rows, width = mixed.shape
    clips = gate.shape[0]
    spots = rows // clips
    sums = []
    for c in range(clips):
        at = slice(c * spots, (c + 1) * spots)
        m = mixed[at]
        moved = xin[at].astype(jnp.float32) + gate[c : c + 1] * m
        next_ref[at] = moved.astype(jnp.bfloat16)
        sums.append(jnp.sum(cot[at].astype(jnp.float32) * m, axis=0, keepdims=True))
    dgate = jnp.concatenate(sums, axis=0)
    for i in range(terms.shape[0]):
        terms[i, :, :width] = dgate
        terms[i, :, width:] = codevec[...]


def near(kernel, rows, width, where, *operands):
    return pl.pallas_call(
        kernel,
        in_specs=[SMEM] + [WHOLE] * len(operands),
        out_specs=WHOLE,
        out_shape=jax.ShapeDtypeStruct((rows, width), jnp.float32),
        compiler_params=SMALL,
    )(where, *operands)


def finish(where, peers, *operands):
    rows, width = operands[6].shape
    clips = operands[8].shape[0]
    smem, vmem = pl.BlockSpec(memory_space=pltpu.SMEM), pl.BlockSpec(memory_space=pltpu.VMEM)
    return pl.pallas_call(
        far_kernel,
        in_specs=[smem] + [vmem] * 11,
        out_specs=[vmem, vmem],
        out_shape=[
            jax.ShapeDtypeStruct((rows, width), jnp.bfloat16),
            jax.ShapeDtypeStruct((peers, clips, width + operands[10].shape[1]), jnp.float32),
        ],
        compiler_params=SMALL,
    )(where, *operands)


def blocks_kernel(core, w_ref, out_ref, sem):
    n, half, width = out_ref.shape
    rows = pl.ds(pl.multiple_of(core[0] * half, half), half)
    copies = [
        pltpu.make_async_copy(w_ref.at[rows, pl.ds(m * width, width)], out_ref.at[m], sem.at[m])
        for m in range(n)
    ]
    for copy in copies:
        copy.start()
    for copy in copies:
        copy.wait()


def column_blocks(w, core, width):
    heads, full = w.shape
    half, n = heads // 2, full // width
    hbm = pl.BlockSpec(memory_space=pltpu.HBM)
    return pl.pallas_call(
        blocks_kernel,
        in_specs=[pl.BlockSpec(memory_space=pltpu.SMEM), hbm],
        out_specs=hbm,
        out_shape=jax.ShapeDtypeStruct((n, half, width), w.dtype),
        scratch_shapes=[pltpu.SemaphoreType.DMA((n,))],
        compiler_params=SMALL,
    )(core, w)


def body(tokens, token_mask, mask_embed, w_qkv, w_out, action_idx, codebook, act_proj, cotangent):
    clips, _, spots, width = tokens.shape
    rows = clips * spots
    zs, cores = lax.axis_size("z"), lax.axis_size("core")
    frames, mp = zs * cores, lax.axis_size(MP)
    depth, heads = w_qkv.shape[0], w_qkv.shape[2]
    z, core = lax.axis_index("z"), lax.axis_index("core")
    core1 = core.reshape(1).astype(jnp.int32)
    xin = jnp.where(token_mask[..., None] == 1, mask_embed, tokens).reshape(rows, width)
    mine = xin.reshape(zs, 2, rows // frames, cores, depth).transpose(0, 3, 2, 1, 4)
    mine = exchange(mine.reshape(frames, rows // frames, 2 * depth), FRAME).reshape(rows, 2 * depth)

    own = w_qkv.transpose(1, 0, 2)
    up1, down1 = shift(own, "z", 1), shift(own, "z", -1)
    middle = rows // 2

    def sideways(block):
        return shift(block, "x", -1), shift(block, "x", 1)

    def onward(right, left):
        return shift(left[:middle], "x", 1), shift(right[middle:], "x", -1)

    other = shift(mine, "yhi", 1)
    side = sideways(mine)
    other_side = sideways(other)
    _, side = lax.optimization_barrier((other, side))
    x, yhi = lax.axis_index("x"), lax.axis_index("yhi")
    shard = (z + jnp.array([0, zs - 1, 1, zs - 2, 2, zs - 3, 3, zs - 4], jnp.int32)) & (zs - 1)
    slots = (2 * (((shard >> 1) - x) & (mp // 2 - 1)) + ((shard & 1) ^ yhi)).astype(jnp.int32)
    up2, down2 = shift(up1, "z", 1), shift(down1, "z", -1)
    far = onward(*side)
    other_side, far, w_out, slots = lax.optimization_barrier((other_side, far, w_out, slots))
    up3, down3 = shift(up2, "z", 1), shift(down2, "z", -1)
    other_far = onward(*other_side)
    blocks = column_blocks(w_out, core1, width)
    other_far, blocks = lax.optimization_barrier((other_far, blocks))
    up4 = shift(up3[:, : depth // 2], "z", 1)
    down4 = shift(down3[:, depth // 2 :], "z", -1)

    half = exchange(blocks, MP)

    features = (mine, *side, *far, other, *other_side, *other_far)
    early = [[(own,), (up1,)], [(down1,), (up2,)], [(down2,), (up3,)], [(down3,)]]
    acc, spare = project(features, early, slots)
    kept, sent = project_last(core1, spare, up4, down4, acc)
    attn = attention(kept, shift(sent, "core", 1), frames)
    attn, half = lax.optimization_barrier((attn, half))
    other_half = shift(half, "core", 1)
    attn = exchange(attn, FRAME).reshape(rows, heads)
    peer = shift(attn, "yhi", 1)
    side = sideways(attn)
    peer_side = sideways(peer)
    _, side = lax.optimization_barrier((peer, side))
    far = onward(*side)
    where = jnp.stack([core, x, yhi]).astype(jnp.int32)
    acc = near(own_kernel, rows, width, where, attn, peer, half, other_half)
    peer_side, acc = lax.optimization_barrier((peer_side, acc))
    peer_far = onward(*peer_side)
    acc = near(
        side_kernel, rows, width, where,
        side[0], peer_side[0], side[1], peer_side[1], half, other_half, acc,
    )
    onehot = (action_idx.reshape(clips)[:, None] == jnp.arange(codebook.shape[0])[None, :]).astype(
        jnp.float32
    )
    codevec = jnp.dot(onehot, codebook, precision=lax.Precision.HIGHEST)
    gate = jnp.dot(codevec, act_proj, precision=lax.Precision.HIGHEST)
    peers = frames * lax.axis_size("dp")
    next_state, terms = finish(
        where, peers, *far, *peer_far, half, other_half, acc, xin, gate,
        cotangent.reshape(rows, width), codevec,
    )
    terms = exchange(terms, FRAME + ("dp",))
    terms = terms.reshape(-1, terms.shape[-1])
    grad_proj = lax.dot_general(
        terms[:, width:],
        terms[:, :width],
        (((0,), (0,)), ((), ())),
        precision=lax.Precision.HIGHEST,
        preferred_element_type=jnp.float32,
    )
    return (next_state.reshape(tokens.shape), grad_proj)


def solution(mesh):
    split = Mesh(
        mesh.devices.reshape(mesh.shape["frame"] // 2, 2, mesh.shape["mp"] // 2, 2, mesh.shape["dp"]),
        ("z", "core", "x", "yhi", "dp"),
    )
    return jax.shard_map(
        body,
        mesh=split,
        in_specs=(
            P("dp", FRAME, None, MP),
            P("dp", FRAME, None),
            P(MP),
            P(FRAME, None, MP),
            P(MP, None),
            P("dp", FRAME),
            P(),
            P(None, MP),
            P("dp", FRAME, None, MP),
        ),
        out_specs=(P("dp", FRAME, None, MP), P(None, MP)),
        check_vma=False,
    )
```
